32 devices in a mesh: dp: 2 (over x), fsdp: 16 (over z, y, core).
Axes of the slice: x: 2, y: 2, z: 4, core: 2. Of those that a mesh axis runs over, the one named last changes fastest.
Arguments:
- tokens: bfloat16 [32, 512, 1024], P(('dp', 'fsdp')), may hold values from -6 to 6
- lengths: int32 [32], P(('dp', 'fsdp')), may hold values from 128 to 512, as said below
- time_embed: bfloat16 [32, 256], P(('dp', 'fsdp')), may hold values from -6 to 6
- cotangent: bfloat16 [32, 512, 1024], P(('dp', 'fsdp')), may hold values from -6 to 6
- time_weight: bfloat16 [256, 1024], P('fsdp'), may hold values from -0.1875 to 0.1875
- attn_gain: bfloat16 [1024], P('fsdp'), may hold values from 0.099609375 to 1.8984375
- attn_shift: bfloat16 [1024], P('fsdp'), may hold values from -3 to 3
- qkv_weight: bfloat16 [1024, 3072], P('fsdp'), may hold values from -0.1875 to 0.1875
- out_weight: bfloat16 [1024, 1024], P('fsdp'), may hold values from -0.75 to 0.75
- mlp_gain: bfloat16 [1024], P('fsdp'), may hold values from 0.099609375 to 1.8984375
- mlp_shift: bfloat16 [1024], P('fsdp'), may hold values from -3 to 3
- up_weight: bfloat16 [1024, 4096], P('fsdp'), may hold values from -0.1875 to 0.1875
- up_bias: bfloat16 [4096], P('fsdp'), may hold values from -3 to 3
- down_weight: bfloat16 [4096, 1024], P('fsdp'), may hold values from -0.09375 to 0.09375
- down_bias: bfloat16 [1024], P('fsdp'), may hold values from -3 to 3
Outputs:
- layer_out: bfloat16 [32, 512, 1024], P(('dp', 'fsdp'))
- token_grad: bfloat16 [32, 512, 1024], P(('dp', 'fsdp'))
- time_weight_grad: float32 [256, 1024], P('fsdp')
- attn_gain_grad: float32 [1024], P('fsdp')
- attn_shift_grad: float32 [1024], P('fsdp')
- qkv_weight_grad: float32 [1024, 3072], P('fsdp')
- out_weight_grad: float32 [1024, 1024], P('fsdp')
- mlp_gain_grad: float32 [1024], P('fsdp')
- mlp_shift_grad: float32 [1024], P('fsdp')
- up_weight_grad: float32 [1024, 4096], P('fsdp')
- up_bias_grad: float32 [4096], P('fsdp')
- down_weight_grad: float32 [4096, 1024], P('fsdp')
- down_bias_grad: float32 [1024], P('fsdp')
The draws below stay inside these ranges and needn't reach their ends.
Inputs may be any that keep to these rules, and one draw needn't show every extreme that they name: `lengths`: each sequence's count of real tokens; one sequence of every draw has 512.
All inputs are finite; a program needn't handle non-finite values.
Results may differ from the reference program's by a relative error of at most 0.02.
Values may be sent and summed in bfloat16 or wider, within the bound.
No kernel may reach another device: no remote copies, remote signals or barrier semaphores. Data moves between devices by JAX's collectives and lax.ppermute only.
A program may use at most 192 MiB of HBM per device.

```python
import math
import jax
import jax.numpy as jnp
from jax import lax

D = 1024
HEADS = 16
HD = 64
FF = 4096
TE = 256
LEN = 512
SEQS = 32


def draw_lengths(key, part):
    first, second, third = jax.random.split(jax.random.fold_in(key, 17), 3)
    halved = jax.random.randint(first, (SEQS,), 0, 4) // 2
    longest = jnp.where(halved == 0, LEN, LEN // 2)
    jitter = jax.random.randint(second, (SEQS,), 0, longest // 2 + 1)
    drawn = longest - jitter
    chosen = jax.random.randint(third, (), 0, SEQS)
    return jnp.where(jnp.arange(SEQS) == chosen, LEN, drawn).astype(jnp.int32)


def level_of(stream_key, shape, pieces, low, largest):
    level, own = 1.0, jax.random.fold_in(stream_key, 6)
    for dim, blocks in pieces:
        draws = jnp.exp(jax.random.uniform(jax.random.fold_in(own, dim), (blocks,), jnp.float32, low / len(pieces), largest / len(pieces)))
        level = level * jnp.repeat(draws, shape[dim] // blocks).reshape([-1 if axis == dim else 1 for axis in range(len(shape))])
    return level


def bell_draw(key, dims, spread, most, shards=(), kind=jnp.bfloat16):
    values = spread * jax.random.normal(key, dims, jnp.float32)
    if shards:
        values = values * level_of(key, dims, shards, -0.22, 0.18)
    return jnp.clip(values, -most, most).astype(kind)


def setup_inputs(seed: int = 0) -> dict:
    key_list = jax.random.split(jax.random.key(seed), 16)
    tokens = bell_draw(key_list[0], (SEQS, LEN, D), 1.0, 6.0, ((0, 32),))
    lengths = draw_lengths(jax.random.fold_in(key_list[15], 71), 0)
    time_embed = bell_draw(key_list[2], (SEQS, TE), 1.0, 6.0, ((0, 32),))
    cotangent = bell_draw(key_list[3], (SEQS, LEN, D), 1.0, 6.0, ((0, 32),))
    time_weight = bell_draw(key_list[4], (TE, D), (4 * TE) ** -0.5, 0.1875, ((0, 16),))
    attn_gain = jnp.clip(1.0 + 0.18 * jax.random.normal(key_list[5], (D,), jnp.float32), 0.099609375, 1.8984375).astype(jnp.bfloat16)
    attn_shift = bell_draw(key_list[6], (D,), 0.5, 3.0, ((0, 16),))
    qkv_weight = bell_draw(key_list[7], (D, 3 * D), D ** -0.5, 0.1875, ((0, 16),))
    out_weight = bell_draw(key_list[8], (D, D), (D // 16) ** -0.5, 0.75, ((0, 16),))
    mlp_gain = jnp.clip(1.0 + 0.18 * jax.random.normal(key_list[9], (D,), jnp.float32), 0.099609375, 1.8984375).astype(jnp.bfloat16)
    mlp_shift = bell_draw(key_list[10], (D,), 0.5, 3.0, ((0, 16),))
    up_weight = bell_draw(key_list[11], (D, FF), D ** -0.5, 0.1875, ((0, 16),))
    up_bias = bell_draw(key_list[12], (FF,), 0.5, 3.0, ((0, 16),))
    down_weight = bell_draw(key_list[13], (FF, D), FF ** -0.5, 0.09375, ((0, 16),))
    down_bias = bell_draw(key_list[14], (D,), 0.5, 3.0, ((0, 16),))
    return {"tokens": tokens, "lengths": lengths, "time_embed": time_embed, "cotangent": cotangent, "time_weight": time_weight, "attn_gain": attn_gain, "attn_shift": attn_shift, "qkv_weight": qkv_weight, "out_weight": out_weight, "mlp_gain": mlp_gain, "mlp_shift": mlp_shift, "up_weight": up_weight, "up_bias": up_bias, "down_weight": down_weight, "down_bias": down_bias}


@jax.custom_vjp
def low(v):
    return lax.optimization_barrier(v.astype(jnp.bfloat16)).astype(jnp.float32)

@jax.custom_vjp
def low_back(v):
    return v

def low_keep(v):
    return (low(v), None)

def low_pass(kept, grad):
    return (grad,)

def back_keep(v):
    return (v, None)

def back_low(kept, grad):
    return (low(grad),)
low.defvjp(low_keep, low_pass)
low_back.defvjp(back_keep, back_low)

def matmul(left, right):
    return jnp.matmul(left, right, precision=lax.Precision.HIGHEST)

def layer_norm(values_in, gain, shift):
    center = values_in - lax.optimization_barrier(jnp.mean(values_in, axis=-1, keepdims=True))
    variance = lax.optimization_barrier(jnp.mean(center * center, axis=-1, keepdims=True))
    return center * lax.rsqrt(variance + 1e-05) * gain + shift

def rotary_tables(length, head_size):
    half_size = head_size // 2
    frequency = jnp.exp(jnp.arange(half_size, dtype=jnp.float32) * (-2.0 * math.log(10000.0) / head_size))
    angles = jnp.arange(length, dtype=jnp.float32)[:, None] * frequency[None, :]
    angles = jnp.concatenate([angles, angles], axis=-1)
    return (jnp.cos(angles)[:, None, :], jnp.sin(angles)[:, None, :])

def rotate(values_in, cosine_table, sine_table):
    half_size = values_in.shape[-1] // 2
    turned = jnp.concatenate([-values_in[..., half_size:], values_in[..., :half_size]], axis=-1)
    return values_in * cosine_table + turned * sine_table

def forward(tokens, time_weight, attn_gain, attn_shift, qkv_weight, out_weight, mlp_gain, mlp_shift, up_weight, up_bias, down_weight, down_bias, time_embed, valid):
    seq_count, length, features = tokens.shape
    time_scale = 1.0 + matmul(time_embed, time_weight)[:, None, :]
    attn_in = low(layer_norm(tokens, attn_gain, attn_shift) * time_scale)
    qkv = low_back(matmul(attn_in, qkv_weight))
    cosine_table, sine_table = rotary_tables(length, HD)
    split = qkv.reshape(seq_count, length, 3, HEADS, HD)
    query = low(rotate(split[:, :, 0], cosine_table, sine_table))
    key_rows = low(rotate(split[:, :, 1], cosine_table, sine_table))
    value_rows = low(split[:, :, 2])
    scores = low_back(jnp.einsum('bqhd,bkhd->bhqk', query, key_rows, precision=lax.Precision.HIGHEST) * HD ** (-0.5))
    scores = jnp.where(valid[:, None, None, :], scores, -1000000000.0)
    attn_probs = low(jax.nn.softmax(scores, axis=-1))
    context = jnp.einsum('bhqk,bkhd->bqhd', attn_probs, value_rows, precision=lax.Precision.HIGHEST)
    context = low_back(low(context.reshape(seq_count, length, features)))
    hidden = tokens + low_back(matmul(context, out_weight))
    mlp_in = low(layer_norm(hidden, mlp_gain, mlp_shift) * time_scale)
    pre_act = low_back(matmul(mlp_in, up_weight) + up_bias)
    active = low(jax.nn.gelu(pre_act))
    return hidden + low_back(matmul(active, down_weight) + down_bias)

def reference(tokens, lengths, time_embed, cotangent, time_weight, attn_gain, attn_shift, qkv_weight, out_weight, mlp_gain, mlp_shift, up_weight, up_bias, down_weight, down_bias):
    weights = tuple((item.astype(jnp.float32) for item in (time_weight, attn_gain, attn_shift, qkv_weight, out_weight, mlp_gain, mlp_shift, up_weight, up_bias, down_weight, down_bias)))
    length = tokens.shape[1]
    group_size = math.gcd(tokens.shape[0], max(1, 4096 // length))
    group_count = tokens.shape[0] // group_size
    positions = jnp.arange(length, dtype=jnp.int32)

    def regroup(array):
        return array.reshape((group_count, group_size) + array.shape[1:])

    def one_group(totals, group_inputs):
        group_tokens, group_lengths, group_embed, group_grad = group_inputs
        valid = positions[None, :] < group_lengths[:, None].astype(jnp.int32)
        embed_full = group_embed.astype(jnp.float32)

        def local_forward(tokens_full, *params):
            return forward(tokens_full, *params, embed_full, valid)
        result, pullback = jax.vjp(local_forward, group_tokens.astype(jnp.float32), *weights)
        pulled = pullback(group_grad.astype(jnp.float32) * valid[:, :, None].astype(jnp.float32))
        totals = tuple((total + part for total, part in zip(totals, pulled[1:])))
        return (totals, (result.astype(jnp.bfloat16), pulled[0].astype(jnp.bfloat16)))
    zeros_init = tuple((jnp.zeros(item.shape, jnp.float32) for item in weights))
    totals, (outs_all, grads_all) = lax.scan(one_group, zeros_init, (regroup(tokens), regroup(lengths), regroup(time_embed), regroup(cotangent)))
    return (outs_all.reshape(tokens.shape), grads_all.reshape(tokens.shape), totals[0], totals[1], totals[2], totals[3], totals[4], totals[5], totals[6], totals[7], totals[8], totals[9], totals[10])
```

```python
import functools
import math

import jax
import jax.numpy as jnp
from jax import lax
from jax.experimental import pallas as pl
from jax.experimental.pallas import tpu as pltpu
from jax.sharding import PartitionSpec as P

HEADS = 16
HD = 64
ZN = 4
F32 = jnp.float32
BF16 = jnp.bfloat16


def normalize(values_in):
    center = values_in - jnp.mean(values_in, axis=-1, keepdims=True)
    inverse = lax.rsqrt(jnp.mean(center * center, axis=-1, keepdims=True) + 1e-05)
    return (center * inverse, inverse)


def norm_back(grad_hat, normed, inverse):
    return inverse * (
        grad_hat
        - jnp.mean(grad_hat, axis=-1, keepdims=True)
        - normed * jnp.mean(grad_hat * normed, axis=-1, keepdims=True)
    )


def rotary_tables(length, head_size):
    half_size = head_size // 2
    frequency = jnp.exp(
        jnp.arange(half_size, dtype=F32) * (-2.0 * math.log(10000.0) / head_size)
    )
    angles = jnp.arange(length, dtype=F32)[:, None] * frequency[None, :]
    angles = jnp.concatenate([angles, angles], axis=-1)
    return (jnp.cos(angles)[:, None, :], jnp.sin(angles)[:, None, :])


def rotate(values_in, cosine_table, sine_table):
    half_size = values_in.shape[-1] // 2
    turned = jnp.concatenate([-values_in[..., half_size:], values_in[..., :half_size]], axis=-1)
    return values_in * cosine_table + turned * sine_table


def rotate_back(grad_in, cosine_table, sine_table):
    half_size = grad_in.shape[-1] // 2
    sined = grad_in * sine_table
    return grad_in * cosine_table + jnp.concatenate(
        [sined[..., half_size:], -sined[..., :half_size]], axis=-1
    )


def rows_dot(left, right):
    return lax.dot_general(
        left, right, (((0,), (0,)), ((), ())), preferred_element_type=F32
    )


def back_dot(grad_in, weight):
    return lax.dot_general(
        grad_in, weight, (((1,), (1,)), ((), ())), preferred_element_type=F32
    )


class Net:
    def __init__(self, dp, fs):
        self.dp, self.fs = dp, fs
        self.yn = fs // (2 * ZN)
        index = lax.axis_index("fsdp")
        self.me = index
        self.z0 = index // (2 * self.yn)
        self.y0 = (index // 2) % self.yn
        self.c0 = index % 2
        self.p0 = lax.axis_index("dp") % 2

    def place(self, z, y, c):
        return ((z % ZN) * self.yn + y % self.yn) * 2 + c % 2

    def split(self, i):
        return i // (2 * self.yn), (i // 2) % self.yn, i % 2

    def perm(self, values_in, dz, dy, dc):
        pairs = []
        for i in range(self.fs):
            z, y, c = self.split(i)
            pairs.append((i, self.place(z + dz, y + dy, c + dc)))
        return lax.ppermute(values_in, "fsdp", pairs)

    def z(self, values_in, k):
        return self.perm(values_in, k, 0, 0)

    def y(self, values_in, s):
        return self.perm(values_in, 0, s, 0)

    def c(self, values_in):
        return self.perm(values_in, 0, 0, 1)

    def x(self, values_in):
        return lax.ppermute(values_in, "dp", [(i, i ^ 1) for i in range(self.dp)])


def assemble_kernel(plan, rows, half, yn, where_ref, *refs):
    pieces, out_ref, held, sems, out_sem = refs[: len(plan)], refs[-4], refs[-3], refs[-2], refs[-1]
    z0, y0, c0, p0 = where_ref[0], where_ref[1], where_ref[2], where_ref[3]
    copies = []
    for piece_ref, (s, q, cq, first, count) in zip(pieces, plan):
        y = lax.rem(y0 + yn - s, yn)
        p = lax.rem(p0 + q, 2)
        c = lax.rem(c0 + cq, 2)
        for k in range(count):
            z = lax.rem(z0 + ZN - (first + k), ZN)
            start = pl.multiple_of(((z * yn + y) * 2 + c) * rows + p * half, half)
            copies.append(
                pltpu.make_async_copy(
                    piece_ref.at[pl.ds(k * half, half), :],
                    held.at[pl.ds(start, half), :],
                    sems.at[len(copies)],
                )
            )
    for copy in copies:
        copy.start()
    for copy in copies:
        copy.wait()
    back = pltpu.make_async_copy(held, out_ref, out_sem)
    back.start()
    back.wait()


def assemble(net, plan, pieces, rows, columns):
    half = rows // 2
    where = jnp.stack([net.z0, net.y0, net.c0, net.p0]).astype(jnp.int32)
    blocks = sum(entry[4] for entry in plan)
    total = net.fs * rows
    return pl.pallas_call(
        functools.partial(assemble_kernel, plan, rows, half, net.yn),
        out_shape=jax.ShapeDtypeStruct((total, columns), BF16),
        grid_spec=pltpu.PrefetchScalarGridSpec(
            num_scalar_prefetch=1,
            grid=(1,),
            in_specs=[pl.BlockSpec(memory_space=pl.ANY)] * len(pieces),
            out_specs=pl.BlockSpec(memory_space=pl.ANY),
            scratch_shapes=[
                pltpu.VMEM((total, columns), BF16),
                pltpu.SemaphoreType.DMA((blocks,)),
                pltpu.SemaphoreType.DMA,
            ],
        ),
        compiler_params=pltpu.CompilerParams(vmem_limit_bytes=24 * 2**20),
        cost_estimate=pl.CostEstimate(
            flops=0, bytes_accessed=4 * total * columns, transcendentals=0
        ),
        name="assemble",
    )(where, *pieces)


def gather_weight(net, shard):
    rows, columns = shard.shape
    half = rows // 2
    own = lax.dynamic_slice_in_dim(shard, net.p0 * half, half, 0)
    line = jnp.concatenate([own] + [net.z(own, k) for k in range(1, ZN)], axis=0)
    across = net.x(line)
    beside = [net.y(line, s) for s in range(1, net.yn)]
    mid = (ZN // 2) * half
    corner_one = [net.x(item[:mid]) for item in beside]
    corner_two = [net.y(across[mid:], s) for s in range(1, net.yn)]
    plan = [(0, 0, 0, ZN), (0, 1, 0, ZN)]
    pieces = [line, across]
    for s in range(1, net.yn):
        plan += [(s, 0, 0, ZN), (s, 1, 0, ZN // 2), (s, 1, ZN // 2, ZN - ZN // 2)]
        pieces += [beside[s - 1], corner_one[s - 1], corner_two[s - 1]]
    full_plan = [(s, q, 0, first, count) for s, q, first, count in plan]
    full_plan += [(s, q, 1, first, count) for s, q, first, count in plan]
    return assemble(net, full_plan, pieces + [net.c(item) for item in pieces], rows, columns)


def gather_small(net, shard):
    rows, columns = shard.shape
    line = jnp.stack([shard] + [net.z(shard, k) for k in range(1, ZN)])
    sides = jnp.stack([line] + [net.y(line, s) for s in range(1, net.yn)], axis=1)
    both = jnp.stack([sides, net.c(sides)], axis=2)
    z_order = (net.z0 - jnp.arange(ZN)) % ZN
    y_order = (net.y0 - jnp.arange(net.yn)) % net.yn
    c_order = (net.c0 - jnp.arange(2)) % 2
    both = both[z_order][:, y_order][:, :, c_order]
    return both.reshape(net.fs, rows, columns)


def relative_order(net, rows, total):
    half = rows // 2
    d = jnp.arange(total, dtype=jnp.int32)
    f, i = d // rows, d % rows
    z, y, c = f // (2 * net.yn), (f // 2) % net.yn, f % 2
    p, j = i // half, i % half
    c, y, p, z = (c - net.c0) % 2, (y - net.y0) % net.yn, (p - net.p0) % 2, (z - net.z0) % ZN
    return (((c * net.yn + y) * 2 + p) * ZN + z) * half + j


def scatter_grad(net, keep, send, rows):
    half = rows // 2
    sent = net.c(send().astype(BF16))
    columns = sent.shape[1]
    total = (keep() + sent.astype(F32)).astype(BF16)
    blocks = total.reshape(net.yn, 2, ZN, half, columns)
    mid = ZN // 2
    zero_other, own = blocks[0, 1], blocks[0, 0].astype(F32)
    side = []
    for s in range(1, net.yn):
        came_x = net.x(blocks[s, 1, :mid])
        came_y = net.y(blocks[s, 1, mid:], s)
        head = (blocks[s, 0, :mid].astype(F32) + came_x.astype(F32)).astype(BF16)
        side.append(jnp.concatenate([head, blocks[s, 0, mid:]], axis=0))
        tail = (zero_other[mid:].astype(F32) + came_y.astype(F32)).astype(BF16)
        zero_other = jnp.concatenate([zero_other[:mid], tail], axis=0)
    own = own + net.x(zero_other).astype(F32)
    for s in range(1, net.yn):
        own = own + net.y(side[s - 1], s).astype(F32)
    own = own.astype(BF16)
    mine = own[0].astype(F32)
    for k in range(1, ZN):
        mine = mine + net.z(own[k], k).astype(F32)
    mine = mine.astype(BF16)
    if net.dp > 2:
        groups = [list(range(q, net.dp, 2)) for q in range(2)]
        mine = lax.psum(mine, "dp", axis_index_groups=groups)
    other = net.x(mine)
    first = jnp.where(net.p0 == 0, mine, other)
    second = jnp.where(net.p0 == 0, other, mine)
    return jnp.concatenate([first, second], axis=0).astype(F32)


def reduce_small(net, sums, rows):
    count = sums.shape[0]
    packed = jnp.concatenate([sums, rows], axis=0)
    if net.dp == 2:
        came = net.x(packed)
        low = jnp.where(net.p0 == 0, packed, came)
        high = jnp.where(net.p0 == 0, came, packed)
        packed = jnp.concatenate([low[:count] + high[:count], low[count:], high[count:]], axis=0)
    else:
        packed = jnp.concatenate(
            [lax.psum(sums, "dp"), lax.all_gather(rows, "dp", axis=0, tiled=True)], axis=0
        )

    def join(came_all):
        total = came_all[0][:count]
        for item in came_all[1:]:
            total = total + item[:count]
        return jnp.concatenate([total] + [item[count:] for item in came_all], axis=0)

    packed = join([packed, net.c(packed)])
    packed = join([packed] + [net.y(packed, s) for s in range(1, net.yn)])
    packed = join([packed] + [net.z(packed, k) for k in range(1, ZN)])
    return packed[:count], packed[count:]


def rows_kernel(order_ref, *refs):
    grad_ref, out_ref = refs[-2], refs[-1]
    for i, left_ref in enumerate(refs[:-2]):
        size = left_ref.shape[1]
        out_ref[i * size : (i + 1) * size, :] = lax.dot_general(
            left_ref[...], grad_ref[...], (((0,), (0,)), ((), ())), preferred_element_type=F32
        ).astype(BF16)


def rows_by_block(order, left, grad, block, per_step):
    depth, columns = grad.shape
    count = order.shape[0]

    def pick(j):
        return lambda i, order_ref: (0, order_ref[i * per_step + j])

    return pl.pallas_call(
        rows_kernel,
        out_shape=jax.ShapeDtypeStruct((count * block, columns), BF16),
        grid_spec=pltpu.PrefetchScalarGridSpec(
            num_scalar_prefetch=1,
            grid=(count // per_step,),
            in_specs=[pl.BlockSpec((depth, block), pick(j)) for j in range(per_step)]
            + [pl.BlockSpec((depth, columns), lambda i, order_ref: (0, 0))],
            out_specs=pl.BlockSpec((per_step * block, columns), lambda i, order_ref: (i, 0)),
        ),
        cost_estimate=pl.CostEstimate(
            flops=2 * depth * count * block * columns,
            bytes_accessed=2 * (depth * columns + count * block * (columns + depth)),
            transcendentals=0,
        ),
        name="rows_by_block",
    )(order, *([left] * per_step), grad)


def scores_of(query_pair, key_pair, key_mask, factor):
    raw_scores = (
        jnp.einsum("bqgd,bkgd->bgqk", query_pair, key_pair, preferred_element_type=F32)
        * factor
    )
    return jnp.where(key_mask[:, None, None, :], raw_scores, -1000000000.0)


def per_device(
    dp,
    fs,
    tokens,
    lengths,
    time_embed,
    cotangent,
    time_weight,
    attn_gain,
    attn_shift,
    qkv_weight,
    out_weight,
    mlp_gain,
    mlp_shift,
    up_weight,
    up_bias,
    down_weight,
    down_bias,
):
    net = Net(dp, fs)
    seq_count, length, features = tokens.shape
    flat_rows = seq_count * length
    pair_count = HEADS // 2
    factor = HD ** (-0.5)
    width = features
    vectors = [attn_gain, attn_shift, mlp_gain, mlp_shift, down_bias, up_bias]
    edges = [0]
    for item in vectors:
        edges.append(edges[-1] + item.shape[0])
    lanes = -(-edges[-1] // width) * width
    strip = jnp.concatenate(vectors + [jnp.zeros((lanes - edges[-1],), BF16)])
    small = jnp.concatenate([time_weight, strip.reshape(-1, width)], axis=0)
    pad = -small.shape[0] % 16
    small = jnp.concatenate([small, jnp.zeros((pad, width), BF16)], axis=0)
    small_full = gather_small(net, small)
    te_rows = time_weight.shape[0]
    time_full = small_full[:, :te_rows].reshape(fs * te_rows, width)
    strips = small_full[:, te_rows : te_rows + lanes // width].reshape(fs, lanes)
    gain_one, shift_one, gain_two, shift_two, down_bias_full, up_bias_full = (
        strips[:, a:b].reshape(-1).astype(F32) for a, b in zip(edges[:-1], edges[1:])
    )
    qkv_full = gather_weight(net, qkv_weight)
    out_full = gather_weight(net, out_weight)
    up_full = gather_weight(net, up_weight)
    down_full = gather_weight(net, down_weight)

    wide_rows = qkv_weight.shape[0]
    order = relative_order(net, wide_rows, features)
    permute = (order[:, None] == jnp.arange(features, dtype=jnp.int32)[None, :]).astype(BF16)

    def reorder(values_in):
        return jnp.dot(values_in, permute, preferred_element_type=F32).astype(BF16)

    key_mask = jnp.arange(length, dtype=jnp.int32)[None, :] < lengths[:, None]
    residual = tokens.astype(F32)
    time_scale = (
        1.0 + jnp.dot(time_embed, time_full, preferred_element_type=F32)[:, None, :]
    )
    normed_one, inverse_one = normalize(residual)
    affine_one = normed_one * gain_one + shift_one
    attn_in = (affine_one * time_scale).astype(BF16).reshape(flat_rows, features)
    qkv = jnp.dot(attn_in, qkv_full, preferred_element_type=F32).reshape(
        seq_count, length, 3, HEADS, HD
    )
    cosine_table, sine_table = rotary_tables(length, HD)
    query_rows = rotate(qkv[:, :, 0], cosine_table, sine_table).astype(BF16)
    key_rows = rotate(qkv[:, :, 1], cosine_table, sine_table).astype(BF16)
    value_rows = qkv[:, :, 2].astype(BF16)

    def by_pairs(values_in):
        return values_in.reshape(seq_count, length, pair_count, 2, HD).transpose(2, 0, 1, 3, 4)

    def from_pairs(values_in):
        return values_in.transpose(1, 2, 0, 3, 4).reshape(seq_count, length, features)

    query_group = by_pairs(query_rows)
    key_group = by_pairs(key_rows)
    value_group = by_pairs(value_rows)

    def attend(operands):
        query_pair, key_pair, value_pair = operands
        scores = scores_of(query_pair, key_pair, key_mask, factor)
        row_max = jnp.max(scores, axis=-1, keepdims=True)
        exponent = jnp.exp(scores - row_max)
        row_total = jnp.sum(exponent, axis=-1, keepdims=True)
        attn_probs = (exponent / row_total).astype(BF16)
        mixed_rows = jnp.einsum(
            "bgqk,bkgd->bqgd", attn_probs, value_pair, preferred_element_type=F32
        )
        return (mixed_rows.astype(BF16), (row_max + jnp.log(row_total))[..., 0])

    context_group, log_totals = lax.map(attend, (query_group, key_group, value_group))
    context = from_pairs(context_group).reshape(flat_rows, features)
    hidden = residual + jnp.dot(context, out_full, preferred_element_type=F32).reshape(
        seq_count, length, features
    )
    normed_two, inverse_two = normalize(hidden)
    affine_two = normed_two * gain_two + shift_two
    mlp_in = (affine_two * time_scale).astype(BF16).reshape(flat_rows, features)
    pre_act = jnp.dot(mlp_in, up_full, preferred_element_type=F32) + up_bias_full
    active = jax.nn.gelu(pre_act).astype(BF16)
    branch_out = jnp.dot(active, down_full, preferred_element_type=F32) + down_bias_full
    layer_out = (hidden + branch_out.reshape(seq_count, length, features)).astype(BF16)

    grad_out = cotangent.astype(F32) * key_mask[:, :, None].astype(F32)
    grad_branch = grad_out.astype(BF16).reshape(flat_rows, features)
    tall_rows = down_weight.shape[0]
    tall_half = tall_rows // 2
    spots = relative_order(net, tall_rows, fs * tall_rows)[::tall_half] // tall_half
    block_order = jnp.argsort(spots).astype(jnp.int32)

    def tall_grad(first, last):
        if tall_half % 128 == 0:
            return rows_by_block(block_order[first:last], active, grad_branch, tall_half, 2)
        whole = rows_dot(active, grad_branch).astype(BF16)
        picked = whole.reshape(-1, tall_half, features)[block_order[first:last]]
        return picked.reshape(-1, features)

    down_weight_grad = scatter_grad(
        net,
        lambda: tall_grad(0, fs).astype(F32),
        lambda: tall_grad(fs, 2 * fs),
        tall_rows,
    )
    down_bias_grad = jnp.sum(grad_branch.astype(F32), axis=0)
    grad_active = back_dot(grad_branch, down_full)
    gelu_value, gelu_pull = jax.vjp(jax.nn.gelu, pre_act)
    grad_pre = gelu_pull(grad_active)[0].astype(BF16)
    up_bias_grad = jnp.sum(grad_pre.astype(F32), axis=0)

    def wide_grad(left, right):
        moved = reorder(left)
        half_width = features // 2
        return scatter_grad(
            net,
            lambda: rows_dot(moved[:, :half_width], right),
            lambda: rows_dot(moved[:, half_width:], right),
            wide_rows,
        )

    up_weight_grad = wide_grad(mlp_in, grad_pre)
    grad_mlp_in = back_dot(grad_pre, up_full).reshape(seq_count, length, features)
    grad_affine_two = grad_mlp_in * time_scale
    grad_scale = jnp.sum(grad_mlp_in * affine_two, axis=1)
    mlp_gain_grad = jnp.sum(grad_affine_two * normed_two, axis=(0, 1))
    mlp_shift_grad = jnp.sum(grad_affine_two, axis=(0, 1))
    grad_hidden = grad_out + norm_back(grad_affine_two * gain_two, normed_two, inverse_two)
    grad_attn = grad_hidden.astype(BF16).reshape(flat_rows, features)
    out_weight_grad = wide_grad(context, grad_attn)
    grad_context = back_dot(grad_attn, out_full).astype(BF16)

    def attend_back(operands):
        query_pair, key_pair, value_pair, log_pair, grad_pair = operands
        scores = scores_of(query_pair, key_pair, key_mask, factor)
        probs_full = jnp.exp(scores - log_pair[..., None])
        attn_probs = probs_full.astype(BF16)
        grad_value = jnp.einsum(
            "bgqk,bqgd->bkgd", attn_probs, grad_pair, preferred_element_type=F32
        )
        grad_probs = jnp.einsum(
            "bqgd,bkgd->bgqk", grad_pair, value_pair, preferred_element_type=F32
        )
        grad_scores = probs_full * (
            grad_probs - jnp.sum(grad_probs * probs_full, axis=-1, keepdims=True)
        )
        grad_scores = grad_scores.astype(BF16)
        grad_query = (
            jnp.einsum("bgqk,bkgd->bqgd", grad_scores, key_pair, preferred_element_type=F32)
            * factor
        )
        grad_key = (
            jnp.einsum("bgqk,bqgd->bkgd", grad_scores, query_pair, preferred_element_type=F32)
            * factor
        )
        return (grad_query, grad_key, grad_value)

    grad_query_group, grad_key_group, grad_value_group = lax.map(
        attend_back, (query_group, key_group, value_group, log_totals, by_pairs(grad_context))
    )
    head_shape = (seq_count, length, HEADS, HD)
    grad_query_raw = rotate_back(
        from_pairs(grad_query_group).reshape(head_shape), cosine_table, sine_table
    )
    grad_key_raw = rotate_back(
        from_pairs(grad_key_group).reshape(head_shape), cosine_table, sine_table
    )
    grad_value_raw = from_pairs(grad_value_group).reshape(head_shape)
    grad_qkv = (
        jnp.stack([grad_query_raw, grad_key_raw, grad_value_raw], axis=2)
        .astype(BF16)
        .reshape(flat_rows, 3 * features)
    )
    qkv_weight_grad = wide_grad(attn_in, grad_qkv)
    grad_attn_in = back_dot(grad_qkv, qkv_full).reshape(seq_count, length, features)
    grad_affine_one = grad_attn_in * time_scale
    grad_scale = grad_scale + jnp.sum(grad_attn_in * affine_one, axis=1)
    attn_gain_grad = jnp.sum(grad_affine_one * normed_one, axis=(0, 1))
    attn_shift_grad = jnp.sum(grad_affine_one, axis=(0, 1))
    token_grad = (
        grad_hidden + norm_back(grad_affine_one * gain_one, normed_one, inverse_one)
    ).astype(BF16)

    sums = [attn_gain_grad, attn_shift_grad, mlp_gain_grad, mlp_shift_grad, down_bias_grad]
    embed = time_embed.shape[1]
    wide = jnp.concatenate(
        [jnp.stack(sums), up_bias_grad.reshape(-1, features)], axis=0
    )
    wide = jnp.concatenate([wide, jnp.zeros((wide.shape[0], embed), F32)], axis=1)
    row = jnp.concatenate([grad_scale, time_embed.astype(F32)], axis=1)
    totals, collected = reduce_small(net, wide, row)
    totals = totals[:, :features]
    vector_grads = [
        lax.dynamic_slice_in_dim(totals[i], net.me * attn_gain.shape[0], attn_gain.shape[0])
        for i in range(5)
    ]
    up_bias_out = lax.dynamic_slice_in_dim(
        totals[5:].reshape(-1), net.me * up_bias.shape[0], up_bias.shape[0]
    )
    embeds = lax.dynamic_slice_in_dim(collected[:, features:], net.me * te_rows, te_rows, 1)
    time_weight_grad = lax.dot_general(
        embeds,
        collected[:, :features],
        (((0,), (0,)), ((), ())),
        precision=lax.Precision.HIGHEST,
        preferred_element_type=F32,
    )
    return (
        layer_out,
        token_grad,
        time_weight_grad,
        vector_grads[0],
        vector_grads[1],
        qkv_weight_grad,
        out_weight_grad,
        vector_grads[2],
        vector_grads[3],
        up_weight_grad,
        up_bias_out,
        down_weight_grad,
        vector_grads[4],
    )


def solution(mesh):
    return jax.shard_map(
        functools.partial(per_device, mesh.shape["dp"], mesh.shape["fsdp"]),
        mesh=mesh,
        in_specs=(
            P(("dp", "fsdp"), None, None),
            P(("dp", "fsdp")),
            P(("dp", "fsdp"), None),
            P(("dp", "fsdp"), None, None),
            P("fsdp", None),
            P("fsdp"),
            P("fsdp"),
            P("fsdp", None),
            P("fsdp", None),
            P("fsdp"),
            P("fsdp"),
            P("fsdp", None),
            P("fsdp"),
            P("fsdp", None),
            P("fsdp"),
        ),
        out_specs=(
            P(("dp", "fsdp"), None, None),
            P(("dp", "fsdp"), None, None),
            P("fsdp", None),
            P("fsdp"),
            P("fsdp"),
            P("fsdp", None),
            P("fsdp", None),
            P("fsdp"),
            P("fsdp"),
            P("fsdp", None),
            P("fsdp"),
            P("fsdp", None),
            P("fsdp"),
        ),
        check_vma=False,
    )
```

```python
import functools
import math

import jax
import jax.numpy as jnp
from jax import lax
from jax.experimental import pallas as pl
from jax.experimental.pallas import tpu as pltpu
from jax.sharding import PartitionSpec as P

HD = 64
ZN = 4
PAIR = 128
LOG2E = math.log2(math.e)
ROOT = math.sqrt(2.0 / math.pi)
F32 = jnp.float32
BF16 = jnp.bfloat16


def normalize(values_in):
    center = values_in - jnp.mean(values_in, axis=-1, keepdims=True)
    inverse = lax.rsqrt(jnp.mean(center * center, axis=-1, keepdims=True) + 1e-05)
    return (center * inverse, inverse)


def norm_back(grad_hat, normed, inverse):
    return inverse * (
        grad_hat
        - jnp.mean(grad_hat, axis=-1, keepdims=True)
        - normed * jnp.mean(grad_hat * normed, axis=-1, keepdims=True)
    )


def rows_dot(left, right):
    return lax.dot_general(
        left, right, (((0,), (0,)), ((), ())), preferred_element_type=F32
    )


def back_dot(grad_in, weight):
    return lax.dot_general(
        grad_in, weight, (((1,), (1,)), ((), ())), preferred_element_type=F32
    )


def rotary_tables(length):
    half_size = HD // 2
    frequency = jnp.exp(
        jnp.arange(half_size, dtype=F32) * (-2.0 * math.log(10000.0) / HD)
    )
    angles = jnp.arange(length, dtype=F32)[:, None] * frequency[None, :]
    angles = jnp.concatenate([angles] * (PAIR // half_size), axis=-1)
    return (jnp.cos(angles), jnp.sin(angles))


class Order:
    def __init__(self):
        self.mark = ()

    def __call__(self, *arrays):
        out = lax.optimization_barrier((*arrays, *self.mark))[: len(arrays)]
        self.mark = (out[0],)
        return out[0] if len(out) == 1 else out

    def note(self, *arrays):
        self.mark = arrays
        return arrays[0] if len(arrays) == 1 else arrays


def scoped(name):
    def wrap(function):
        @functools.wraps(function)
        def inner(*args, **kwargs):
            with jax.named_scope(name):
                return function(*args, **kwargs)

        return inner

    return wrap


class Net:
    def __init__(self, dp, fs):
        self.dp, self.fs = dp, fs
        self.yn = fs // (2 * ZN)
        index = lax.axis_index("fsdp")
        self.me = index
        self.z0 = index // (2 * self.yn)
        self.y0 = (index // 2) % self.yn
        self.c0 = index % 2
        self.p0 = lax.axis_index("dp") % 2

    def perm(self, values_in, zx, dy, dc):
        pairs = []
        for i in range(self.fs):
            z, y, c = i // (2 * self.yn), (i // 2) % self.yn, i % 2
            to = ((z ^ zx) * self.yn + (y + dy) % self.yn) * 2 + (c ^ dc)
            pairs.append((i, to))
        return lax.ppermute(values_in, "fsdp", pairs)

    @scoped("z_hop")
    def z(self, values_in, k):
        return self.perm(values_in, k, 0, 0)

    @scoped("y_hop")
    def y(self, values_in, s):
        return self.perm(values_in, 0, s, 0)

    @scoped("core_hop")
    def c(self, values_in):
        return self.perm(values_in, 0, 0, 1)

    @scoped("x_hop")
    def x(self, values_in):
        return lax.ppermute(values_in, "dp", [(i, i ^ 1) for i in range(self.dp)])


def stack_kernel(*refs):
    at = 0
    for item in refs[:-1]:
        rows = item.shape[0]
        refs[-1][at : at + rows, :] = item[...]
        at += rows


def stack_rows(*items):
    rows = sum(item.shape[0] for item in items)
    return pl.pallas_call(
        stack_kernel,
        out_shape=jax.ShapeDtypeStruct((rows, items[0].shape[1]), items[0].dtype),
        cost_estimate=cost(),
        name="stack_rows",
    )(*items)


class Gather:
    def __init__(self, net, shard):
        self.net = net
        self.rows, self.columns = shard.shape
        self.half = self.rows // 2
        self.own = lax.dynamic_slice_in_dim(shard, net.p0 * self.half, self.half, 0)

    def along(self, own):
        self.own = own
        self.parts = [self.net.z(own, k) for k in range(1, ZN)]

    def join_line(self, order):
        self.line = stack_rows(*order(self.own, *self.parts))

    def across(self):
        net = self.net
        self.over = net.x(self.line)
        self.beside = [net.y(self.line, s) for s in range(1, net.yn)]

    def join_across(self, order):
        self.over, *self.beside = order(self.over, *self.beside)

    def corners(self):
        net = self.net
        mid = (ZN // 2) * self.half
        self.corner_one = [net.x(item[:mid]) for item in self.beside]
        self.corner_two = [net.y(self.over[mid:], s) for s in range(1, net.yn)]
        self.pieces = [self.line, self.over] + self.beside
        self.plan = [(0, 0, 0, ZN), (0, 1, 0, ZN)]
        self.plan += [(s, 0, 0, ZN) for s in range(1, net.yn)]
        self.moved = [net.c(item) for item in self.pieces]

    def finish(self, order):
        net = self.net
        late = order(*self.corner_one, *self.corner_two)
        plan = [(s, 1, 0, ZN // 2) for s in range(1, net.yn)]
        plan += [(s, 1, ZN // 2, ZN - ZN // 2) for s in range(1, net.yn)]
        pieces = self.pieces + list(late) + self.moved + [net.c(item) for item in late]
        plan = self.plan + plan
        full = [(s, q, side, first, count) for side in range(2) for s, q, first, count in plan]
        return full, pieces


def piece_spots(plan, where_ref, rows, half, yn):
    z0, y0, c0, p0 = where_ref[0], where_ref[1], where_ref[2], where_ref[3]
    spots = []
    for i, (s, q, side, first, count) in enumerate(plan):
        y = lax.rem(y0 + yn - s, yn)
        p = lax.rem(p0 + q, 2)
        c = lax.rem(c0 + side, 2)
        for k in range(count):
            z = lax.bitwise_xor(z0, jnp.int32(first + k))
            start = pl.multiple_of(((z * yn + y) * 2 + c) * rows + p * half, half)
            spots.append((i, k * half, first + k, start))
    return spots


def pack_kernel(*refs):
    time_ref, vectors, out_ref = refs[0], refs[1:-1], refs[-1]
    out_ref[...] = jnp.zeros_like(out_ref)
    rows = time_ref.shape[0]
    out_ref[:rows, :] = time_ref[...]
    for i, item in enumerate(vectors):
        out_ref[rows + i : rows + i + 1, : item.shape[1]] = item[...]


def small_kernel(rows, te_rows, sizes, yn, where_ref, embed_ref, own_ref, other_ref, *refs):
    scale_ref, all_ref, outs, held, sems = refs[0], refs[1], refs[2:-2], refs[-2], refs[-1]
    z0, y0, c0 = where_ref[0], where_ref[1], where_ref[2]
    copies = []
    for side, piece_ref in enumerate((own_ref, other_ref)):
        c = lax.rem(c0 + side, 2)
        for s in range(yn):
            y = lax.rem(y0 + yn - s, yn)
            for k in range(ZN):
                z = lax.bitwise_xor(z0, jnp.int32(k))
                copies.append(
                    pltpu.make_async_copy(
                        piece_ref.at[s * ZN + k],
                        held.at[(z * yn + y) * 2 + c],
                        sems.at[len(copies)],
                    )
                )
    for copy in copies:
        copy.start()
    for copy in copies:
        copy.wait()
    fs = held.shape[0]
    scale = jnp.ones_like(scale_ref)
    whole = jnp.concatenate([held[f, :te_rows, :] for f in range(fs)], axis=0)
    scale_ref[...] = scale + jnp.dot(embed_ref[...], whole, preferred_element_type=F32)
    for i, (size, out_ref) in enumerate(zip(sizes, outs)):
        pieces = [
            held[f, te_rows + i : te_rows + i + 1, :size].astype(F32) for f in range(fs)
        ]
        out_ref[...] = jnp.concatenate(pieces, axis=1)
    last, wide = te_rows + len(sizes), embed_ref.shape[1]
    all_ref[...] = jnp.concatenate(
        [held[f, last : last + 1, :wide].astype(F32) for f in range(fs)], axis=0
    )


class SmallGather:
    def __init__(self, net, time_weight, vectors, embed):
        self.net, self.sizes = net, [item.shape[0] for item in vectors]
        self.te_rows, self.width = time_weight.shape
        self.rows = self.te_rows + len(vectors) + 1
        self.rows += -self.rows % 16
        self.packed = pl.pallas_call(
            pack_kernel,
            out_shape=jax.ShapeDtypeStruct((self.rows, self.width), BF16),
            cost_estimate=cost(),
            name="pack_small",
        )(time_weight, *[item.reshape(1, -1) for item in vectors], embed)
        self.parts = [net.z(self.packed, k) for k in range(1, ZN)]

    def across(self, order):
        net = self.net
        self.line = jnp.stack(order(self.packed, *self.parts))
        self.beside = [net.y(self.line, s) for s in range(1, net.yn)]

    def other(self, order):
        self.line, *self.beside = order(self.line, *self.beside)
        self.sides = jnp.concatenate([self.line] + self.beside, axis=0)
        self.moved = self.net.c(self.sides)

    def finish(self, order, embed):
        net, fs = self.net, self.net.fs
        moved = order(self.moved)
        where = jnp.stack([net.z0, net.y0, net.c0]).astype(jnp.int32)
        shapes = [(1, self.width), (fs, embed.shape[1])]
        shapes += [(1, size * fs) for size in self.sizes]
        outs = pl.pallas_call(
            functools.partial(small_kernel, self.rows, self.te_rows, self.sizes, net.yn),
            out_shape=[jax.ShapeDtypeStruct(shape, F32) for shape in shapes],
            grid_spec=pltpu.PrefetchScalarGridSpec(
                num_scalar_prefetch=1,
                grid=(1,),
                in_specs=[pl.BlockSpec(embed.shape, lambda i, r: (0, 0))]
                + [pl.BlockSpec(memory_space=pl.ANY)] * 2,
                out_specs=[whole_spec(shape) for shape in shapes],
                scratch_shapes=[
                    pltpu.VMEM((fs, self.rows, self.width), BF16),
                    pltpu.SemaphoreType.DMA((fs,)),
                ],
            ),
            cost_estimate=cost(),
            name="small_join",
        )(where, embed, self.sides, moved)
        order.note(outs[0])
        return outs


def relative_order(net, rows, total):
    half = rows // 2
    d = jnp.arange(total, dtype=jnp.int32)
    f, i = d // rows, d % rows
    z, y, c = f // (2 * net.yn), (f // 2) % net.yn, f % 2
    p, j = i // half, i % half
    c, y, p, z = c ^ net.c0, (y - net.y0) % net.yn, p ^ net.p0, z ^ net.z0
    return (((c * net.yn + y) * 2 + p) * ZN + z) * half + j


def add_low(*items):
    total = items[0].astype(F32)
    for item in items[1:]:
        total = total + item.astype(F32)
    return total.astype(BF16)


def sum_kernel(counts, keep, *refs):
    total = sum(counts)
    kept_ref, sent_ref = refs[total], refs[total + 1]
    at, column = 0, 0
    for count in counts:
        items = refs[at : at + count]
        at += count
        wide = items[0].shape[1]
        value = items[0][...].astype(F32)
        for item in items[1:]:
            value = value + item[...].astype(F32)
        kept_ref[:, column : column + wide] = value[:keep, :]
        sent_ref[:, column : column + wide] = value[keep:, :].astype(BF16)
        column += wide


def sum_split(groups, keep):
    rows = groups[0][0].shape[0]
    columns = sum(group[0].shape[1] for group in groups)
    return pl.pallas_call(
        functools.partial(sum_kernel, [len(group) for group in groups], keep),
        out_shape=[
            jax.ShapeDtypeStruct((keep, columns), F32),
            jax.ShapeDtypeStruct((rows - keep, columns), BF16),
        ],
        cost_estimate=cost(),
        name="sum_split",
    )(*[item for group in groups for item in group])


class Scatter:
    def __init__(self, net, by_x):
        self.net, self.by_x = net, by_x

    def core(self, send):
        self.sent = self.net.c(send)

    def join_core(self, order):
        self.sent = order(self.sent)
        return self.sent

    def corners(self, own, over, *rest):
        net = self.net
        self.own, self.over, self.side = own, over, list(rest[0::2])
        if self.by_x:
            self.came = [net.x(item) for item in rest[1::2]]
        else:
            self.came = [net.y(item, s + 1) for s, item in enumerate(rest[1::2])]

    def across(self, order):
        net = self.net
        came = order(*self.came) if len(self.came) > 1 else [order(*self.came)]
        if self.by_x:
            self.side = [add_low(a, b) for a, b in zip(self.side, came)]
        else:
            self.over = add_low(self.over, *came)
        self.over = net.x(self.over)
        self.side = [net.y(item, s + 1) for s, item in enumerate(self.side)]

    def group(self, order):
        return [self.own, *order(self.over, *self.side)]


class Line:
    def __init__(self, net, half, groups):
        self.net, self.half = net, half
        self.kept, far = sum_split(groups, (ZN // 2) * half)
        self.far = net.z(far, 2)

    def nearer(self, order):
        self.here, near = sum_split([[self.kept, order(self.far)]], self.half)
        self.near = self.net.z(near, 1)

    def last(self, order):
        net = self.net
        mine = add_low(self.here, order(self.near))
        if net.dp > 2:
            groups = [list(range(q, net.dp, 2)) for q in range(2)]
            mine = lax.psum(mine, "dp", axis_index_groups=groups)
        self.mine, self.other = mine, net.x(mine)

    def finish(self, order):
        mine, other = self.mine, order(self.other)
        first = jnp.where(self.net.p0 == 0, mine, other)
        second = jnp.where(self.net.p0 == 0, other, mine)
        return jnp.concatenate([first, second], axis=0).astype(F32)


def kept_parts(yn, half):
    line = ZN * half
    return [(i * line, line) for i in range(2 * yn)]


def cost():
    return pl.CostEstimate(flops=1000, bytes_accessed=1000, transcendentals=0)


def weight_copies(plan, where_ref, rows, half, yn, pieces, targets, sems):
    spots = piece_spots(plan, where_ref, rows, half, yn)
    groups, count, column = [], 0, 0
    for target, first, wide in targets:
        group = []
        for i, row, shift, start in spots:
            group.append(
                pltpu.make_async_copy(
                    pieces[i].at[pl.ds(row, half), pl.ds(column, wide)],
                    target.at[pl.ds(start, half), pl.ds(first, wide)],
                    sems.at[count],
                )
            )
            count += 1
        column += wide
        groups.append(group)
    for group in groups:
        for copy in group:
            copy.start()
    return groups


def finish_copies(copies):
    for copy in copies:
        copy.wait()


def back_copy(held, out, first, wide, sem):
    spot = pl.ds(first, wide)
    copy = pltpu.make_async_copy(held.at[:, spot], out.at[:, spot], sem)
    copy.start()
    return copy


def qkv_kernel(plan, rows, half, yn, where_ref, x_ref, cos_ref, sin_ref, *refs):
    pieces = refs[: len(plan)]
    out_ref, wq_ref, wo_ref, wq, wo, low, sems, back_sems = refs[len(plan) :]
    wide = wo.shape[1]
    targets = [(wq, part * wide, wide) for part in range(3)] + [(wo, 0, wide)]
    groups = weight_copies(plan, where_ref, rows, half, yn, pieces, targets, sems)
    cosine, sine = cos_ref[...], sin_ref[...]
    front = lax.broadcasted_iota(jnp.int32, cosine.shape, 1) % HD < HD // 2
    backs = []
    for part in range(3):
        finish_copies(groups[part])
        backs.append(back_copy(wq, wq_ref, part * wide, wide, back_sems.at[part]))
        for j in range(wide // (2 * PAIR)):
            first = part * wide + j * 2 * PAIR
            acc = jnp.dot(
                x_ref[...], wq[:, first : first + 2 * PAIR], preferred_element_type=F32
            )
            for i in range(2):
                piece = acc[:, i * PAIR : (i + 1) * PAIR]
                if part < 2:
                    turned = jnp.where(
                        front,
                        -pltpu.roll(piece, PAIR - HD // 2, 1),
                        pltpu.roll(piece, HD // 2, 1),
                    )
                    piece = piece * cosine + turned * sine
                low[:, first + i * PAIR : first + (i + 1) * PAIR] = piece.astype(BF16)
        backs.append(back_copy(low, out_ref, part * wide, wide, back_sems.at[4 + part]))
    finish_copies(groups[3])
    backs.append(back_copy(wo, wo_ref, 0, wide, back_sems.at[3]))
    finish_copies(backs)


def where_of(net):
    return jnp.stack([net.z0, net.y0, net.c0, net.p0]).astype(jnp.int32)


ANY = pl.BlockSpec(memory_space=pl.ANY)


def whole_spec(shape):
    return pl.BlockSpec(shape, lambda i, r: (0, 0))


def qkv_rotated(net, x, plan, pieces, rows, cosine, sine):
    tokens, depth = x.shape
    total = net.fs * rows
    blocks = sum(entry[4] for entry in plan)
    half = rows // 2
    return pl.pallas_call(
        functools.partial(qkv_kernel, plan, rows, half, net.yn),
        grid_spec=pltpu.PrefetchScalarGridSpec(
            num_scalar_prefetch=1,
            grid=(1,),
            in_specs=[whole_spec(x.shape), whole_spec(cosine.shape), whole_spec(sine.shape)]
            + [ANY] * len(pieces),
            out_specs=[ANY] * 3,
            scratch_shapes=[
                pltpu.VMEM((total, 3 * depth), BF16),
                pltpu.VMEM((total, depth), BF16),
                pltpu.VMEM((tokens, 3 * depth), BF16),
                pltpu.SemaphoreType.DMA((4 * blocks,)),
                pltpu.SemaphoreType.DMA((7,)),
            ],
        ),
        out_shape=[
            jax.ShapeDtypeStruct((tokens, 3 * depth), BF16),
            jax.ShapeDtypeStruct((total, 3 * depth), BF16),
            jax.ShapeDtypeStruct((total, depth), BF16),
        ],
        compiler_params=pltpu.CompilerParams(vmem_limit_bytes=32 * 2**20),
        cost_estimate=cost(),
        name="qkv_rotated",
    )(where_of(net), x, cosine, sine, *pieces)


def up_kernel(x_ref, w_ref, b_ref, act_ref, slope_ref):
    wide = w_ref.shape[1]
    step = min(256, wide)
    for first in range(0, wide, step):
        spot = slice(first, first + step)
        v = jnp.dot(x_ref[...], w_ref[:, spot], preferred_element_type=F32) + b_ref[:, spot]
        square = v * v
        bend = jnp.tanh(v * (ROOT + ROOT * 0.044715 * square))
        half_up = 0.5 + 0.5 * bend
        act_ref[:, spot] = (v * half_up).astype(BF16)
        rise = 0.5 * ROOT + (1.5 * 0.044715 * ROOT) * square
        slope_ref[:, spot] = (half_up + v * (1.0 - bend * bend) * rise).astype(BF16)


def up_gelu(x, w, bias):
    rows, depth = x.shape
    total = w.shape[1]
    wide = min(1024, total)
    return pl.pallas_call(
        up_kernel,
        grid=(total // wide,),
        in_specs=[
            pl.BlockSpec((rows, depth), lambda j: (0, 0)),
            pl.BlockSpec((depth, wide), lambda j: (0, j)),
            pl.BlockSpec((1, wide), lambda j: (0, j)),
        ],
        out_specs=[pl.BlockSpec((rows, wide), lambda j: (0, j))] * 2,
        out_shape=[jax.ShapeDtypeStruct((rows, total), BF16)] * 2,
        cost_estimate=cost(),
        name="up_gelu",
    )(x, w, bias)


def down_kernel(plan, rows, half, yn, where_ref, g_ref, slope_ref, *refs):
    pieces = refs[: len(plan)]
    out_ref, sum_ref, w_ref, w, slope, low, sems, slope_sems, back_sems = refs[len(plan) :]
    spots = piece_spots(plan, where_ref, rows, half, yn)
    group_rows = w.shape[0] // ZN
    step = min(256, group_rows)
    z0 = where_ref[0]
    groups = [[] for _ in range(ZN)]
    for count, (i, row, shift, start) in enumerate(spots):
        copy = pltpu.make_async_copy(
            pieces[i].at[pl.ds(row, half), :], w.at[pl.ds(start, half), :], sems.at[count]
        )
        groups[shift].append(copy)
    slopes = []
    for k in range(ZN):
        at = pl.multiple_of(lax.bitwise_xor(z0, jnp.int32(k)) * group_rows, group_rows)
        for copy in groups[k]:
            copy.start()
        copy = pltpu.make_async_copy(
            slope_ref.at[:, pl.ds(at, group_rows)], slope.at[k], slope_sems.at[k]
        )
        copy.start()
        slopes.append(copy)
    backs = []
    for k in range(ZN):
        at = pl.multiple_of(lax.bitwise_xor(z0, jnp.int32(k)) * group_rows, group_rows)
        finish_copies(groups[k])
        slopes[k].wait()
        here = pl.ds(at, group_rows)
        copy = pltpu.make_async_copy(w.at[here, :], w_ref.at[here, :], back_sems.at[2 * k])
        copy.start()
        backs.append(copy)
        for j in range(group_rows // step):
            spot = slice(j * step, (j + 1) * step)
            inner = pl.multiple_of(at + j * step, step)
            acc = lax.dot_general(
                g_ref[...],
                w[pl.ds(inner, step), :],
                (((1,), (1,)), ((), ())),
                preferred_element_type=F32,
            )
            rounded = (acc * slope[k, :, spot].astype(F32)).astype(BF16)
            low[k, :, spot] = rounded
            sum_ref[:, pl.ds(inner, step)] = jnp.sum(
                rounded.astype(F32), axis=0, keepdims=True
            )
        copy = pltpu.make_async_copy(low.at[k], out_ref.at[:, here], back_sems.at[2 * k + 1])
        copy.start()
        backs.append(copy)
    finish_copies(backs)


def down_back(net, grad, plan, pieces, rows, slope):
    tokens, depth = grad.shape
    total = slope.shape[1]
    blocks = sum(entry[4] for entry in plan)
    return pl.pallas_call(
        functools.partial(down_kernel, plan, rows, rows // 2, net.yn),
        grid_spec=pltpu.PrefetchScalarGridSpec(
            num_scalar_prefetch=1,
            grid=(1,),
            in_specs=[whole_spec(grad.shape), ANY] + [ANY] * len(pieces),
            out_specs=[ANY, pl.BlockSpec((1, total), lambda i, r: (0, 0)), ANY],
            scratch_shapes=[
                pltpu.VMEM((total, depth), BF16),
                pltpu.VMEM((ZN, tokens, total // ZN), BF16),
                pltpu.VMEM((ZN, tokens, total // ZN), BF16),
                pltpu.SemaphoreType.DMA((blocks,)),
                pltpu.SemaphoreType.DMA((ZN,)),
                pltpu.SemaphoreType.DMA((2 * ZN,)),
            ],
        ),
        out_shape=[
            jax.ShapeDtypeStruct((tokens, total), BF16),
            jax.ShapeDtypeStruct((1, total), F32),
            jax.ShapeDtypeStruct((total, depth), BF16),
        ],
        compiler_params=pltpu.CompilerParams(vmem_limit_bytes=40 * 2**20),
        cost_estimate=cost(),
        name="down_back",
    )(where_of(net), grad, slope, *pieces)


def attend_kernel(len_ref, q_ref, k_ref, v_ref, out_ref):
    q, k, v = q_ref[...], k_ref[...], v_ref[...]
    length = k.shape[0]
    first = lax.broadcasted_iota(jnp.int32, q.shape, 1) < HD
    valid = lax.broadcasted_iota(jnp.int32, (1, length), 1) < len_ref[0]
    zero = jnp.zeros_like(q)
    outs = []
    for h in range(2):
        one = jnp.where(first, q, zero) if h == 0 else jnp.where(first, zero, q)
        scores = lax.dot_general(
            one, k, (((1,), (1,)), ((), ())), preferred_element_type=F32
        )
        scores = jnp.where(valid, scores * HD**-0.5, -1000000000.0)
        top = jnp.max(scores, axis=1, keepdims=True)
        exponent = jnp.exp2((scores - top) * LOG2E)
        total = jnp.sum(exponent, axis=1, keepdims=True)
        mixed = jnp.dot(exponent.astype(BF16), v, preferred_element_type=F32)
        outs.append(mixed * (1.0 / total))
    out_ref[...] = jnp.where(first, outs[0], outs[1]).astype(BF16)


def attend(length, qkv, first_pair, pairs):
    rows, total = qkv.shape
    count = total // 3 // PAIR

    def pick(part):
        return pl.BlockSpec((rows, PAIR), lambda j, r: (0, part * count + first_pair + j))

    return pl.pallas_call(
        attend_kernel,
        grid_spec=pltpu.PrefetchScalarGridSpec(
            num_scalar_prefetch=1,
            grid=(pairs,),
            in_specs=[pick(0), pick(1), pick(2)],
            out_specs=pl.BlockSpec((rows, PAIR), lambda j, r: (0, j)),
        ),
        out_shape=jax.ShapeDtypeStruct((rows, pairs * PAIR), BF16),
        cost_estimate=cost(),
        name="attend",
    )(length, qkv, qkv, qkv)


def attend_back_kernel(len_ref, q_ref, k_ref, v_ref, g_ref, cos_ref, sin_ref, out_ref):
    q, k, v, g = q_ref[...], k_ref[...], v_ref[...], g_ref[...]
    length = k.shape[0]
    lane = lax.broadcasted_iota(jnp.int32, q.shape, 1)
    first = lane < HD
    valid = lax.broadcasted_iota(jnp.int32, (length, length), 0) < len_ref[0]
    zero = jnp.zeros_like(q)
    grads = []
    for h in range(2):
        key = jnp.where(first, k, zero) if h == 0 else jnp.where(first, zero, k)
        value = jnp.where(first, v, zero) if h == 0 else jnp.where(first, zero, v)
        scores = lax.dot_general(
            key, q, (((1,), (1,)), ((), ())), preferred_element_type=F32
        )
        scores = jnp.where(valid, scores * HD**-0.5, -1000000000.0)
        top = jnp.max(scores, axis=0, keepdims=True)
        exponent = jnp.exp2((scores - top) * LOG2E)
        total = jnp.sum(exponent, axis=0, keepdims=True)
        probs = exponent * (1.0 / total)
        grad_probs = lax.dot_general(
            value, g, (((1,), (1,)), ((), ())), preferred_element_type=F32
        )
        delta = jnp.sum(grad_probs * probs, axis=0, keepdims=True)
        grad_scores = (probs * (grad_probs - delta)).astype(BF16)
        grads.append(
            (
                lax.dot_general(
                    grad_scores, k, (((0,), (0,)), ((), ())), preferred_element_type=F32
                ),
                jnp.dot(grad_scores, q, preferred_element_type=F32),
                jnp.dot(probs.astype(BF16), g, preferred_element_type=F32),
            )
        )
    front = lane % HD < HD // 2
    cosine, sine = cos_ref[...] * HD**-0.5, sin_ref[...] * HD**-0.5
    for i in range(2):
        grad = jnp.where(first, grads[0][i], grads[1][i])
        sined = grad * sine
        turned = jnp.where(
            front, pltpu.roll(sined, PAIR - HD // 2, 1), -pltpu.roll(sined, HD // 2, 1)
        )
        out_ref[i] = (grad * cosine + turned).astype(BF16)
    out_ref[2] = jnp.where(first, grads[0][2], grads[1][2]).astype(BF16)


def attend_back(length, qkv, grad, cosine, sine, first_pair, pairs):
    rows, total = qkv.shape
    count = total // 3 // PAIR

    def pick(part):
        return pl.BlockSpec((rows, PAIR), lambda j, r: (0, part * count + first_pair + j))

    table = pl.BlockSpec((rows, PAIR), lambda j, r: (0, 0))
    return pl.pallas_call(
        attend_back_kernel,
        grid_spec=pltpu.PrefetchScalarGridSpec(
            num_scalar_prefetch=1,
            grid=(pairs,),
            in_specs=[pick(0), pick(1), pick(2), pick(0), table, table],
            out_specs=pl.BlockSpec((3, rows, PAIR), lambda j, r: (0, 0, j)),
        ),
        out_shape=jax.ShapeDtypeStruct((3, rows, pairs * PAIR), BF16),
        cost_estimate=cost(),
        name="attend_back",
    )(length, qkv, qkv, qkv, grad, cosine, sine)


def tall_kernel(left_ref, grad_ref, out_ref):
    out_ref[...] = lax.dot_general(
        left_ref[...], grad_ref[...], (((0,), (0,)), ((), ())), preferred_element_type=F32
    ).astype(BF16)


def tall_rows_dot(left, grad):
    depth, columns = grad.shape
    total = left.shape[1]
    tall = min(1024, total)
    return pl.pallas_call(
        tall_kernel,
        grid=(total // tall,),
        in_specs=[
            pl.BlockSpec((depth, tall), lambda i: (0, i)),
            pl.BlockSpec((depth, columns), lambda i: (0, 0)),
        ],
        out_specs=pl.BlockSpec((tall, columns), lambda i: (i, 0)),
        out_shape=jax.ShapeDtypeStruct((total, columns), BF16),
        cost_estimate=cost(),
        name="tall_rows_dot",
    )(left, grad)


def wide_kernel(bounds, parts, *refs):
    step = pl.program_id(0)
    operands, rest = refs[: 2 * len(bounds)], refs[2 * len(bounds) :]

    def write(left_ref, grad_ref):
        grad = grad_ref[0] if len(grad_ref.shape) == 3 else grad_ref[...]
        acc = jnp.dot(left_ref[...], grad, preferred_element_type=F32)
        if parts is None:
            rest[-1][...] = acc.astype(BF16)
            return
        acc = acc + rest[0][...].astype(F32)
        for (first, rows), out_ref in zip(parts, rest[1:]):
            out_ref[...] = acc[first : first + rows, :].astype(BF16)

    for i, (low, high) in enumerate(bounds):

        @pl.when((step >= low) & (step < high))
        def _(i=i):
            write(operands[2 * i], operands[2 * i + 1])


def wide_rows_dot(at, rows, pairs, extra=None, parts=None):
    in_specs, args, bounds, done = [], [], [], 0
    wide = min(min(1024, grad.shape[-1]) for _, grad in pairs)
    for left, grad in pairs:
        depth = left.shape[1]
        count = grad.shape[0] if grad.ndim == 3 else grad.shape[1] // wide
        in_specs.append(pl.BlockSpec((rows, depth), lambda j: (at, 0)))

        def clip(j, done=done, count=count):
            return jnp.clip(j - done, 0, count - 1)

        if grad.ndim == 3:
            in_specs.append(pl.BlockSpec((1, depth, wide), lambda j, clip=clip: (clip(j), 0, 0)))
        else:
            in_specs.append(pl.BlockSpec((depth, wide), lambda j, clip=clip: (0, clip(j))))
        args += [left, grad]
        bounds.append((done, done + count))
        done += count
    spec = pl.BlockSpec((rows, wide), lambda j: (0, j))
    columns = done * wide
    if parts is None:
        out_specs, out_shape = spec, jax.ShapeDtypeStruct((rows, columns), BF16)
    else:
        in_specs.append(spec)
        args.append(extra)
        out_specs = [pl.BlockSpec((count, wide), lambda j: (0, j)) for _, count in parts]
        out_shape = [jax.ShapeDtypeStruct((count, columns), BF16) for _, count in parts]
    return pl.pallas_call(
        functools.partial(wide_kernel, bounds, parts),
        grid=(done,),
        in_specs=in_specs,
        out_specs=out_specs,
        out_shape=out_shape,
        cost_estimate=cost(),
        name="wide_rows_dot",
    )(*args)


def per_device(
    dp,
    fs,
    tokens,
    lengths,
    time_embed,
    cotangent,
    time_weight,
    attn_gain,
    attn_shift,
    qkv_weight,
    out_weight,
    mlp_gain,
    mlp_shift,
    up_weight,
    up_bias,
    down_weight,
    down_bias,
):
    net = Net(dp, fs)
    length, width = tokens.shape[1:]
    tokens, cotangent = tokens.reshape(length, width), cotangent.reshape(length, width)
    order = Order()
    wide_rows, tall_rows = qkv_weight.shape[0], down_weight.shape[0]
    te_rows = time_weight.shape[0]
    heads = width // HD
    half = width // 2
    with jax.named_scope("up_gather"):
        up_full = lax.all_gather(up_weight, "fsdp", axis=0, tiled=True)
    with jax.named_scope("small_gather"):
        small = SmallGather(
            net,
            time_weight,
            [attn_gain, attn_shift, mlp_gain, mlp_shift, down_bias, up_bias],
            time_embed,
        )
    order.note(small.packed)
    with jax.named_scope("attn_gather"):
        attn_net = Gather(net, jnp.concatenate([qkv_weight, out_weight], axis=1))
        attn_net.along(order(attn_net.own))
    down_net = Gather(net, down_weight)
    residual = tokens.astype(F32)
    normed_one, inverse_one = normalize(residual)
    ready = order(inverse_one, down_net.own)
    down_net.own = ready[1]
    with jax.named_scope("small_gather"):
        small.across(order)
    with jax.named_scope("attn_gather"):
        attn_net.join_line(order)
        order.note(attn_net.line)
        attn_net.across()
    with jax.named_scope("small_gather"):
        small.other(order)
    with jax.named_scope("down_gather"):
        down_net.along(order(down_net.own))
    with jax.named_scope("small_gather"):
        (
            time_scale,
            embeds,
            gain_one,
            shift_one,
            gain_two,
            shift_two,
            down_bias_full,
            up_bias_full,
        ) = small.finish(order, time_embed)

    place = relative_order(net, wide_rows, width)
    permute = (jnp.arange(width, dtype=jnp.int32)[:, None] == place[None, :]).astype(BF16)

    def turn(values_in):
        return back_dot(permute, values_in).astype(BF16)

    key_mask = jnp.arange(length, dtype=jnp.int32)[:, None] < lengths[None, :]
    affine_one = normed_one * gain_one + shift_one
    attn_in = (affine_one * time_scale).astype(BF16)
    cosine, sine = rotary_tables(length)
    order.note(attn_in, cosine, sine)
    turned_one = order.note(turn(order(attn_in)))
    with jax.named_scope("attn_gather"):
        attn_net.join_across(order)
        attn_net.corners()
    with jax.named_scope("down_gather"):
        down_net.join_line(order)
        order.note(down_net.line)
        down_net.across()
    with jax.named_scope("attn_gather"):
        plan, pieces = attn_net.finish(order)
    qkv, qkv_full, out_full = qkv_rotated(net, attn_in, plan, pieces, wide_rows, cosine, sine)
    order.note(qkv)
    pairs = heads // 2
    part = pairs // 2
    with jax.named_scope("down_gather"):
        down_net.join_across(order)
        down_net.corners()
    context = order.note(attend(lengths, order(qkv), 0, pairs))
    context = order(context)
    hidden = residual + jnp.dot(context, out_full, preferred_element_type=F32)
    normed_two, inverse_two = normalize(hidden)
    affine_two = normed_two * gain_two + shift_two
    mlp_in = (affine_two * time_scale).astype(BF16)
    order.note(mlp_in)
    active, slope = up_gelu(order(mlp_in), up_full, up_bias_full)
    order.note(active)

    grad_out = cotangent.astype(F32) * key_mask.astype(F32)
    grad_branch = grad_out.astype(BF16)
    with jax.named_scope("down_grad"):
        tall = order.note(tall_rows_dot(order(active), grad_branch))
        down_mine = lax.psum_scatter(tall, "fsdp", scatter_dimension=0, tiled=True)
    down_bias_grad = jnp.sum(grad_branch.astype(F32), axis=0, keepdims=True)
    with jax.named_scope("down_gather"):
        plan, pieces = down_net.finish(order)
    grad_pre, up_bias_grad, down_full = down_back(
        net, order(grad_branch), plan, pieces, tall_rows, slope
    )
    grad_pre = order(order.note(grad_pre))
    grad_mlp_in = back_dot(grad_pre, up_full)
    grad_affine_two = grad_mlp_in * time_scale
    grad_scale = jnp.sum(grad_mlp_in * affine_two, axis=0, keepdims=True)
    mlp_gain_grad = jnp.sum(grad_affine_two * normed_two, axis=0, keepdims=True)
    mlp_shift_grad = jnp.sum(grad_affine_two, axis=0, keepdims=True)
    grad_hidden = grad_out + norm_back(grad_affine_two * gain_two, normed_two, inverse_two)
    grad_attn = order.note(grad_hidden.astype(BF16))
    turned_ctx = order.note(turn(order(context)))
    turned_two = order.note(turn(order(mlp_in)))
    wide_half = wide_rows // 2
    wide_parts = kept_parts(net.yn, wide_half)
    up_red, low_red, high_red = Scatter(net, True), Scatter(net, False), Scatter(net, True)
    up_pairs = [(turned_two, grad_pre), (turned_ctx, grad_attn)]
    with jax.named_scope("up_grad"):
        order(grad_pre)
        up_red.core(order.note(wide_rows_dot(1, half, up_pairs)))
    grad_context = order.note(back_dot(order(grad_attn), out_full).astype(BF16))
    with jax.named_scope("up_grad"):
        sent = up_red.join_core(order)
        kept = wide_rows_dot(0, half, up_pairs, sent, wide_parts)
        order.note(kept[0])
        up_red.corners(*kept)
    low = attend_back(lengths, qkv, order(grad_context), cosine, sine, 0, part)
    order.note(low)
    with jax.named_scope("qkv_grad"):
        low_red.core(order.note(wide_rows_dot(1, half, [(turned_one, order(low))])))
    with jax.named_scope("up_grad"):
        up_red.across(order)
    high = attend_back(lengths, qkv, order(grad_context), cosine, sine, part, pairs - part)
    order.note(high)
    with jax.named_scope("qkv_grad"):
        sent = low_red.join_core(order)
        kept = wide_rows_dot(0, half, [(turned_one, low)], sent, wide_parts)
        order.note(kept[0])
        low_red.corners(*kept)
        high_red.core(order.note(wide_rows_dot(1, half, [(turned_one, order(high))])))
        sent = high_red.join_core(order)
        kept = wide_rows_dot(0, half, [(turned_one, high)], sent, wide_parts)
        order.note(kept[0])
        high_red.corners(*kept)
    with jax.named_scope("up_grad"):
        up_line = Line(net, wide_half, [up_red.group(order)])
        order.note(up_line.kept)
    with jax.named_scope("qkv_grad"):
        low_red.across(order)
    grad_qkv = jnp.concatenate([item for i in range(3) for item in (low[i], high[i])], axis=1)
    grad_attn_in = back_dot(order(grad_qkv), qkv_full)
    grad_affine_one = grad_attn_in * time_scale
    grad_scale = grad_scale + jnp.sum(grad_attn_in * affine_one, axis=0, keepdims=True)
    attn_gain_grad = jnp.sum(grad_affine_one * normed_one, axis=0, keepdims=True)
    attn_shift_grad = jnp.sum(grad_affine_one, axis=0, keepdims=True)
    token_grad = (
        grad_hidden + norm_back(grad_affine_one * gain_one, normed_one, inverse_one)
    ).astype(BF16)
    order.note(token_grad, grad_scale)
    with jax.named_scope("qkv_grad"):
        high_red.across(order)
    with jax.named_scope("small_sums"):
        sums = jnp.concatenate(
            [
                attn_gain_grad,
                attn_shift_grad,
                mlp_gain_grad,
                mlp_shift_grad,
                down_bias_grad,
                up_bias_grad.reshape(-1, width),
            ],
            axis=0,
        )
        count = sums.shape[0]
        spots = jnp.arange(fs, dtype=jnp.int32)[:, None] == net.me
        packed = jnp.concatenate([sums, jnp.where(spots, grad_scale, 0.0)], axis=0)
        moved = net.c(packed)
    with jax.named_scope("up_grad"):
        up_line.nearer(order)
    with jax.named_scope("small_sums"):
        packed = packed + order(moved)
        moved = [net.y(packed, s) for s in range(1, net.yn)]
    branch_out = jnp.dot(order(active), down_full, preferred_element_type=F32) + down_bias_full
    layer_out = (hidden + branch_out).astype(BF16)
    order.note(layer_out)
    with jax.named_scope("small_sums"):
        for item in moved:
            packed = packed + order(item)
        moved = net.z(packed, 1)
    with jax.named_scope("qkv_grad"):
        qkv_line = Line(net, wide_half, [low_red.group(order), high_red.group(order)])
    with jax.named_scope("small_sums"):
        packed = packed + order(moved)
        moved = net.z(packed, 2)
    with jax.named_scope("up_grad"):
        up_line.last(order)
    with jax.named_scope("qkv_grad"):
        qkv_line.nearer(order)
    with jax.named_scope("small_sums"):
        packed = packed + order(moved)
        mine = lax.dynamic_slice_in_dim(embeds, net.me * te_rows, te_rows, 1)
        time_part = lax.dot_general(
            mine,
            packed[count:],
            (((0,), (0,)), ((), ())),
            precision=lax.Precision.HIGHEST,
            preferred_element_type=F32,
        )
        each = attn_gain.shape[0]
        vector_part = lax.dynamic_slice_in_dim(packed[:5], net.me * each, each, 1)
        bias_part = lax.dynamic_slice_in_dim(
            packed[5:count].reshape(1, -1), net.me * up_bias.shape[0], up_bias.shape[0], 1
        )
        packed = jnp.concatenate(
            [
                time_part,
                jnp.pad(vector_part, ((0, 0), (0, width - each))),
                jnp.pad(bias_part, ((0, 0), (0, width - up_bias.shape[0]))),
            ],
            axis=0,
        )
        if dp > 2:
            packed = lax.psum(packed, "dp")
        else:
            packed = packed + net.x(packed)
        time_weight_grad = packed[:te_rows]
        vector_grads = [packed[te_rows + i, :each] for i in range(5)]
        up_bias_out = packed[te_rows + 5, : up_bias.shape[0]]
    with jax.named_scope("down_grad"):
        down_mine = order(down_mine)
        if dp > 2:
            down_weight_grad = lax.psum(down_mine, "dp").astype(F32)
        else:
            down_other = net.x(down_mine)
    with jax.named_scope("qkv_grad"):
        qkv_line.last(order)
        whole = qkv_line.finish(order)
    with jax.named_scope("up_grad"):
        both = up_line.finish(order)
        ups = grad_pre.shape[1]
        up_weight_grad, out_weight_grad = both[:, :ups], both[:, ups:]
    if dp == 2:
        down_weight_grad = down_mine.astype(F32) + down_other.astype(F32)
    wide_low, wide_high = low.shape[2], high.shape[2]
    low_part, high_part = whole[:, : 3 * wide_low], whole[:, 3 * wide_low :]
    qkv_weight_grad = jnp.concatenate(
        [
            item
            for i in range(3)
            for item in (
                low_part[:, i * wide_low : (i + 1) * wide_low],
                high_part[:, i * wide_high : (i + 1) * wide_high],
            )
        ],
        axis=1,
    )
    return (
        layer_out[None],
        token_grad[None],
        time_weight_grad,
        vector_grads[0],
        vector_grads[1],
        qkv_weight_grad,
        out_weight_grad,
        vector_grads[2],
        vector_grads[3],
        up_weight_grad,
        up_bias_out,
        down_weight_grad,
        vector_grads[4],
    )


def solution(mesh):
    return jax.shard_map(
        functools.partial(per_device, mesh.shape["dp"], mesh.shape["fsdp"]),
        mesh=mesh,
        in_specs=(
            P(("dp", "fsdp"), None, None),
            P(("dp", "fsdp")),
            P(("dp", "fsdp"), None),
            P(("dp", "fsdp"), None, None),
            P("fsdp", None),
            P("fsdp"),
            P("fsdp"),
            P("fsdp", None),
            P("fsdp", None),
            P("fsdp"),
            P("fsdp"),
            P("fsdp", None),
            P("fsdp"),
            P("fsdp", None),
            P("fsdp"),
        ),
        out_specs=(
            P(("dp", "fsdp"), None, None),
            P(("dp", "fsdp"), None, None),
            P("fsdp", None),
            P("fsdp"),
            P("fsdp"),
            P("fsdp", None),
            P("fsdp", None),
            P("fsdp"),
            P("fsdp"),
            P("fsdp", None),
            P("fsdp"),
            P("fsdp", None),
            P("fsdp"),
        ),
        check_vma=False,
    )
```

```python
import functools
import math

import jax
import jax.numpy as jnp
from jax import lax
from jax.experimental import pallas as pl
from jax.experimental.pallas import tpu as pltpu
from jax.sharding import PartitionSpec as P

HD = 64
ZN = 4
PAIR = 128
LOG2E = math.log2(math.e)
ROOT = math.sqrt(2.0 / math.pi)
F32 = jnp.float32
BF16 = jnp.bfloat16


def normalize(values_in):
    center = values_in - jnp.mean(values_in, axis=-1, keepdims=True)
    inverse = lax.rsqrt(jnp.mean(center * center, axis=-1, keepdims=True) + 1e-05)
    return (center * inverse, inverse)


def norm_back(grad_hat, normed, inverse):
    return inverse * (
        grad_hat
        - jnp.mean(grad_hat, axis=-1, keepdims=True)
        - normed * jnp.mean(grad_hat * normed, axis=-1, keepdims=True)
    )


def rows_dot(left, right):
    return lax.dot_general(
        left, right, (((0,), (0,)), ((), ())), preferred_element_type=F32
    )


def back_dot(grad_in, weight):
    return lax.dot_general(
        grad_in, weight, (((1,), (1,)), ((), ())), preferred_element_type=F32
    )


def rotary_tables(length):
    half_size = HD // 2
    frequency = jnp.exp(
        jnp.arange(half_size, dtype=F32) * (-2.0 * math.log(10000.0) / HD)
    )
    angles = jnp.arange(length, dtype=F32)[:, None] * frequency[None, :]
    angles = jnp.concatenate([angles] * (PAIR // half_size), axis=-1)
    return (jnp.cos(angles), jnp.sin(angles))


class Order:
    def __init__(self):
        self.mark = ()

    def __call__(self, *arrays):
        out = lax.optimization_barrier((*arrays, *self.mark))[: len(arrays)]
        self.mark = (out[0],)
        return out[0] if len(out) == 1 else out

    def note(self, *arrays):
        self.mark = arrays
        return arrays[0] if len(arrays) == 1 else arrays


def scoped(name):
    def wrap(function):
        @functools.wraps(function)
        def inner(*args, **kwargs):
            with jax.named_scope(name):
                return function(*args, **kwargs)

        return inner

    return wrap


class Net:
    def __init__(self, dp, fs):
        self.dp, self.fs = dp, fs
        self.yn = fs // (2 * ZN)
        index = lax.axis_index("fsdp")
        self.me = index
        self.z0 = index // (2 * self.yn)
        self.y0 = (index // 2) % self.yn
        self.c0 = index % 2
        self.p0 = lax.axis_index("dp") % 2

    def perm(self, values_in, zx, dy, dc):
        pairs = []
        for i in range(self.fs):
            z, y, c = i // (2 * self.yn), (i // 2) % self.yn, i % 2
            to = ((z ^ zx) * self.yn + (y + dy) % self.yn) * 2 + (c ^ dc)
            pairs.append((i, to))
        return lax.ppermute(values_in, "fsdp", pairs)

    @scoped("z_hop")
    def z(self, values_in, k):
        return self.perm(values_in, k, 0, 0)

    @scoped("y_hop")
    def y(self, values_in, s):
        return self.perm(values_in, 0, s, 0)

    @scoped("core_hop")
    def c(self, values_in):
        return self.perm(values_in, 0, 0, 1)

    @scoped("x_hop")
    def x(self, values_in):
        return lax.ppermute(values_in, "dp", [(i, i ^ 1) for i in range(self.dp)])


def stack_kernel(*refs):
    at = 0
    for item in refs[:-1]:
        rows = item.shape[0]
        refs[-1][at : at + rows, :] = item[...]
        at += rows


def stack_rows(*items):
    rows = sum(item.shape[0] for item in items)
    return pl.pallas_call(
        stack_kernel,
        out_shape=jax.ShapeDtypeStruct((rows, items[0].shape[1]), items[0].dtype),
        cost_estimate=cost(),
        name="stack_rows",
    )(*items)


class Gather:
    def __init__(self, net, shard):
        self.net = net
        self.rows, self.columns = shard.shape
        self.half = self.rows // 2
        self.own = lax.dynamic_slice_in_dim(shard, net.p0 * self.half, self.half, 0)

    def along(self, own):
        self.own = own
        self.parts = [self.net.z(own, k) for k in range(1, ZN)]

    def join_line(self, order):
        self.line = stack_rows(*order(self.own, *self.parts))

    def across(self):
        net = self.net
        self.over = net.x(self.line)
        self.beside = [net.y(self.line, s) for s in range(1, net.yn)]

    def join_across(self, order):
        self.over, *self.beside = order(self.over, *self.beside)

    def corners(self):
        net = self.net
        mid = (ZN // 2) * self.half
        self.corner_one = [net.x(item[:mid]) for item in self.beside]
        self.corner_two = [net.y(self.over[mid:], s) for s in range(1, net.yn)]
        self.pieces = [self.line, self.over] + self.beside
        self.plan = [(0, 0, 0, ZN), (0, 1, 0, ZN)]
        self.plan += [(s, 0, 0, ZN) for s in range(1, net.yn)]
        self.moved = [net.c(item) for item in self.pieces]

    def finish(self, order):
        net = self.net
        late = order(*self.corner_one, *self.corner_two)
        plan = [(s, 1, 0, ZN // 2) for s in range(1, net.yn)]
        plan += [(s, 1, ZN // 2, ZN - ZN // 2) for s in range(1, net.yn)]
        pieces = self.pieces + list(late) + self.moved + [net.c(item) for item in late]
        plan = self.plan + plan
        full = [(s, q, side, first, count) for side in range(2) for s, q, first, count in plan]
        return full, pieces


def piece_spots(plan, where_ref, rows, half, yn):
    z0, y0, c0, p0 = where_ref[0], where_ref[1], where_ref[2], where_ref[3]
    spots = []
    for i, (s, q, side, first, count) in enumerate(plan):
        y = lax.rem(y0 + yn - s, yn)
        p = lax.rem(p0 + q, 2)
        c = lax.rem(c0 + side, 2)
        for k in range(count):
            z = lax.bitwise_xor(z0, jnp.int32(first + k))
            start = pl.multiple_of(((z * yn + y) * 2 + c) * rows + p * half, half)
            spots.append((i, k * half, first + k, start))
    return spots


def pack_kernel(*refs):
    time_ref, vectors, out_ref = refs[0], refs[1:-1], refs[-1]
    out_ref[...] = jnp.zeros_like(out_ref)
    rows = time_ref.shape[0]
    out_ref[:rows, :] = time_ref[...]
    for i, item in enumerate(vectors):
        out_ref[rows + i : rows + i + 1, : item.shape[1]] = item[...]


def small_kernel(rows, te_rows, sizes, yn, where_ref, embed_ref, own_ref, other_ref, *refs):
    scale_ref, all_ref, outs, held, sems = refs[0], refs[1], refs[2:-2], refs[-2], refs[-1]
    z0, y0, c0 = where_ref[0], where_ref[1], where_ref[2]
    copies = []
    for side, piece_ref in enumerate((own_ref, other_ref)):
        c = lax.rem(c0 + side, 2)
        for s in range(yn):
            y = lax.rem(y0 + yn - s, yn)
            for k in range(ZN):
                z = lax.bitwise_xor(z0, jnp.int32(k))
                copies.append(
                    pltpu.make_async_copy(
                        piece_ref.at[s * ZN + k],
                        held.at[(z * yn + y) * 2 + c],
                        sems.at[len(copies)],
                    )
                )
    for copy in copies:
        copy.start()
    for copy in copies:
        copy.wait()
    fs = held.shape[0]
    scale = jnp.ones_like(scale_ref)
    whole = jnp.concatenate([held[f, :te_rows, :] for f in range(fs)], axis=0)
    scale_ref[...] = scale + jnp.dot(embed_ref[...], whole, preferred_element_type=F32)
    for i, (size, out_ref) in enumerate(zip(sizes, outs)):
        pieces = [
            held[f, te_rows + i : te_rows + i + 1, :size].astype(F32) for f in range(fs)
        ]
        out_ref[...] = jnp.concatenate(pieces, axis=1)
    last, wide = te_rows + len(sizes), embed_ref.shape[1]
    all_ref[...] = jnp.concatenate(
        [held[f, last : last + 1, :wide].astype(F32) for f in range(fs)], axis=0
    )


class SmallGather:
    def __init__(self, net, time_weight, vectors, embed):
        self.net, self.sizes = net, [item.shape[0] for item in vectors]
        self.te_rows, self.width = time_weight.shape
        self.rows = self.te_rows + len(vectors) + 1
        self.rows += -self.rows % 16
        self.packed = pl.pallas_call(
            pack_kernel,
            out_shape=jax.ShapeDtypeStruct((self.rows, self.width), BF16),
            cost_estimate=cost(),
            name="pack_small",
        )(time_weight, *[item.reshape(1, -1) for item in vectors], embed)
        self.parts = [net.z(self.packed, k) for k in range(1, ZN)]

    def across(self, order):
        net = self.net
        self.line = jnp.stack(order(self.packed, *self.parts))
        self.beside = [net.y(self.line, s) for s in range(1, net.yn)]

    def other(self, order):
        self.line, *self.beside = order(self.line, *self.beside)
        self.sides = jnp.concatenate([self.line] + self.beside, axis=0)
        self.moved = self.net.c(self.sides)

    def finish(self, order, embed):
        net, fs = self.net, self.net.fs
        moved = order(self.moved)
        where = jnp.stack([net.z0, net.y0, net.c0]).astype(jnp.int32)
        shapes = [(1, self.width), (fs, embed.shape[1])]
        shapes += [(1, size * fs) for size in self.sizes]
        outs = pl.pallas_call(
            functools.partial(small_kernel, self.rows, self.te_rows, self.sizes, net.yn),
            out_shape=[jax.ShapeDtypeStruct(shape, F32) for shape in shapes],
            grid_spec=pltpu.PrefetchScalarGridSpec(
                num_scalar_prefetch=1,
                grid=(1,),
                in_specs=[pl.BlockSpec(embed.shape, lambda i, r: (0, 0))]
                + [pl.BlockSpec(memory_space=pl.ANY)] * 2,
                out_specs=[whole_spec(shape) for shape in shapes],
                scratch_shapes=[
                    pltpu.VMEM((fs, self.rows, self.width), BF16),
                    pltpu.SemaphoreType.DMA((fs,)),
                ],
            ),
            cost_estimate=cost(),
            name="small_join",
        )(where, embed, self.sides, moved)
        order.note(outs[0])
        return outs


def relative_order(net, rows, total):
    half = rows // 2
    d = jnp.arange(total, dtype=jnp.int32)
    f, i = d // rows, d % rows
    z, y, c = f // (2 * net.yn), (f // 2) % net.yn, f % 2
    p, j = i // half, i % half
    c, y, p, z = c ^ net.c0, (y - net.y0) % net.yn, p ^ net.p0, z ^ net.z0
    return (((c * net.yn + y) * 2 + p) * ZN + z) * half + j


def add_low(*items):
    total = items[0].astype(F32)
    for item in items[1:]:
        total = total + item.astype(F32)
    return total.astype(BF16)


def sum_kernel(counts, keep, *refs):
    total = sum(counts)
    kept_ref, sent_ref = refs[total], refs[total + 1]
    at, column = 0, 0
    for count in counts:
        items = refs[at : at + count]
        at += count
        wide = items[0].shape[1]
        value = items[0][...].astype(F32)
        for item in items[1:]:
            value = value + item[...].astype(F32)
        kept_ref[:, column : column + wide] = value[:keep, :]
        sent_ref[:, column : column + wide] = value[keep:, :].astype(BF16)
        column += wide


def sum_split(groups, keep):
    rows = groups[0][0].shape[0]
    columns = sum(group[0].shape[1] for group in groups)
    return pl.pallas_call(
        functools.partial(sum_kernel, [len(group) for group in groups], keep),
        out_shape=[
            jax.ShapeDtypeStruct((keep, columns), F32),
            jax.ShapeDtypeStruct((rows - keep, columns), BF16),
        ],
        cost_estimate=cost(),
        name="sum_split",
    )(*[item for group in groups for item in group])


class Scatter:
    def __init__(self, net, by_x):
        self.net, self.by_x = net, by_x

    def core(self, send):
        self.sent = self.net.c(send)

    def join_core(self, order):
        self.sent = order(self.sent)
        return self.sent

    def corners(self, own, over, *rest):
        net = self.net
        self.own, self.over, self.side = own, over, list(rest[0::2])
        if self.by_x:
            self.came = [net.x(item) for item in rest[1::2]]
        else:
            self.came = [net.y(item, s + 1) for s, item in enumerate(rest[1::2])]

    def across(self, order):
        net = self.net
        came = order(*self.came) if len(self.came) > 1 else [order(*self.came)]
        if self.by_x:
            self.side = [add_low(a, b) for a, b in zip(self.side, came)]
        else:
            self.over = add_low(self.over, *came)
        self.over = net.x(self.over)
        self.side = [net.y(item, s + 1) for s, item in enumerate(self.side)]

    def group(self, order):
        return [self.own, *order(self.over, *self.side)]


class Line:
    def __init__(self, net, half, groups):
        self.net, self.half = net, half
        self.kept, far = sum_split(groups, (ZN // 2) * half)
        self.far = net.z(far, 2)

    def nearer(self, order):
        self.here, near = sum_split([[self.kept, order(self.far)]], self.half)
        self.near = self.net.z(near, 1)

    def last(self, order):
        net = self.net
        mine = add_low(self.here, order(self.near))
        if net.dp > 2:
            groups = [list(range(q, net.dp, 2)) for q in range(2)]
            mine = lax.psum(mine, "dp", axis_index_groups=groups)
        self.mine, self.other = mine, net.x(mine)

    def finish(self, order):
        mine, other = self.mine, order(self.other)
        first = jnp.where(self.net.p0 == 0, mine, other)
        second = jnp.where(self.net.p0 == 0, other, mine)
        return jnp.concatenate([first, second], axis=0).astype(F32)


def kept_parts(yn, half):
    line = ZN * half
    return [(i * line, line) for i in range(2 * yn)]


def cost():
    return pl.CostEstimate(flops=1000, bytes_accessed=1000, transcendentals=0)


def weight_copies(plan, where_ref, rows, half, yn, pieces, targets, sems):
    spots = piece_spots(plan, where_ref, rows, half, yn)
    groups, count, column = [], 0, 0
    for target, first, wide in targets:
        group = []
        for i, row, shift, start in spots:
            group.append(
                pltpu.make_async_copy(
                    pieces[i].at[pl.ds(row, half), pl.ds(column, wide)],
                    target.at[pl.ds(start, half), pl.ds(first, wide)],
                    sems.at[count],
                )
            )
            count += 1
        column += wide
        groups.append(group)
    for group in groups:
        for copy in group:
            copy.start()
    return groups


def finish_copies(copies):
    for copy in copies:
        copy.wait()


def back_copy(held, out, first, wide, sem):
    spot = pl.ds(first, wide)
    copy = pltpu.make_async_copy(held.at[:, spot], out.at[:, spot], sem)
    copy.start()
    return copy


def qkv_kernel(plan, rows, half, yn, where_ref, x_ref, cos_ref, sin_ref, *refs):
    pieces = refs[: len(plan)]
    out_ref, wq_ref, wo_ref, wq, wo, low, sems, back_sems = refs[len(plan) :]
    wide = wo.shape[1]
    targets = [(wq, part * wide, wide) for part in range(3)] + [(wo, 0, wide)]
    groups = weight_copies(plan, where_ref, rows, half, yn, pieces, targets, sems)
    cosine, sine = cos_ref[...], sin_ref[...]
    front = lax.broadcasted_iota(jnp.int32, cosine.shape, 1) % HD < HD // 2
    backs = []
    for part in range(3):
        finish_copies(groups[part])
        backs.append(back_copy(wq, wq_ref, part * wide, wide, back_sems.at[part]))
        for j in range(wide // (2 * PAIR)):
            first = part * wide + j * 2 * PAIR
            acc = jnp.dot(
                x_ref[...], wq[:, first : first + 2 * PAIR], preferred_element_type=F32
            )
            for i in range(2):
                piece = acc[:, i * PAIR : (i + 1) * PAIR]
                if part < 2:
                    turned = jnp.where(
                        front,
                        -pltpu.roll(piece, PAIR - HD // 2, 1),
                        pltpu.roll(piece, HD // 2, 1),
                    )
                    piece = piece * cosine + turned * sine
                low[:, first + i * PAIR : first + (i + 1) * PAIR] = piece.astype(BF16)
        backs.append(back_copy(low, out_ref, part * wide, wide, back_sems.at[4 + part]))
    finish_copies(groups[3])
    backs.append(back_copy(wo, wo_ref, 0, wide, back_sems.at[3]))
    finish_copies(backs)


def where_of(net):
    return jnp.stack([net.z0, net.y0, net.c0, net.p0]).astype(jnp.int32)


ANY = pl.BlockSpec(memory_space=pl.ANY)


def whole_spec(shape):
    return pl.BlockSpec(shape, lambda i, r: (0, 0))


def qkv_rotated(net, x, plan, pieces, rows, cosine, sine):
    tokens, depth = x.shape
    total = net.fs * rows
    blocks = sum(entry[4] for entry in plan)
    half = rows // 2
    return pl.pallas_call(
        functools.partial(qkv_kernel, plan, rows, half, net.yn),
        grid_spec=pltpu.PrefetchScalarGridSpec(
            num_scalar_prefetch=1,
            grid=(1,),
            in_specs=[whole_spec(x.shape), whole_spec(cosine.shape), whole_spec(sine.shape)]
            + [ANY] * len(pieces),
            out_specs=[ANY] * 3,
            scratch_shapes=[
                pltpu.VMEM((total, 3 * depth), BF16),
                pltpu.VMEM((total, depth), BF16),
                pltpu.VMEM((tokens, 3 * depth), BF16),
                pltpu.SemaphoreType.DMA((4 * blocks,)),
                pltpu.SemaphoreType.DMA((7,)),
            ],
        ),
        out_shape=[
            jax.ShapeDtypeStruct((tokens, 3 * depth), BF16),
            jax.ShapeDtypeStruct((total, 3 * depth), BF16),
            jax.ShapeDtypeStruct((total, depth), BF16),
        ],
        compiler_params=pltpu.CompilerParams(vmem_limit_bytes=32 * 2**20),
        cost_estimate=cost(),
        name="qkv_rotated",
    )(where_of(net), x, cosine, sine, *pieces)


def up_kernel(plan, rows, half, yn, where_ref, x_ref, b_ref, *refs):
    pieces = refs[: len(plan)]
    act_out, slope_out, w_out, w, act, slope, sems, back_sems = refs[len(plan) :]
    total = w.shape[1]
    wide = min(1024, total)
    step = min(256, wide)
    parts = total // wide
    targets = [(w, part * wide, wide) for part in range(parts)]
    groups = weight_copies(plan, where_ref, rows, half, yn, pieces, targets, sems)
    backs = []
    for part in range(parts):
        finish_copies(groups[part])
        backs.append(back_copy(w, w_out, part * wide, wide, back_sems.at[3 * part]))
        for first in range(part * wide, (part + 1) * wide, step):
            spot = slice(first, first + step)
            v = jnp.dot(x_ref[...], w[:, spot], preferred_element_type=F32) + b_ref[:, spot]
            square = v * v
            bend = jnp.tanh(v * (ROOT + ROOT * 0.044715 * square))
            half_up = 0.5 + 0.5 * bend
            act[:, spot] = (v * half_up).astype(BF16)
            rise = 0.5 * ROOT + (1.5 * 0.044715 * ROOT) * square
            slope[:, spot] = (half_up + v * (1.0 - bend * bend) * rise).astype(BF16)
        backs.append(back_copy(act, act_out, part * wide, wide, back_sems.at[3 * part + 1]))
        backs.append(back_copy(slope, slope_out, part * wide, wide, back_sems.at[3 * part + 2]))
    finish_copies(backs)


def up_gelu(net, x, plan, pieces, rows, bias):
    tokens, depth = x.shape
    total = bias.shape[1]
    parts = total // min(1024, total)
    blocks = sum(entry[4] for entry in plan)
    return pl.pallas_call(
        functools.partial(up_kernel, plan, rows, rows // 2, net.yn),
        grid_spec=pltpu.PrefetchScalarGridSpec(
            num_scalar_prefetch=1,
            grid=(1,),
            in_specs=[whole_spec(x.shape), whole_spec(bias.shape)] + [ANY] * len(pieces),
            out_specs=[ANY] * 3,
            scratch_shapes=[
                pltpu.VMEM((depth, total), BF16),
                pltpu.VMEM((tokens, total), BF16),
                pltpu.VMEM((tokens, total), BF16),
                pltpu.SemaphoreType.DMA((parts * blocks,)),
                pltpu.SemaphoreType.DMA((3 * parts,)),
            ],
        ),
        out_shape=[
            jax.ShapeDtypeStruct((tokens, total), BF16),
            jax.ShapeDtypeStruct((tokens, total), BF16),
            jax.ShapeDtypeStruct((depth, total), BF16),
        ],
        compiler_params=pltpu.CompilerParams(vmem_limit_bytes=40 * 2**20),
        cost_estimate=cost(),
        name="up_gelu",
    )(where_of(net), x, bias, *pieces)


def down_kernel(plan, rows, half, yn, where_ref, g_ref, slope_ref, *refs):
    pieces = refs[: len(plan)]
    out_ref, sum_ref, w_ref, w, slope, low, sems, slope_sems, back_sems = refs[len(plan) :]
    spots = piece_spots(plan, where_ref, rows, half, yn)
    group_rows = w.shape[0] // ZN
    step = min(256, group_rows)
    z0 = where_ref[0]
    groups = [[] for _ in range(ZN)]
    for count, (i, row, shift, start) in enumerate(spots):
        copy = pltpu.make_async_copy(
            pieces[i].at[pl.ds(row, half), :], w.at[pl.ds(start, half), :], sems.at[count]
        )
        groups[shift].append(copy)
    slopes = []
    for k in range(ZN):
        at = pl.multiple_of(lax.bitwise_xor(z0, jnp.int32(k)) * group_rows, group_rows)
        for copy in groups[k]:
            copy.start()
        copy = pltpu.make_async_copy(
            slope_ref.at[:, pl.ds(at, group_rows)], slope.at[k], slope_sems.at[k]
        )
        copy.start()
        slopes.append(copy)
    backs = []
    for k in range(ZN):
        at = pl.multiple_of(lax.bitwise_xor(z0, jnp.int32(k)) * group_rows, group_rows)
        finish_copies(groups[k])
        slopes[k].wait()
        here = pl.ds(at, group_rows)
        copy = pltpu.make_async_copy(w.at[here, :], w_ref.at[here, :], back_sems.at[2 * k])
        copy.start()
        backs.append(copy)
        for j in range(group_rows // step):
            spot = slice(j * step, (j + 1) * step)
            inner = pl.multiple_of(at + j * step, step)
            acc = lax.dot_general(
                g_ref[...],
                w[pl.ds(inner, step), :],
                (((1,), (1,)), ((), ())),
                preferred_element_type=F32,
            )
            rounded = (acc * slope[k, :, spot].astype(F32)).astype(BF16)
            low[k, :, spot] = rounded
            sum_ref[:, pl.ds(inner, step)] = jnp.sum(
                rounded.astype(F32), axis=0, keepdims=True
            )
        copy = pltpu.make_async_copy(low.at[k], out_ref.at[:, here], back_sems.at[2 * k + 1])
        copy.start()
        backs.append(copy)
    finish_copies(backs)


def down_back(net, grad, plan, pieces, rows, slope):
    tokens, depth = grad.shape
    total = slope.shape[1]
    blocks = sum(entry[4] for entry in plan)
    return pl.pallas_call(
        functools.partial(down_kernel, plan, rows, rows // 2, net.yn),
        grid_spec=pltpu.PrefetchScalarGridSpec(
            num_scalar_prefetch=1,
            grid=(1,),
            in_specs=[whole_spec(grad.shape), ANY] + [ANY] * len(pieces),
            out_specs=[ANY, pl.BlockSpec((1, total), lambda i, r: (0, 0)), ANY],
            scratch_shapes=[
                pltpu.VMEM((total, depth), BF16),
                pltpu.VMEM((ZN, tokens, total // ZN), BF16),
                pltpu.VMEM((ZN, tokens, total // ZN), BF16),
                pltpu.SemaphoreType.DMA((blocks,)),
                pltpu.SemaphoreType.DMA((ZN,)),
                pltpu.SemaphoreType.DMA((2 * ZN,)),
            ],
        ),
        out_shape=[
            jax.ShapeDtypeStruct((tokens, total), BF16),
            jax.ShapeDtypeStruct((1, total), F32),
            jax.ShapeDtypeStruct((total, depth), BF16),
        ],
        compiler_params=pltpu.CompilerParams(vmem_limit_bytes=40 * 2**20),
        cost_estimate=cost(),
        name="down_back",
    )(where_of(net), grad, slope, *pieces)


def attend_kernel(len_ref, q_ref, k_ref, v_ref, out_ref):
    q, k, v = q_ref[...], k_ref[...], v_ref[...]
    length = k.shape[0]
    first = lax.broadcasted_iota(jnp.int32, q.shape, 1) < HD
    valid = lax.broadcasted_iota(jnp.int32, (1, length), 1) < len_ref[0]
    zero = jnp.zeros_like(q)
    outs = []
    for h in range(2):
        one = jnp.where(first, q, zero) if h == 0 else jnp.where(first, zero, q)
        scores = lax.dot_general(
            one, k, (((1,), (1,)), ((), ())), preferred_element_type=F32
        )
        scores = jnp.where(valid, scores * HD**-0.5, -1000000000.0)
        top = jnp.max(scores, axis=1, keepdims=True)
        exponent = jnp.exp2((scores - top) * LOG2E)
        total = jnp.sum(exponent, axis=1, keepdims=True)
        mixed = jnp.dot(exponent.astype(BF16), v, preferred_element_type=F32)
        outs.append(mixed * (1.0 / total))
    out_ref[...] = jnp.where(first, outs[0], outs[1]).astype(BF16)


def attend(length, qkv, first_pair, pairs):
    rows, total = qkv.shape
    count = total // 3 // PAIR

    def pick(part):
        return pl.BlockSpec((rows, PAIR), lambda j, r: (0, part * count + first_pair + j))

    return pl.pallas_call(
        attend_kernel,
        grid_spec=pltpu.PrefetchScalarGridSpec(
            num_scalar_prefetch=1,
            grid=(pairs,),
            in_specs=[pick(0), pick(1), pick(2)],
            out_specs=pl.BlockSpec((rows, PAIR), lambda j, r: (0, j)),
        ),
        out_shape=jax.ShapeDtypeStruct((rows, pairs * PAIR), BF16),
        cost_estimate=cost(),
        name="attend",
    )(length, qkv, qkv, qkv)


def attend_back_kernel(len_ref, q_ref, k_ref, v_ref, g_ref, cos_ref, sin_ref, out_ref):
    q, k, v, g = q_ref[...], k_ref[...], v_ref[...], g_ref[...]
    length = k.shape[0]
    lane = lax.broadcasted_iota(jnp.int32, q.shape, 1)
    first = lane < HD
    valid = lax.broadcasted_iota(jnp.int32, (length, length), 0) < len_ref[0]
    zero = jnp.zeros_like(q)
    grads = []
    for h in range(2):
        key = jnp.where(first, k, zero) if h == 0 else jnp.where(first, zero, k)
        value = jnp.where(first, v, zero) if h == 0 else jnp.where(first, zero, v)
        scores = lax.dot_general(
            key, q, (((1,), (1,)), ((), ())), preferred_element_type=F32
        )
        scores = jnp.where(valid, scores * HD**-0.5, -1000000000.0)
        top = jnp.max(scores, axis=0, keepdims=True)
        exponent = jnp.exp2((scores - top) * LOG2E)
        total = jnp.sum(exponent, axis=0, keepdims=True)
        probs = exponent * (1.0 / total)
        grad_probs = lax.dot_general(
            value, g, (((1,), (1,)), ((), ())), preferred_element_type=F32
        )
        delta = jnp.sum(grad_probs * probs, axis=0, keepdims=True)
        grad_scores = (probs * (grad_probs - delta)).astype(BF16)
        grads.append(
            (
                lax.dot_general(
                    grad_scores, k, (((0,), (0,)), ((), ())), preferred_element_type=F32
                ),
                jnp.dot(grad_scores, q, preferred_element_type=F32),
                jnp.dot(probs.astype(BF16), g, preferred_element_type=F32),
            )
        )
    front = lane % HD < HD // 2
    cosine, sine = cos_ref[...] * HD**-0.5, sin_ref[...] * HD**-0.5
    for i in range(2):
        grad = jnp.where(first, grads[0][i], grads[1][i])
        sined = grad * sine
        turned = jnp.where(
            front, pltpu.roll(sined, PAIR - HD // 2, 1), -pltpu.roll(sined, HD // 2, 1)
        )
        out_ref[i] = (grad * cosine + turned).astype(BF16)
    out_ref[2] = jnp.where(first, grads[0][2], grads[1][2]).astype(BF16)


def attend_back(length, qkv, grad, cosine, sine, first_pair, pairs):
    rows, total = qkv.shape
    count = total // 3 // PAIR

    def pick(part):
        return pl.BlockSpec((rows, PAIR), lambda j, r: (0, part * count + first_pair + j))

    table = pl.BlockSpec((rows, PAIR), lambda j, r: (0, 0))
    return pl.pallas_call(
        attend_back_kernel,
        grid_spec=pltpu.PrefetchScalarGridSpec(
            num_scalar_prefetch=1,
            grid=(pairs,),
            in_specs=[pick(0), pick(1), pick(2), pick(0), table, table],
            out_specs=pl.BlockSpec((3, rows, PAIR), lambda j, r: (0, 0, j)),
        ),
        out_shape=jax.ShapeDtypeStruct((3, rows, pairs * PAIR), BF16),
        cost_estimate=cost(),
        name="attend_back",
    )(length, qkv, qkv, qkv, grad, cosine, sine)


def tall_kernel(left_ref, grad_ref, out_ref):
    out_ref[...] = lax.dot_general(
        left_ref[...], grad_ref[...], (((0,), (0,)), ((), ())), preferred_element_type=F32
    ).astype(BF16)


def tall_rows_dot(left, grad):
    depth, columns = grad.shape
    total = left.shape[1]
    tall = min(1024, total)
    return pl.pallas_call(
        tall_kernel,
        grid=(total // tall,),
        in_specs=[
            pl.BlockSpec((depth, tall), lambda i: (0, i)),
            pl.BlockSpec((depth, columns), lambda i: (0, 0)),
        ],
        out_specs=pl.BlockSpec((tall, columns), lambda i: (i, 0)),
        out_shape=jax.ShapeDtypeStruct((total, columns), BF16),
        cost_estimate=cost(),
        name="tall_rows_dot",
    )(left, grad)


def wide_kernel(bounds, parts, *refs):
    step = pl.program_id(0)
    operands, rest = refs[: 2 * len(bounds)], refs[2 * len(bounds) :]

    def write(left_ref, grad_ref):
        grad = grad_ref[0] if len(grad_ref.shape) == 3 else grad_ref[...]
        acc = jnp.dot(left_ref[...], grad, preferred_element_type=F32)
        if parts is None:
            rest[-1][...] = acc.astype(BF16)
            return
        acc = acc + rest[0][...].astype(F32)
        for (first, rows), out_ref in zip(parts, rest[1:]):
            out_ref[...] = acc[first : first + rows, :].astype(BF16)

    for i, (low, high) in enumerate(bounds):

        @pl.when((step >= low) & (step < high))
        def _(i=i):
            write(operands[2 * i], operands[2 * i + 1])


def wide_rows_dot(at, rows, pairs, extra=None, parts=None):
    in_specs, args, bounds, done = [], [], [], 0
    wide = min(min(1024, grad.shape[-1]) for _, grad in pairs)
    for left, grad in pairs:
        depth = left.shape[1]
        count = grad.shape[0] if grad.ndim == 3 else grad.shape[1] // wide
        in_specs.append(pl.BlockSpec((rows, depth), lambda j: (at, 0)))

        def clip(j, done=done, count=count):
            return jnp.clip(j - done, 0, count - 1)

        if grad.ndim == 3:
            in_specs.append(pl.BlockSpec((1, depth, wide), lambda j, clip=clip: (clip(j), 0, 0)))
        else:
            in_specs.append(pl.BlockSpec((depth, wide), lambda j, clip=clip: (0, clip(j))))
        args += [left, grad]
        bounds.append((done, done + count))
        done += count
    spec = pl.BlockSpec((rows, wide), lambda j: (0, j))
    columns = done * wide
    if parts is None:
        out_specs, out_shape = spec, jax.ShapeDtypeStruct((rows, columns), BF16)
    else:
        in_specs.append(spec)
        args.append(extra)
        out_specs = [pl.BlockSpec((count, wide), lambda j: (0, j)) for _, count in parts]
        out_shape = [jax.ShapeDtypeStruct((count, columns), BF16) for _, count in parts]
    return pl.pallas_call(
        functools.partial(wide_kernel, bounds, parts),
        grid=(done,),
        in_specs=in_specs,
        out_specs=out_specs,
        out_shape=out_shape,
        cost_estimate=cost(),
        name="wide_rows_dot",
    )(*args)


def per_device(
    dp,
    fs,
    tokens,
    lengths,
    time_embed,
    cotangent,
    time_weight,
    attn_gain,
    attn_shift,
    qkv_weight,
    out_weight,
    mlp_gain,
    mlp_shift,
    up_weight,
    up_bias,
    down_weight,
    down_bias,
):
    net = Net(dp, fs)
    length, width = tokens.shape[1:]
    tokens, cotangent = tokens.reshape(length, width), cotangent.reshape(length, width)
    order = Order()
    wide_rows, tall_rows = qkv_weight.shape[0], down_weight.shape[0]
    te_rows = time_weight.shape[0]
    heads = width // HD
    half = width // 2
    with jax.named_scope("small_gather"):
        small = SmallGather(
            net,
            time_weight,
            [attn_gain, attn_shift, mlp_gain, mlp_shift, down_bias, up_bias],
            time_embed,
        )
    order.note(small.packed)
    with jax.named_scope("attn_gather"):
        attn_net = Gather(net, jnp.concatenate([qkv_weight, out_weight], axis=1))
        attn_net.along(order(attn_net.own))
    up_net = Gather(net, up_weight)
    down_net = Gather(net, down_weight)
    residual = tokens.astype(F32)
    normed_one, inverse_one = normalize(residual)
    up_net.own, down_net.own = order(inverse_one, up_net.own, down_net.own)[1:]
    with jax.named_scope("small_gather"):
        small.across(order)
    with jax.named_scope("attn_gather"):
        attn_net.join_line(order)
        order.note(attn_net.line)
        attn_net.across()
    with jax.named_scope("small_gather"):
        small.other(order)
    with jax.named_scope("up_gather"):
        up_net.along(order(up_net.own))
    with jax.named_scope("small_gather"):
        (
            time_scale,
            embeds,
            gain_one,
            shift_one,
            gain_two,
            shift_two,
            down_bias_full,
            up_bias_full,
        ) = small.finish(order, time_embed)

    place = relative_order(net, wide_rows, width)
    permute = (jnp.arange(width, dtype=jnp.int32)[:, None] == place[None, :]).astype(BF16)

    def turn(values_in):
        return back_dot(permute, values_in).astype(BF16)

    key_mask = jnp.arange(length, dtype=jnp.int32)[:, None] < lengths[None, :]
    affine_one = normed_one * gain_one + shift_one
    attn_in = (affine_one * time_scale).astype(BF16)
    cosine, sine = rotary_tables(length)
    order.note(attn_in, cosine, sine)
    turned_one = order.note(turn(order(attn_in)))
    with jax.named_scope("attn_gather"):
        attn_net.join_across(order)
        attn_net.corners()
    with jax.named_scope("up_gather"):
        up_net.join_line(order)
        order.note(up_net.line)
    with jax.named_scope("down_gather"):
        down_net.along(order(down_net.own))
    with jax.named_scope("attn_gather"):
        plan, pieces = attn_net.finish(order)
    with jax.named_scope("up_gather"):
        up_net.line = order(up_net.line)
        up_net.across()
    qkv, qkv_full, out_full = qkv_rotated(net, attn_in, plan, pieces, wide_rows, cosine, sine)
    order.note(qkv)
    pairs = heads // 2
    part = pairs // 2
    with jax.named_scope("down_gather"):
        down_net.join_line(order)
        order.note(down_net.line)
    context = order.note(attend(lengths, order(qkv), 0, pairs))
    with jax.named_scope("up_gather"):
        up_net.join_across(order)
        up_net.corners()
    context = order(context)
    hidden = residual + jnp.dot(context, out_full, preferred_element_type=F32)
    normed_two, inverse_two = normalize(hidden)
    affine_two = normed_two * gain_two + shift_two
    mlp_in = (affine_two * time_scale).astype(BF16)
    order.note(mlp_in)
    turned_ctx = order.note(turn(order(context)))
    with jax.named_scope("up_gather"):
        plan, pieces = up_net.finish(order)
    with jax.named_scope("down_gather"):
        down_net.line = order(down_net.line)
        down_net.across()
    active, slope, up_full = up_gelu(
        net, order(mlp_in), plan, pieces, wide_rows, up_bias_full
    )
    order.note(active)

    grad_out = cotangent.astype(F32) * key_mask.astype(F32)
    grad_branch = grad_out.astype(BF16)
    with jax.named_scope("down_grad"):
        tall = order.note(tall_rows_dot(order(active), grad_branch))
        down_mine = lax.psum_scatter(tall, "fsdp", scatter_dimension=0, tiled=True)
    down_bias_grad = jnp.sum(grad_branch.astype(F32), axis=0, keepdims=True)
    with jax.named_scope("down_gather"):
        down_net.join_across(order)
        down_net.corners()
    turned_two = order.note(turn(order(mlp_in)))
    with jax.named_scope("down_gather"):
        plan, pieces = down_net.finish(order)
    grad_pre, up_bias_grad, down_full = down_back(
        net, order(grad_branch), plan, pieces, tall_rows, slope
    )
    grad_pre = order(order.note(grad_pre))
    grad_mlp_in = back_dot(grad_pre, up_full)
    grad_affine_two = grad_mlp_in * time_scale
    grad_scale = jnp.sum(grad_mlp_in * affine_two, axis=0, keepdims=True)
    mlp_gain_grad = jnp.sum(grad_affine_two * normed_two, axis=0, keepdims=True)
    mlp_shift_grad = jnp.sum(grad_affine_two, axis=0, keepdims=True)
    grad_hidden = grad_out + norm_back(grad_affine_two * gain_two, normed_two, inverse_two)
    grad_attn = order.note(grad_hidden.astype(BF16))
    wide_half = wide_rows // 2
    wide_parts = kept_parts(net.yn, wide_half)
    up_red, low_red, high_red = Scatter(net, True), Scatter(net, False), Scatter(net, True)
    up_pairs = [(turned_two, grad_pre), (turned_ctx, grad_attn)]
    with jax.named_scope("up_grad"):
        order(grad_pre)
        up_red.core(order.note(wide_rows_dot(1, half, up_pairs)))
    grad_context = order.note(back_dot(order(grad_attn), out_full).astype(BF16))
    with jax.named_scope("up_grad"):
        sent = up_red.join_core(order)
        kept = wide_rows_dot(0, half, up_pairs, sent, wide_parts)
        order.note(kept[0])
        up_red.corners(*kept)
    low = attend_back(lengths, qkv, order(grad_context), cosine, sine, 0, part)
    order.note(low)
    with jax.named_scope("qkv_grad"):
        low_red.core(order.note(wide_rows_dot(1, half, [(turned_one, order(low))])))
    with jax.named_scope("up_grad"):
        up_red.across(order)
    high = attend_back(lengths, qkv, order(grad_context), cosine, sine, part, pairs - part)
    order.note(high)
    with jax.named_scope("qkv_grad"):
        sent = low_red.join_core(order)
        kept = wide_rows_dot(0, half, [(turned_one, low)], sent, wide_parts)
        order.note(kept[0])
        low_red.corners(*kept)
        high_red.core(order.note(wide_rows_dot(1, half, [(turned_one, order(high))])))
        sent = high_red.join_core(order)
        kept = wide_rows_dot(0, half, [(turned_one, high)], sent, wide_parts)
        order.note(kept[0])
        high_red.corners(*kept)
    with jax.named_scope("up_grad"):
        up_line = Line(net, wide_half, [up_red.group(order)])
        order.note(up_line.kept)
    with jax.named_scope("qkv_grad"):
        low_red.across(order)
    grad_qkv = jnp.concatenate([item for i in range(3) for item in (low[i], high[i])], axis=1)
    grad_attn_in = back_dot(order(grad_qkv), qkv_full)
    grad_affine_one = grad_attn_in * time_scale
    grad_scale = grad_scale + jnp.sum(grad_attn_in * affine_one, axis=0, keepdims=True)
    attn_gain_grad = jnp.sum(grad_affine_one * normed_one, axis=0, keepdims=True)
    attn_shift_grad = jnp.sum(grad_affine_one, axis=0, keepdims=True)
    token_grad = (
        grad_hidden + norm_back(grad_affine_one * gain_one, normed_one, inverse_one)
    ).astype(BF16)
    order.note(token_grad, grad_scale)
    with jax.named_scope("qkv_grad"):
        high_red.across(order)
    with jax.named_scope("small_sums"):
        sums = jnp.concatenate(
            [
                attn_gain_grad,
                attn_shift_grad,
                mlp_gain_grad,
                mlp_shift_grad,
                down_bias_grad,
                up_bias_grad.reshape(-1, width),
            ],
            axis=0,
        )
        count = sums.shape[0]
        spots = jnp.arange(fs, dtype=jnp.int32)[:, None] == net.me
        packed = jnp.concatenate([sums, jnp.where(spots, grad_scale, 0.0)], axis=0)
        moved = net.c(packed)
    with jax.named_scope("up_grad"):
        up_line.nearer(order)
    with jax.named_scope("small_sums"):
        packed = packed + order(moved)
        moved = [net.y(packed, s) for s in range(1, net.yn)]
    branch_out = jnp.dot(order(active), down_full, preferred_element_type=F32) + down_bias_full
    layer_out = (hidden + branch_out).astype(BF16)
    order.note(layer_out)
    with jax.named_scope("small_sums"):
        for item in moved:
            packed = packed + order(item)
        moved = net.z(packed, 1)
    with jax.named_scope("qkv_grad"):
        qkv_line = Line(net, wide_half, [low_red.group(order), high_red.group(order)])
    with jax.named_scope("small_sums"):
        packed = packed + order(moved)
        moved = net.z(packed, 2)
    with jax.named_scope("up_grad"):
        up_line.last(order)
    with jax.named_scope("qkv_grad"):
        qkv_line.nearer(order)
    with jax.named_scope("small_sums"):
        packed = packed + order(moved)
        mine = lax.dynamic_slice_in_dim(embeds, net.me * te_rows, te_rows, 1)
        time_part = lax.dot_general(
            mine,
            packed[count:],
            (((0,), (0,)), ((), ())),
            precision=lax.Precision.HIGHEST,
            preferred_element_type=F32,
        )
        each = attn_gain.shape[0]
        vector_part = lax.dynamic_slice_in_dim(packed[:5], net.me * each, each, 1)
        bias_part = lax.dynamic_slice_in_dim(
            packed[5:count].reshape(1, -1), net.me * up_bias.shape[0], up_bias.shape[0], 1
        )
        packed = jnp.concatenate(
            [
                time_part,
                jnp.pad(vector_part, ((0, 0), (0, width - each))),
                jnp.pad(bias_part, ((0, 0), (0, width - up_bias.shape[0]))),
            ],
            axis=0,
        )
        if dp > 2:
            packed = lax.psum(packed, "dp")
        else:
            packed = packed + net.x(packed)
        time_weight_grad = packed[:te_rows]
        vector_grads = [packed[te_rows + i, :each] for i in range(5)]
        up_bias_out = packed[te_rows + 5, : up_bias.shape[0]]
    with jax.named_scope("down_grad"):
        down_mine = order(down_mine)
        if dp > 2:
            down_weight_grad = lax.psum(down_mine, "dp").astype(F32)
        else:
            down_other = net.x(down_mine)
    with jax.named_scope("qkv_grad"):
        qkv_line.last(order)
        whole = qkv_line.finish(order)
    with jax.named_scope("up_grad"):
        both = up_line.finish(order)
        ups = grad_pre.shape[1]
        up_weight_grad, out_weight_grad = both[:, :ups], both[:, ups:]
    if dp == 2:
        down_weight_grad = down_mine.astype(F32) + down_other.astype(F32)
    wide_low, wide_high = low.shape[2], high.shape[2]
    low_part, high_part = whole[:, : 3 * wide_low], whole[:, 3 * wide_low :]
    qkv_weight_grad = jnp.concatenate(
        [
            item
            for i in range(3)
            for item in (
                low_part[:, i * wide_low : (i + 1) * wide_low],
                high_part[:, i * wide_high : (i + 1) * wide_high],
            )
        ],
        axis=1,
    )
    return (
        layer_out[None],
        token_grad[None],
        time_weight_grad,
        vector_grads[0],
        vector_grads[1],
        qkv_weight_grad,
        out_weight_grad,
        vector_grads[2],
        vector_grads[3],
        up_weight_grad,
        up_bias_out,
        down_weight_grad,
        vector_grads[4],
    )


def solution(mesh):
    return jax.shard_map(
        functools.partial(per_device, mesh.shape["dp"], mesh.shape["fsdp"]),
        mesh=mesh,
        in_specs=(
            P(("dp", "fsdp"), None, None),
            P(("dp", "fsdp")),
            P(("dp", "fsdp"), None),
            P(("dp", "fsdp"), None, None),
            P("fsdp", None),
            P("fsdp"),
            P("fsdp"),
            P("fsdp", None),
            P("fsdp", None),
            P("fsdp"),
            P("fsdp"),
            P("fsdp", None),
            P("fsdp"),
            P("fsdp", None),
            P("fsdp"),
        ),
        out_specs=(
            P(("dp", "fsdp"), None, None),
            P(("dp", "fsdp"), None, None),
            P("fsdp", None),
            P("fsdp"),
            P("fsdp"),
            P("fsdp", None),
            P("fsdp", None),
            P("fsdp"),
            P("fsdp"),
            P("fsdp", None),
            P("fsdp"),
            P("fsdp", None),
            P("fsdp"),
        ),
        check_vma=False,
    )
```

```python
import functools
import math

import jax
import jax.numpy as jnp
from jax import lax
from jax.experimental import pallas as pl
from jax.experimental.pallas import tpu as pltpu
from jax.sharding import PartitionSpec as P

HD = 64
ZN = 4
PAIR = 128
LOG2E = math.log2(math.e)
ROOT = math.sqrt(2.0 / math.pi)
F32 = jnp.float32
BF16 = jnp.bfloat16


def normalize(values_in):
    center = values_in - jnp.mean(values_in, axis=-1, keepdims=True)
    inverse = lax.rsqrt(jnp.mean(center * center, axis=-1, keepdims=True) + 1e-05)
    return (center * inverse, inverse)


def norm_back(grad_hat, normed, inverse):
    return inverse * (
        grad_hat
        - jnp.mean(grad_hat, axis=-1, keepdims=True)
        - normed * jnp.mean(grad_hat * normed, axis=-1, keepdims=True)
    )


def rows_dot(left, right):
    return lax.dot_general(
        left, right, (((0,), (0,)), ((), ())), preferred_element_type=F32
    )


def back_dot(grad_in, weight):
    return lax.dot_general(
        grad_in, weight, (((1,), (1,)), ((), ())), preferred_element_type=F32
    )


def rotary_tables(length):
    half_size = HD // 2
    frequency = jnp.exp(
        jnp.arange(half_size, dtype=F32) * (-2.0 * math.log(10000.0) / HD)
    )
    angles = jnp.arange(length, dtype=F32)[:, None] * frequency[None, :]
    angles = jnp.concatenate([angles] * (PAIR // half_size), axis=-1)
    return (jnp.cos(angles), jnp.sin(angles))


class Order:
    def __init__(self):
        self.mark = ()

    def __call__(self, *arrays):
        out = lax.optimization_barrier((*arrays, *self.mark))[: len(arrays)]
        self.mark = (out[0],)
        return out[0] if len(out) == 1 else out

    def note(self, *arrays):
        self.mark = arrays
        return arrays[0] if len(arrays) == 1 else arrays


def scoped(name):
    def wrap(function):
        @functools.wraps(function)
        def inner(*args, **kwargs):
            with jax.named_scope(name):
                return function(*args, **kwargs)

        return inner

    return wrap


class Net:
    def __init__(self, dp, fs):
        self.dp, self.fs = dp, fs
        self.yn = fs // (2 * ZN)
        index = lax.axis_index("fsdp")
        self.me = index
        self.z0 = index // (2 * self.yn)
        self.y0 = (index // 2) % self.yn
        self.c0 = index % 2
        self.p0 = lax.axis_index("dp") % 2

    def perm(self, values_in, zx, dy, dc):
        pairs = []
        for i in range(self.fs):
            z, y, c = i // (2 * self.yn), (i // 2) % self.yn, i % 2
            to = ((z ^ zx) * self.yn + (y + dy) % self.yn) * 2 + (c ^ dc)
            pairs.append((i, to))
        return lax.ppermute(values_in, "fsdp", pairs)

    @scoped("z_hop")
    def z(self, values_in, k):
        return self.perm(values_in, k, 0, 0)

    @scoped("y_hop")
    def y(self, values_in, s):
        return self.perm(values_in, 0, s, 0)

    @scoped("core_hop")
    def c(self, values_in):
        return self.perm(values_in, 0, 0, 1)

    @scoped("x_hop")
    def x(self, values_in):
        return lax.ppermute(values_in, "dp", [(i, i ^ 1) for i in range(self.dp)])


def stack_kernel(*refs):
    at = 0
    for item in refs[:-1]:
        rows = item.shape[0]
        refs[-1][at : at + rows, :] = item[...]
        at += rows


def stack_rows(*items):
    rows = sum(item.shape[0] for item in items)
    return pl.pallas_call(
        stack_kernel,
        out_shape=jax.ShapeDtypeStruct((rows, items[0].shape[1]), items[0].dtype),
        cost_estimate=cost(),
        name="stack_rows",
    )(*items)


class Gather:
    def __init__(self, net, shard):
        self.net = net
        self.rows, self.columns = shard.shape
        self.half = self.rows // 2
        self.own = lax.dynamic_slice_in_dim(shard, net.p0 * self.half, self.half, 0)

    def along(self, own):
        self.own = own
        self.parts = [self.net.z(own, k) for k in range(1, ZN)]

    def join_line(self, order):
        self.line = stack_rows(*order(self.own, *self.parts))

    def across(self):
        net = self.net
        self.over = net.x(self.line)
        self.beside = [net.y(self.line, s) for s in range(1, net.yn)]

    def join_across(self, order):
        self.over, *self.beside = order(self.over, *self.beside)

    def corners(self):
        net = self.net
        mid = (ZN // 2) * self.half
        self.corner_one = [net.x(item[:mid]) for item in self.beside]
        self.corner_two = [net.y(self.over[mid:], s) for s in range(1, net.yn)]
        self.pieces = [self.line, self.over] + self.beside
        self.plan = [(0, 0, 0, ZN), (0, 1, 0, ZN)]
        self.plan += [(s, 0, 0, ZN) for s in range(1, net.yn)]
        self.moved = [net.c(item) for item in self.pieces]

    def finish(self, order):
        net = self.net
        late = order(*self.corner_one, *self.corner_two)
        plan = [(s, 1, 0, ZN // 2) for s in range(1, net.yn)]
        plan += [(s, 1, ZN // 2, ZN - ZN // 2) for s in range(1, net.yn)]
        pieces = self.pieces + list(late) + self.moved + [net.c(item) for item in late]
        plan = self.plan + plan
        full = [(s, q, side, first, count) for side in range(2) for s, q, first, count in plan]
        return full, pieces


def piece_spots(plan, where_ref, rows, half, yn):
    z0, y0, c0, p0 = where_ref[0], where_ref[1], where_ref[2], where_ref[3]
    spots = []
    for i, (s, q, side, first, count) in enumerate(plan):
        y = lax.rem(y0 + yn - s, yn)
        p = lax.rem(p0 + q, 2)
        c = lax.rem(c0 + side, 2)
        for k in range(count):
            z = lax.bitwise_xor(z0, jnp.int32(first + k))
            start = pl.multiple_of(((z * yn + y) * 2 + c) * rows + p * half, half)
            spots.append((i, k * half, first + k, start))
    return spots


def pack_kernel(*refs):
    time_ref, vectors, out_ref = refs[0], refs[1:-1], refs[-1]
    out_ref[...] = jnp.zeros_like(out_ref)
    rows = time_ref.shape[0]
    out_ref[:rows, :] = time_ref[...]
    for i, item in enumerate(vectors):
        out_ref[rows + i : rows + i + 1, : item.shape[1]] = item[...]


def small_kernel(rows, te_rows, sizes, yn, where_ref, embed_ref, own_ref, other_ref, *refs):
    scale_ref, all_ref, outs, held, sems = refs[0], refs[1], refs[2:-2], refs[-2], refs[-1]
    z0, y0, c0 = where_ref[0], where_ref[1], where_ref[2]
    copies = []
    for side, piece_ref in enumerate((own_ref, other_ref)):
        c = lax.rem(c0 + side, 2)
        for s in range(yn):
            y = lax.rem(y0 + yn - s, yn)
            for k in range(ZN):
                z = lax.bitwise_xor(z0, jnp.int32(k))
                copies.append(
                    pltpu.make_async_copy(
                        piece_ref.at[s * ZN + k],
                        held.at[(z * yn + y) * 2 + c],
                        sems.at[len(copies)],
                    )
                )
    for copy in copies:
        copy.start()
    for copy in copies:
        copy.wait()
    fs = held.shape[0]
    scale = jnp.ones_like(scale_ref)
    whole = jnp.concatenate([held[f, :te_rows, :] for f in range(fs)], axis=0)
    scale_ref[...] = scale + jnp.dot(embed_ref[...], whole, preferred_element_type=F32)
    for i, (size, out_ref) in enumerate(zip(sizes, outs)):
        pieces = [
            held[f, te_rows + i : te_rows + i + 1, :size].astype(F32) for f in range(fs)
        ]
        out_ref[...] = jnp.concatenate(pieces, axis=1)
    last, wide = te_rows + len(sizes), embed_ref.shape[1]
    all_ref[...] = jnp.concatenate(
        [held[f, last : last + 1, :wide].astype(F32) for f in range(fs)], axis=0
    )


class SmallGather:
    def __init__(self, net, time_weight, vectors, embed):
        self.net, self.sizes = net, [item.shape[0] for item in vectors]
        self.te_rows, self.width = time_weight.shape
        self.rows = self.te_rows + len(vectors) + 1
        self.rows += -self.rows % 16
        self.packed = pl.pallas_call(
            pack_kernel,
            out_shape=jax.ShapeDtypeStruct((self.rows, self.width), BF16),
            cost_estimate=cost(),
            name="pack_small",
        )(time_weight, *[item.reshape(1, -1) for item in vectors], embed)
        self.parts = [net.z(self.packed, k) for k in range(1, ZN)]

    def across(self, order):
        net = self.net
        self.line = jnp.stack(order(self.packed, *self.parts))
        self.beside = [net.y(self.line, s) for s in range(1, net.yn)]

    def other(self, order):
        self.line, *self.beside = order(self.line, *self.beside)
        self.sides = jnp.concatenate([self.line] + self.beside, axis=0)
        self.moved = self.net.c(self.sides)

    def finish(self, order, embed):
        net, fs = self.net, self.net.fs
        moved = order(self.moved)
        where = jnp.stack([net.z0, net.y0, net.c0]).astype(jnp.int32)
        shapes = [(1, self.width), (fs, embed.shape[1])]
        shapes += [(1, size * fs) for size in self.sizes]
        outs = pl.pallas_call(
            functools.partial(small_kernel, self.rows, self.te_rows, self.sizes, net.yn),
            out_shape=[jax.ShapeDtypeStruct(shape, F32) for shape in shapes],
            grid_spec=pltpu.PrefetchScalarGridSpec(
                num_scalar_prefetch=1,
                grid=(1,),
                in_specs=[pl.BlockSpec(embed.shape, lambda i, r: (0, 0))]
                + [pl.BlockSpec(memory_space=pl.ANY)] * 2,
                out_specs=[whole_spec(shape) for shape in shapes],
                scratch_shapes=[
                    pltpu.VMEM((fs, self.rows, self.width), BF16),
                    pltpu.SemaphoreType.DMA((fs,)),
                ],
            ),
            cost_estimate=cost(),
            name="small_join",
        )(where, embed, self.sides, moved)
        order.note(outs[0])
        return outs


def relative_order(net, rows, total):
    half = rows // 2
    d = jnp.arange(total, dtype=jnp.int32)
    f, i = d // rows, d % rows
    z, y, c = f // (2 * net.yn), (f // 2) % net.yn, f % 2
    p, j = i // half, i % half
    c, y, p, z = c ^ net.c0, (y - net.y0) % net.yn, p ^ net.p0, z ^ net.z0
    return (((c * net.yn + y) * 2 + p) * ZN + z) * half + j


def add_low(*items):
    total = items[0].astype(F32)
    for item in items[1:]:
        total = total + item.astype(F32)
    return total.astype(BF16)


def sum_kernel(counts, keep, *refs):
    total = sum(counts)
    kept_ref, sent_ref = refs[total], refs[total + 1]
    at, column = 0, 0
    for count in counts:
        items = refs[at : at + count]
        at += count
        wide = items[0].shape[1]
        value = items[0][...].astype(F32)
        for item in items[1:]:
            value = value + item[...].astype(F32)
        kept_ref[:, column : column + wide] = value[:keep, :]
        sent_ref[:, column : column + wide] = value[keep:, :].astype(BF16)
        column += wide


def sum_split(groups, keep):
    rows = groups[0][0].shape[0]
    columns = sum(group[0].shape[1] for group in groups)
    return pl.pallas_call(
        functools.partial(sum_kernel, [len(group) for group in groups], keep),
        out_shape=[
            jax.ShapeDtypeStruct((keep, columns), F32),
            jax.ShapeDtypeStruct((rows - keep, columns), BF16),
        ],
        cost_estimate=cost(),
        name="sum_split",
    )(*[item for group in groups for item in group])


def merge_kernel(shifts, over_ref, *refs):
    sides, came_x, came_y = (refs[i * shifts : (i + 1) * shifts] for i in range(3))
    over_out, outs = refs[3 * shifts], refs[3 * shifts + 1 :]
    half = over_ref.shape[0] // 2
    over_out[:half, :] = over_ref[:half, :]
    value = over_ref[half:, :].astype(F32)
    for item in came_y:
        value = value + item[...].astype(F32)
    over_out[half:, :] = value.astype(BF16)
    for side_ref, item, out_ref in zip(sides, came_x, outs):
        value = side_ref[:half, :].astype(F32) + item[...].astype(F32)
        out_ref[:half, :] = value.astype(BF16)
        out_ref[half:, :] = side_ref[half:, :]


def merge_corners(over, sides, came_x, came_y):
    shape = jax.ShapeDtypeStruct(over.shape, BF16)
    return pl.pallas_call(
        functools.partial(merge_kernel, len(sides)),
        out_shape=[shape] * (1 + len(sides)),
        cost_estimate=cost(),
        name="merge_corners",
    )(over, *sides, *came_x, *came_y)


class Scatter:
    def __init__(self, net):
        self.net = net

    def core(self, send):
        self.sent = self.net.c(send)

    def join_core(self, order):
        self.sent = order(self.sent)
        return self.sent

    def corners(self, own, over, *rest):
        net = self.net
        self.own, self.over, self.side = own, over, list(rest[0::3])
        self.came_x = [net.x(item) for item in rest[1::3]]
        self.came_y = [net.y(item, s + 1) for s, item in enumerate(rest[2::3])]

    def across(self, order):
        net, count = self.net, len(self.side)
        came = order(*self.came_x, *self.came_y)
        self.over, *self.side = merge_corners(self.over, self.side, came[:count], came[count:])
        order.note(self.over)
        self.over = net.x(self.over)
        self.side = [net.y(item, s + 1) for s, item in enumerate(self.side)]

    def group(self, order):
        return [self.own, *order(self.over, *self.side)]


class Line:
    def __init__(self, net, half, groups):
        self.net, self.half = net, half
        self.kept, far = sum_split(groups, (ZN // 2) * half)
        self.far = net.z(far, 2)

    def nearer(self, order):
        self.here, near = sum_split([[self.kept, order(self.far)]], self.half)
        self.near = self.net.z(near, 1)

    def last(self, order):
        net = self.net
        mine = add_low(self.here, order(self.near))
        if net.dp > 2:
            groups = [list(range(q, net.dp, 2)) for q in range(2)]
            mine = lax.psum(mine, "dp", axis_index_groups=groups)
        self.mine, self.other = mine, net.x(mine)

    def finish(self, order):
        mine, other = self.mine, order(self.other)
        first = jnp.where(self.net.p0 == 0, mine, other)
        second = jnp.where(self.net.p0 == 0, other, mine)
        return jnp.concatenate([first, second], axis=0).astype(F32)


def kept_parts(yn, half):
    line = ZN * half
    spots = [(0, line), (line, line)]
    for s in range(1, yn):
        first = 2 * s * line
        spots.append((first, line))
        spots += [(first + line + i * (line // 2), line // 2) for i in range(2)]
    return spots


def cost():
    return pl.CostEstimate(flops=1000, bytes_accessed=1000, transcendentals=0)


def weight_copies(plan, where_ref, rows, half, yn, pieces, targets, sems):
    spots = piece_spots(plan, where_ref, rows, half, yn)
    groups, count, column = [], 0, 0
    for target, first, wide in targets:
        group = []
        for i, row, shift, start in spots:
            group.append(
                pltpu.make_async_copy(
                    pieces[i].at[pl.ds(row, half), pl.ds(column, wide)],
                    target.at[pl.ds(start, half), pl.ds(first, wide)],
                    sems.at[count],
                )
            )
            count += 1
        column += wide
        groups.append(group)
    for group in groups:
        for copy in group:
            copy.start()
    return groups


def finish_copies(copies):
    for copy in copies:
        copy.wait()


def back_copy(held, out, first, wide, sem):
    spot = pl.ds(first, wide)
    copy = pltpu.make_async_copy(held.at[:, spot], out.at[:, spot], sem)
    copy.start()
    return copy


def qkv_kernel(plan, rows, half, yn, where_ref, x_ref, cos_ref, sin_ref, *refs):
    pieces = refs[: len(plan)]
    out_ref, wq_ref, wo_ref, wq, wo, low, sems, back_sems = refs[len(plan) :]
    wide = wo.shape[1]
    targets = [(wq, part * wide, wide) for part in range(3)] + [(wo, 0, wide)]
    groups = weight_copies(plan, where_ref, rows, half, yn, pieces, targets, sems)
    cosine, sine = cos_ref[...], sin_ref[...]
    front = lax.broadcasted_iota(jnp.int32, cosine.shape, 1) % HD < HD // 2
    backs = []
    for part in range(3):
        finish_copies(groups[part])
        backs.append(back_copy(wq, wq_ref, part * wide, wide, back_sems.at[part]))
        for j in range(wide // (2 * PAIR)):
            first = part * wide + j * 2 * PAIR
            acc = jnp.dot(
                x_ref[...], wq[:, first : first + 2 * PAIR], preferred_element_type=F32
            )
            for i in range(2):
                piece = acc[:, i * PAIR : (i + 1) * PAIR]
                if part < 2:
                    turned = jnp.where(
                        front,
                        -pltpu.roll(piece, PAIR - HD // 2, 1),
                        pltpu.roll(piece, HD // 2, 1),
                    )
                    piece = piece * cosine + turned * sine
                low[:, first + i * PAIR : first + (i + 1) * PAIR] = piece.astype(BF16)
        backs.append(back_copy(low, out_ref, part * wide, wide, back_sems.at[4 + part]))
    finish_copies(groups[3])
    backs.append(back_copy(wo, wo_ref, 0, wide, back_sems.at[3]))
    finish_copies(backs)


def where_of(net):
    return jnp.stack([net.z0, net.y0, net.c0, net.p0]).astype(jnp.int32)


ANY = pl.BlockSpec(memory_space=pl.ANY)


def whole_spec(shape):
    return pl.BlockSpec(shape, lambda i, r: (0, 0))


def qkv_rotated(net, x, plan, pieces, rows, cosine, sine):
    tokens, depth = x.shape
    total = net.fs * rows
    blocks = sum(entry[4] for entry in plan)
    half = rows // 2
    return pl.pallas_call(
        functools.partial(qkv_kernel, plan, rows, half, net.yn),
        grid_spec=pltpu.PrefetchScalarGridSpec(
            num_scalar_prefetch=1,
            grid=(1,),
            in_specs=[whole_spec(x.shape), whole_spec(cosine.shape), whole_spec(sine.shape)]
            + [ANY] * len(pieces),
            out_specs=[ANY] * 3,
            scratch_shapes=[
                pltpu.VMEM((total, 3 * depth), BF16),
                pltpu.VMEM((total, depth), BF16),
                pltpu.VMEM((tokens, 3 * depth), BF16),
                pltpu.SemaphoreType.DMA((4 * blocks,)),
                pltpu.SemaphoreType.DMA((7,)),
            ],
        ),
        out_shape=[
            jax.ShapeDtypeStruct((tokens, 3 * depth), BF16),
            jax.ShapeDtypeStruct((total, 3 * depth), BF16),
            jax.ShapeDtypeStruct((total, depth), BF16),
        ],
        compiler_params=pltpu.CompilerParams(vmem_limit_bytes=32 * 2**20),
        cost_estimate=cost(),
        name="qkv_rotated",
    )(where_of(net), x, cosine, sine, *pieces)


def up_kernel(plan, rows, half, yn, where_ref, x_ref, b_ref, *refs):
    pieces = refs[: len(plan)]
    act_out, slope_out, w_out, w, act, slope, sems, back_sems = refs[len(plan) :]
    total = w.shape[1]
    wide = min(1024, total)
    step = min(256, wide)
    parts = total // wide
    targets = [(w, part * wide, wide) for part in range(parts)]
    groups = weight_copies(plan, where_ref, rows, half, yn, pieces, targets, sems)
    backs = []
    for part in range(parts):
        finish_copies(groups[part])
        backs.append(back_copy(w, w_out, part * wide, wide, back_sems.at[3 * part]))
        for first in range(part * wide, (part + 1) * wide, step):
            spot = slice(first, first + step)
            v = jnp.dot(x_ref[...], w[:, spot], preferred_element_type=F32) + b_ref[:, spot]
            square = v * v
            bend = jnp.tanh(v * (ROOT + ROOT * 0.044715 * square))
            half_up = 0.5 + 0.5 * bend
            act[:, spot] = (v * half_up).astype(BF16)
            rise = 0.5 * ROOT + (1.5 * 0.044715 * ROOT) * square
            slope[:, spot] = (half_up + v * (1.0 - bend * bend) * rise).astype(BF16)
        backs.append(back_copy(act, act_out, part * wide, wide, back_sems.at[3 * part + 1]))
        backs.append(back_copy(slope, slope_out, part * wide, wide, back_sems.at[3 * part + 2]))
    finish_copies(backs)


def up_gelu(net, x, plan, pieces, rows, bias):
    tokens, depth = x.shape
    total = bias.shape[1]
    parts = total // min(1024, total)
    blocks = sum(entry[4] for entry in plan)
    return pl.pallas_call(
        functools.partial(up_kernel, plan, rows, rows // 2, net.yn),
        grid_spec=pltpu.PrefetchScalarGridSpec(
            num_scalar_prefetch=1,
            grid=(1,),
            in_specs=[whole_spec(x.shape), whole_spec(bias.shape)] + [ANY] * len(pieces),
            out_specs=[ANY] * 3,
            scratch_shapes=[
                pltpu.VMEM((depth, total), BF16),
                pltpu.VMEM((tokens, total), BF16),
                pltpu.VMEM((tokens, total), BF16),
                pltpu.SemaphoreType.DMA((parts * blocks,)),
                pltpu.SemaphoreType.DMA((3 * parts,)),
            ],
        ),
        out_shape=[
            jax.ShapeDtypeStruct((tokens, total), BF16),
            jax.ShapeDtypeStruct((tokens, total), BF16),
            jax.ShapeDtypeStruct((depth, total), BF16),
        ],
        compiler_params=pltpu.CompilerParams(vmem_limit_bytes=40 * 2**20),
        cost_estimate=cost(),
        name="up_gelu",
    )(where_of(net), x, bias, *pieces)


def down_kernel(plan, rows, half, yn, where_ref, g_ref, slope_ref, *refs):
    pieces = refs[: len(plan)]
    out_ref, sum_ref, w_ref, w, slope, low, sems, slope_sems, back_sems = refs[len(plan) :]
    spots = piece_spots(plan, where_ref, rows, half, yn)
    group_rows = w.shape[0] // ZN
    step = min(256, group_rows)
    z0 = where_ref[0]
    groups = [[] for _ in range(ZN)]
    for count, (i, row, shift, start) in enumerate(spots):
        copy = pltpu.make_async_copy(
            pieces[i].at[pl.ds(row, half), :], w.at[pl.ds(start, half), :], sems.at[count]
        )
        groups[shift].append(copy)
    slopes = []
    for k in range(ZN):
        at = pl.multiple_of(lax.bitwise_xor(z0, jnp.int32(k)) * group_rows, group_rows)
        for copy in groups[k]:
            copy.start()
        copy = pltpu.make_async_copy(
            slope_ref.at[:, pl.ds(at, group_rows)], slope.at[k], slope_sems.at[k]
        )
        copy.start()
        slopes.append(copy)
    backs = []
    for k in range(ZN):
        at = pl.multiple_of(lax.bitwise_xor(z0, jnp.int32(k)) * group_rows, group_rows)
        finish_copies(groups[k])
        slopes[k].wait()
        here = pl.ds(at, group_rows)
        copy = pltpu.make_async_copy(w.at[here, :], w_ref.at[here, :], back_sems.at[2 * k])
        copy.start()
        backs.append(copy)
        for j in range(group_rows // step):
            spot = slice(j * step, (j + 1) * step)
            inner = pl.multiple_of(at + j * step, step)
            acc = lax.dot_general(
                g_ref[...],
                w[pl.ds(inner, step), :],
                (((1,), (1,)), ((), ())),
                preferred_element_type=F32,
            )
            rounded = (acc * slope[k, :, spot].astype(F32)).astype(BF16)
            low[k, :, spot] = rounded
            sum_ref[:, pl.ds(inner, step)] = jnp.sum(
                rounded.astype(F32), axis=0, keepdims=True
            )
        copy = pltpu.make_async_copy(low.at[k], out_ref.at[:, here], back_sems.at[2 * k + 1])
        copy.start()
        backs.append(copy)
    finish_copies(backs)


def down_back(net, grad, plan, pieces, rows, slope):
    tokens, depth = grad.shape
    total = slope.shape[1]
    blocks = sum(entry[4] for entry in plan)
    return pl.pallas_call(
        functools.partial(down_kernel, plan, rows, rows // 2, net.yn),
        grid_spec=pltpu.PrefetchScalarGridSpec(
            num_scalar_prefetch=1,
            grid=(1,),
            in_specs=[whole_spec(grad.shape), ANY] + [ANY] * len(pieces),
            out_specs=[ANY, pl.BlockSpec((1, total), lambda i, r: (0, 0)), ANY],
            scratch_shapes=[
                pltpu.VMEM((total, depth), BF16),
                pltpu.VMEM((ZN, tokens, total // ZN), BF16),
                pltpu.VMEM((ZN, tokens, total // ZN), BF16),
                pltpu.SemaphoreType.DMA((blocks,)),
                pltpu.SemaphoreType.DMA((ZN,)),
                pltpu.SemaphoreType.DMA((2 * ZN,)),
            ],
        ),
        out_shape=[
            jax.ShapeDtypeStruct((tokens, total), BF16),
            jax.ShapeDtypeStruct((1, total), F32),
            jax.ShapeDtypeStruct((total, depth), BF16),
        ],
        compiler_params=pltpu.CompilerParams(vmem_limit_bytes=40 * 2**20),
        cost_estimate=cost(),
        name="down_back",
    )(where_of(net), grad, slope, *pieces)


def attend_kernel(len_ref, q_ref, k_ref, v_ref, out_ref):
    q, k, v = q_ref[...], k_ref[...], v_ref[...]
    length = k.shape[0]
    first = lax.broadcasted_iota(jnp.int32, q.shape, 1) < HD
    valid = lax.broadcasted_iota(jnp.int32, (1, length), 1) < len_ref[0]
    zero = jnp.zeros_like(q)
    outs = []
    for h in range(2):
        one = jnp.where(first, q, zero) if h == 0 else jnp.where(first, zero, q)
        scores = lax.dot_general(
            one, k, (((1,), (1,)), ((), ())), preferred_element_type=F32
        )
        scores = jnp.where(valid, scores * HD**-0.5, -1000000000.0)
        top = jnp.max(scores, axis=1, keepdims=True)
        exponent = jnp.exp2((scores - top) * LOG2E)
        total = jnp.sum(exponent, axis=1, keepdims=True)
        mixed = jnp.dot(exponent.astype(BF16), v, preferred_element_type=F32)
        outs.append(mixed * (1.0 / total))
    out_ref[...] = jnp.where(first, outs[0], outs[1]).astype(BF16)


def attend(length, qkv, first_pair, pairs):
    rows, total = qkv.shape
    count = total // 3 // PAIR

    def pick(part):
        return pl.BlockSpec((rows, PAIR), lambda j, r: (0, part * count + first_pair + j))

    return pl.pallas_call(
        attend_kernel,
        grid_spec=pltpu.PrefetchScalarGridSpec(
            num_scalar_prefetch=1,
            grid=(pairs,),
            in_specs=[pick(0), pick(1), pick(2)],
            out_specs=pl.BlockSpec((rows, PAIR), lambda j, r: (0, j)),
        ),
        out_shape=jax.ShapeDtypeStruct((rows, pairs * PAIR), BF16),
        cost_estimate=cost(),
        name="attend",
    )(length, qkv, qkv, qkv)


def attend_back_kernel(len_ref, q_ref, k_ref, v_ref, g_ref, cos_ref, sin_ref, out_ref):
    q, k, v, g = q_ref[...], k_ref[...], v_ref[...], g_ref[...]
    length = k.shape[0]
    lane = lax.broadcasted_iota(jnp.int32, q.shape, 1)
    first = lane < HD
    valid = lax.broadcasted_iota(jnp.int32, (length, length), 0) < len_ref[0]
    zero = jnp.zeros_like(q)
    grads = []
    for h in range(2):
        key = jnp.where(first, k, zero) if h == 0 else jnp.where(first, zero, k)
        value = jnp.where(first, v, zero) if h == 0 else jnp.where(first, zero, v)
        scores = lax.dot_general(
            key, q, (((1,), (1,)), ((), ())), preferred_element_type=F32
        )
        scores = jnp.where(valid, scores * HD**-0.5, -1000000000.0)
        top = jnp.max(scores, axis=0, keepdims=True)
        exponent = jnp.exp2((scores - top) * LOG2E)
        total = jnp.sum(exponent, axis=0, keepdims=True)
        probs = exponent * (1.0 / total)
        grad_probs = lax.dot_general(
            value, g, (((1,), (1,)), ((), ())), preferred_element_type=F32
        )
        delta = jnp.sum(grad_probs * probs, axis=0, keepdims=True)
        grad_scores = (probs * (grad_probs - delta)).astype(BF16)
        grads.append(
            (
                lax.dot_general(
                    grad_scores, k, (((0,), (0,)), ((), ())), preferred_element_type=F32
                ),
                jnp.dot(grad_scores, q, preferred_element_type=F32),
                jnp.dot(probs.astype(BF16), g, preferred_element_type=F32),
            )
        )
    front = lane % HD < HD // 2
    cosine, sine = cos_ref[...] * HD**-0.5, sin_ref[...] * HD**-0.5
    for i in range(2):
        grad = jnp.where(first, grads[0][i], grads[1][i])
        sined = grad * sine
        turned = jnp.where(
            front, pltpu.roll(sined, PAIR - HD // 2, 1), -pltpu.roll(sined, HD // 2, 1)
        )
        out_ref[i] = (grad * cosine + turned).astype(BF16)
    out_ref[2] = jnp.where(first, grads[0][2], grads[1][2]).astype(BF16)


def attend_back(length, qkv, grad, cosine, sine, first_pair, pairs):
    rows, total = qkv.shape
    count = total // 3 // PAIR

    def pick(part):
        return pl.BlockSpec((rows, PAIR), lambda j, r: (0, part * count + first_pair + j))

    table = pl.BlockSpec((rows, PAIR), lambda j, r: (0, 0))
    return pl.pallas_call(
        attend_back_kernel,
        grid_spec=pltpu.PrefetchScalarGridSpec(
            num_scalar_prefetch=1,
            grid=(pairs,),
            in_specs=[pick(0), pick(1), pick(2), pick(0), table, table],
            out_specs=pl.BlockSpec((3, rows, PAIR), lambda j, r: (0, 0, j)),
        ),
        out_shape=jax.ShapeDtypeStruct((3, rows, pairs * PAIR), BF16),
        cost_estimate=cost(),
        name="attend_back",
    )(length, qkv, qkv, qkv, grad, cosine, sine)


def tall_kernel(left_ref, grad_ref, out_ref):
    out_ref[...] = lax.dot_general(
        left_ref[...], grad_ref[...], (((0,), (0,)), ((), ())), preferred_element_type=F32
    ).astype(BF16)


def tall_rows_dot(left, grad):
    depth, columns = grad.shape
    total = left.shape[1]
    tall = min(1024, total)
    return pl.pallas_call(
        tall_kernel,
        grid=(total // tall,),
        in_specs=[
            pl.BlockSpec((depth, tall), lambda i: (0, i)),
            pl.BlockSpec((depth, columns), lambda i: (0, 0)),
        ],
        out_specs=pl.BlockSpec((tall, columns), lambda i: (i, 0)),
        out_shape=jax.ShapeDtypeStruct((total, columns), BF16),
        cost_estimate=cost(),
        name="tall_rows_dot",
    )(left, grad)


def wide_kernel(bounds, parts, *refs):
    step = pl.program_id(0)
    operands, rest = refs[: 2 * len(bounds)], refs[2 * len(bounds) :]

    def write(left_ref, grad_ref):
        grad = grad_ref[0] if len(grad_ref.shape) == 3 else grad_ref[...]
        acc = jnp.dot(left_ref[...], grad, preferred_element_type=F32)
        if parts is None:
            rest[-1][...] = acc.astype(BF16)
            return
        acc = acc + rest[0][...].astype(F32)
        for (first, rows), out_ref in zip(parts, rest[1:]):
            out_ref[...] = acc[first : first + rows, :].astype(BF16)

    for i, (low, high) in enumerate(bounds):

        @pl.when((step >= low) & (step < high))
        def _(i=i):
            write(operands[2 * i], operands[2 * i + 1])


def wide_rows_dot(at, rows, pairs, extra=None, parts=None):
    in_specs, args, bounds, done = [], [], [], 0
    wide = min(min(1024, grad.shape[-1]) for _, grad in pairs)
    for left, grad in pairs:
        depth = left.shape[1]
        count = grad.shape[0] if grad.ndim == 3 else grad.shape[1] // wide
        in_specs.append(pl.BlockSpec((rows, depth), lambda j: (at, 0)))

        def clip(j, done=done, count=count):
            return jnp.clip(j - done, 0, count - 1)

        if grad.ndim == 3:
            in_specs.append(pl.BlockSpec((1, depth, wide), lambda j, clip=clip: (clip(j), 0, 0)))
        else:
            in_specs.append(pl.BlockSpec((depth, wide), lambda j, clip=clip: (0, clip(j))))
        args += [left, grad]
        bounds.append((done, done + count))
        done += count
    spec = pl.BlockSpec((rows, wide), lambda j: (0, j))
    columns = done * wide
    if parts is None:
        out_specs, out_shape = spec, jax.ShapeDtypeStruct((rows, columns), BF16)
    else:
        in_specs.append(spec)
        args.append(extra)
        out_specs = [pl.BlockSpec((count, wide), lambda j: (0, j)) for _, count in parts]
        out_shape = [jax.ShapeDtypeStruct((count, columns), BF16) for _, count in parts]
    return pl.pallas_call(
        functools.partial(wide_kernel, bounds, parts),
        grid=(done,),
        in_specs=in_specs,
        out_specs=out_specs,
        out_shape=out_shape,
        cost_estimate=cost(),
        name="wide_rows_dot",
    )(*args)


def per_device(
    dp,
    fs,
    tokens,
    lengths,
    time_embed,
    cotangent,
    time_weight,
    attn_gain,
    attn_shift,
    qkv_weight,
    out_weight,
    mlp_gain,
    mlp_shift,
    up_weight,
    up_bias,
    down_weight,
    down_bias,
):
    net = Net(dp, fs)
    length, width = tokens.shape[1:]
    tokens, cotangent = tokens.reshape(length, width), cotangent.reshape(length, width)
    order = Order()
    wide_rows, tall_rows = qkv_weight.shape[0], down_weight.shape[0]
    te_rows = time_weight.shape[0]
    heads = width // HD
    half = width // 2
    with jax.named_scope("small_gather"):
        small = SmallGather(
            net,
            time_weight,
            [attn_gain, attn_shift, mlp_gain, mlp_shift, down_bias, up_bias],
            time_embed,
        )
    order.note(small.packed)
    with jax.named_scope("attn_gather"):
        attn_net = Gather(net, jnp.concatenate([qkv_weight, out_weight], axis=1))
        attn_net.along(order(attn_net.own))
    up_net = Gather(net, up_weight)
    down_net = Gather(net, down_weight)
    residual = tokens.astype(F32)
    normed_one, inverse_one = normalize(residual)
    up_net.own, down_net.own = order(inverse_one, up_net.own, down_net.own)[1:]
    with jax.named_scope("small_gather"):
        small.across(order)
    with jax.named_scope("attn_gather"):
        attn_net.join_line(order)
        order.note(attn_net.line)
        attn_net.across()
    with jax.named_scope("small_gather"):
        small.other(order)
    with jax.named_scope("up_gather"):
        up_net.along(order(up_net.own))
    with jax.named_scope("small_gather"):
        (
            time_scale,
            embeds,
            gain_one,
            shift_one,
            gain_two,
            shift_two,
            down_bias_full,
            up_bias_full,
        ) = small.finish(order, time_embed)

    place = relative_order(net, wide_rows, width)
    permute = (jnp.arange(width, dtype=jnp.int32)[:, None] == place[None, :]).astype(BF16)

    def turn(values_in):
        return back_dot(permute, values_in).astype(BF16)

    key_mask = jnp.arange(length, dtype=jnp.int32)[:, None] < lengths[None, :]
    affine_one = normed_one * gain_one + shift_one
    attn_in = (affine_one * time_scale).astype(BF16)
    cosine, sine = rotary_tables(length)
    order.note(attn_in, cosine, sine)
    turned_one = order.note(turn(order(attn_in)))
    with jax.named_scope("up_gather"):
        up_net.join_line(order)
        order.note(up_net.line)
    with jax.named_scope("attn_gather"):
        attn_net.join_across(order)
        attn_net.corners()
    with jax.named_scope("down_gather"):
        down_net.along(order(down_net.own))
    with jax.named_scope("attn_gather"):
        plan, pieces = attn_net.finish(order)
    with jax.named_scope("up_gather"):
        up_net.line = order(up_net.line)
        up_net.across()
    qkv, qkv_full, out_full = qkv_rotated(net, attn_in, plan, pieces, wide_rows, cosine, sine)
    order.note(qkv)
    pairs = heads // 2
    part = pairs // 2
    with jax.named_scope("down_gather"):
        down_net.join_line(order)
        order.note(down_net.line)
    with jax.named_scope("up_gather"):
        up_net.join_across(order)
        up_net.corners()
    context = order.note(attend(lengths, order(qkv), 0, pairs))
    with jax.named_scope("up_gather"):
        plan, pieces = up_net.finish(order)
    with jax.named_scope("down_gather"):
        down_net.line = order(down_net.line)
        down_net.across()
    context = order(context)
    hidden = residual + jnp.dot(context, out_full, preferred_element_type=F32)
    normed_two, inverse_two = normalize(hidden)
    affine_two = normed_two * gain_two + shift_two
    mlp_in = (affine_two * time_scale).astype(BF16)
    order.note(mlp_in)
    turned_ctx = order.note(turn(order(context)))
    active, slope, up_full = up_gelu(
        net, order(mlp_in), plan, pieces, wide_rows, up_bias_full
    )
    order.note(active)
    with jax.named_scope("down_gather"):
        down_net.join_across(order)
        down_net.corners()

    grad_out = cotangent.astype(F32) * key_mask.astype(F32)
    grad_branch = grad_out.astype(BF16)
    with jax.named_scope("down_grad"):
        tall = order.note(tall_rows_dot(order(active), grad_branch))
        down_mine = lax.psum_scatter(tall, "fsdp", scatter_dimension=0, tiled=True)
    down_bias_grad = jnp.sum(grad_branch.astype(F32), axis=0, keepdims=True)
    turned_two = order.note(turn(order(mlp_in)))
    with jax.named_scope("down_gather"):
        plan, pieces = down_net.finish(order)
    grad_pre, up_bias_grad, down_full = down_back(
        net, order(grad_branch), plan, pieces, tall_rows, slope
    )
    grad_pre = order(order.note(grad_pre))
    grad_mlp_in = back_dot(grad_pre, up_full)
    grad_affine_two = grad_mlp_in * time_scale
    grad_scale = jnp.sum(grad_mlp_in * affine_two, axis=0, keepdims=True)
    mlp_gain_grad = jnp.sum(grad_affine_two * normed_two, axis=0, keepdims=True)
    mlp_shift_grad = jnp.sum(grad_affine_two, axis=0, keepdims=True)
    grad_hidden = grad_out + norm_back(grad_affine_two * gain_two, normed_two, inverse_two)
    grad_attn = order.note(grad_hidden.astype(BF16))
    wide_half = wide_rows // 2
    wide_parts = kept_parts(net.yn, wide_half)
    up_red, low_red, high_red = Scatter(net), Scatter(net), Scatter(net)
    up_pairs = [(turned_two, grad_pre), (turned_ctx, grad_attn)]
    with jax.named_scope("up_grad"):
        order(grad_pre)
        up_red.core(order.note(wide_rows_dot(1, half, up_pairs)))
    grad_context = order.note(back_dot(order(grad_attn), out_full).astype(BF16))
    with jax.named_scope("up_grad"):
        sent = up_red.join_core(order)
        kept = wide_rows_dot(0, half, up_pairs, sent, wide_parts)
        order.note(kept[0])
        up_red.corners(*kept)
    low = attend_back(lengths, qkv, order(grad_context), cosine, sine, 0, part)
    order.note(low)
    with jax.named_scope("qkv_grad"):
        low_red.core(order.note(wide_rows_dot(1, half, [(turned_one, order(low))])))
    with jax.named_scope("up_grad"):
        up_red.across(order)
    high = attend_back(lengths, qkv, order(grad_context), cosine, sine, part, pairs - part)
    order.note(high)
    with jax.named_scope("qkv_grad"):
        sent = low_red.join_core(order)
        kept = wide_rows_dot(0, half, [(turned_one, low)], sent, wide_parts)
        order.note(kept[0])
        low_red.corners(*kept)
        high_red.core(order.note(wide_rows_dot(1, half, [(turned_one, order(high))])))
    grad_qkv = jnp.concatenate([item for i in range(3) for item in (low[i], high[i])], axis=1)
    grad_attn_in = back_dot(order(grad_qkv), qkv_full)
    grad_affine_one = grad_attn_in * time_scale
    grad_scale = grad_scale + jnp.sum(grad_attn_in * affine_one, axis=0, keepdims=True)
    attn_gain_grad = jnp.sum(grad_affine_one * normed_one, axis=0, keepdims=True)
    attn_shift_grad = jnp.sum(grad_affine_one, axis=0, keepdims=True)
    token_grad = (
        grad_hidden + norm_back(grad_affine_one * gain_one, normed_one, inverse_one)
    ).astype(BF16)
    order.note(token_grad, grad_scale)
    with jax.named_scope("qkv_grad"):
        sent = high_red.join_core(order)
        kept = wide_rows_dot(0, half, [(turned_one, high)], sent, wide_parts)
        order.note(kept[0])
        high_red.corners(*kept)
    with jax.named_scope("small_sums"):
        sums = jnp.concatenate(
            [
                attn_gain_grad,
                attn_shift_grad,
                mlp_gain_grad,
                mlp_shift_grad,
                down_bias_grad,
                up_bias_grad.reshape(-1, width),
            ],
            axis=0,
        )
        count = sums.shape[0]
        spots = jnp.arange(fs, dtype=jnp.int32)[:, None] == net.me
        packed = jnp.concatenate([sums, jnp.where(spots, grad_scale, 0.0)], axis=0)
        moved = net.c(packed)
    with jax.named_scope("up_grad"):
        up_line = Line(net, wide_half, [up_red.group(order)])
        order.note(up_line.kept)
    with jax.named_scope("qkv_grad"):
        low_red.across(order)
        high_red.across(order)
    branch_out = jnp.dot(order(active), down_full, preferred_element_type=F32) + down_bias_full
    layer_out = (hidden + branch_out).astype(BF16)
    order.note(layer_out)
    with jax.named_scope("small_sums"):
        packed = packed + order(moved)
        order.note(packed)
        moved = [net.y(packed, s) for s in range(1, net.yn)]
    with jax.named_scope("up_grad"):
        up_line.nearer(order)
        order.note(up_line.here)
    with jax.named_scope("small_sums"):
        for item in moved:
            packed = packed + order(item)
        order.note(packed)
        moved = [net.z(packed, k) for k in range(1, ZN)]
    with jax.named_scope("qkv_grad"):
        qkv_line = Line(net, wide_half, [low_red.group(order), high_red.group(order)])
        order.note(qkv_line.kept)
    with jax.named_scope("down_grad"):
        down_mine = order(down_mine)
        if dp > 2:
            down_weight_grad = lax.psum(down_mine, "dp").astype(F32)
        else:
            down_other = net.x(down_mine)
    with jax.named_scope("up_grad"):
        up_line.last(order)
    with jax.named_scope("qkv_grad"):
        qkv_line.nearer(order)
    with jax.named_scope("small_sums"):
        for item in order(*moved):
            packed = packed + item
        mine = lax.dynamic_slice_in_dim(embeds, net.me * te_rows, te_rows, 1)
        time_part = lax.dot_general(
            mine,
            packed[count:],
            (((0,), (0,)), ((), ())),
            precision=lax.Precision.HIGHEST,
            preferred_element_type=F32,
        )
        each = attn_gain.shape[0]
        vector_part = lax.dynamic_slice_in_dim(packed[:5], net.me * each, each, 1)
        bias_part = lax.dynamic_slice_in_dim(
            packed[5:count].reshape(1, -1), net.me * up_bias.shape[0], up_bias.shape[0], 1
        )
        packed = jnp.concatenate(
            [
                time_part,
                jnp.pad(vector_part, ((0, 0), (0, width - each))),
                jnp.pad(bias_part, ((0, 0), (0, width - up_bias.shape[0]))),
            ],
            axis=0,
        )
        if dp > 2:
            packed = lax.psum(packed, "dp")
        else:
            packed = packed + net.x(packed)
        time_weight_grad = packed[:te_rows]
        vector_grads = [packed[te_rows + i, :each] for i in range(5)]
        up_bias_out = packed[te_rows + 5, : up_bias.shape[0]]
    with jax.named_scope("qkv_grad"):
        qkv_line.last(order)
        whole = qkv_line.finish(order)
    with jax.named_scope("up_grad"):
        both = up_line.finish(order)
        ups = grad_pre.shape[1]
        up_weight_grad, out_weight_grad = both[:, :ups], both[:, ups:]
    if dp == 2:
        down_weight_grad = down_mine.astype(F32) + down_other.astype(F32)
    wide_low, wide_high = low.shape[2], high.shape[2]
    low_part, high_part = whole[:, : 3 * wide_low], whole[:, 3 * wide_low :]
    qkv_weight_grad = jnp.concatenate(
        [
            item
            for i in range(3)
            for item in (
                low_part[:, i * wide_low : (i + 1) * wide_low],
                high_part[:, i * wide_high : (i + 1) * wide_high],
            )
        ],
        axis=1,
    )
    return (
        layer_out[None],
        token_grad[None],
        time_weight_grad,
        vector_grads[0],
        vector_grads[1],
        qkv_weight_grad,
        out_weight_grad,
        vector_grads[2],
        vector_grads[3],
        up_weight_grad,
        up_bias_out,
        down_weight_grad,
        vector_grads[4],
    )


def solution(mesh):
    return jax.shard_map(
        functools.partial(per_device, mesh.shape["dp"], mesh.shape["fsdp"]),
        mesh=mesh,
        in_specs=(
            P(("dp", "fsdp"), None, None),
            P(("dp", "fsdp")),
            P(("dp", "fsdp"), None),
            P(("dp", "fsdp"), None, None),
            P("fsdp", None),
            P("fsdp"),
            P("fsdp"),
            P("fsdp", None),
            P("fsdp", None),
            P("fsdp"),
            P("fsdp"),
            P("fsdp", None),
            P("fsdp"),
            P("fsdp", None),
            P("fsdp"),
        ),
        out_specs=(
            P(("dp", "fsdp"), None, None),
            P(("dp", "fsdp"), None, None),
            P("fsdp", None),
            P("fsdp"),
            P("fsdp"),
            P("fsdp", None),
            P("fsdp", None),
            P("fsdp"),
            P("fsdp"),
            P("fsdp", None),
            P("fsdp"),
            P("fsdp", None),
            P("fsdp"),
        ),
        check_vma=False,
    )
```

```python
import functools
import math

import jax
import jax.numpy as jnp
from jax import lax
from jax.experimental import pallas as pl
from jax.experimental.pallas import tpu as pltpu
from jax.sharding import PartitionSpec as P

HD = 64
ZN = 4
PAIR = 128
LOG2E = math.log2(math.e)
ROOT = math.sqrt(2.0 / math.pi)
F32 = jnp.float32
BF16 = jnp.bfloat16


def normalize(values_in):
    center = values_in - jnp.mean(values_in, axis=-1, keepdims=True)
    inverse = lax.rsqrt(jnp.mean(center * center, axis=-1, keepdims=True) + 1e-05)
    return (center * inverse, inverse)


def norm_back(grad_hat, normed, inverse):
    return inverse * (
        grad_hat
        - jnp.mean(grad_hat, axis=-1, keepdims=True)
        - normed * jnp.mean(grad_hat * normed, axis=-1, keepdims=True)
    )


def rows_dot(left, right):
    return lax.dot_general(
        left, right, (((0,), (0,)), ((), ())), preferred_element_type=F32
    )


def back_dot(grad_in, weight):
    return lax.dot_general(
        grad_in, weight, (((1,), (1,)), ((), ())), preferred_element_type=F32
    )


def rotary_tables(length):
    half_size = HD // 2
    frequency = jnp.exp(
        jnp.arange(half_size, dtype=F32) * (-2.0 * math.log(10000.0) / HD)
    )
    angles = jnp.arange(length, dtype=F32)[:, None] * frequency[None, :]
    angles = jnp.concatenate([angles] * (PAIR // half_size), axis=-1)
    return (jnp.cos(angles), jnp.sin(angles))


class Order:
    def __init__(self):
        self.mark = ()

    def __call__(self, *arrays):
        out = lax.optimization_barrier((*arrays, *self.mark))[: len(arrays)]
        self.mark = (out[0],)
        return out[0] if len(out) == 1 else out

    def note(self, *arrays):
        self.mark = arrays
        return arrays[0] if len(arrays) == 1 else arrays


def scoped(name):
    def wrap(function):
        @functools.wraps(function)
        def inner(*args, **kwargs):
            with jax.named_scope(name):
                return function(*args, **kwargs)

        return inner

    return wrap


class Net:
    def __init__(self, dp, fs):
        self.dp, self.fs = dp, fs
        self.yn = fs // (2 * ZN)
        index = lax.axis_index("fsdp")
        self.me = index
        self.z0 = index // (2 * self.yn)
        self.y0 = (index // 2) % self.yn
        self.c0 = index % 2
        self.p0 = lax.axis_index("dp") % 2

    def perm(self, values_in, zx, dy, dc):
        pairs = []
        for i in range(self.fs):
            z, y, c = i // (2 * self.yn), (i // 2) % self.yn, i % 2
            to = ((z ^ zx) * self.yn + (y + dy) % self.yn) * 2 + (c ^ dc)
            pairs.append((i, to))
        return lax.ppermute(values_in, "fsdp", pairs)

    @scoped("z_hop")
    def z(self, values_in, k):
        return self.perm(values_in, k, 0, 0)

    @scoped("y_hop")
    def y(self, values_in, s):
        return self.perm(values_in, 0, s, 0)

    @scoped("core_hop")
    def c(self, values_in):
        return self.perm(values_in, 0, 0, 1)

    @scoped("x_hop")
    def x(self, values_in):
        return lax.ppermute(values_in, "dp", [(i, i ^ 1) for i in range(self.dp)])


def stack_kernel(*refs):
    at = 0
    for item in refs[:-1]:
        rows = item.shape[0]
        refs[-1][at : at + rows, :] = item[...]
        at += rows


def stack_rows(*items):
    rows = sum(item.shape[0] for item in items)
    return pl.pallas_call(
        stack_kernel,
        out_shape=jax.ShapeDtypeStruct((rows, items[0].shape[1]), items[0].dtype),
        cost_estimate=cost(2.0),
        name="stack_rows",
    )(*items)


class Gather:
    def __init__(self, net, shard):
        self.net = net
        self.rows, self.columns = shard.shape
        self.half = self.rows // 2
        self.own = lax.dynamic_slice_in_dim(shard, net.p0 * self.half, self.half, 0)

    def along(self, own):
        self.own = own
        self.parts = [self.net.z(own, k) for k in range(1, ZN)]

    def join_line(self, order):
        self.line = stack_rows(*order(self.own, *self.parts))

    def across(self):
        net = self.net
        self.over = net.x(self.line)
        self.beside = [net.y(self.line, s) for s in range(1, net.yn)]

    def join_across(self, order):
        self.over, *self.beside = order(self.over, *self.beside)

    def corners(self):
        net = self.net
        mid = (ZN // 2) * self.half
        self.corner_one = [net.x(item[:mid]) for item in self.beside]
        self.corner_two = [net.y(self.over[mid:], s) for s in range(1, net.yn)]
        self.pieces = [self.line, self.over] + self.beside
        self.plan = [(0, 0, 0, ZN), (0, 1, 0, ZN)]
        self.plan += [(s, 0, 0, ZN) for s in range(1, net.yn)]
        self.moved = [net.c(item) for item in self.pieces]

    def finish(self, order):
        net = self.net
        late = order(*self.corner_one, *self.corner_two)
        plan = [(s, 1, 0, ZN // 2) for s in range(1, net.yn)]
        plan += [(s, 1, ZN // 2, ZN - ZN // 2) for s in range(1, net.yn)]
        pieces = self.pieces + list(late) + self.moved + [net.c(item) for item in late]
        plan = self.plan + plan
        full = [(s, q, side, first, count) for side in range(2) for s, q, first, count in plan]
        return full, pieces


def piece_spots(plan, where_ref, rows, half, yn):
    z0, y0, c0, p0 = where_ref[0], where_ref[1], where_ref[2], where_ref[3]
    spots = []
    for i, (s, q, side, first, count) in enumerate(plan):
        y = lax.rem(y0 + yn - s, yn)
        p = lax.rem(p0 + q, 2)
        c = lax.rem(c0 + side, 2)
        for k in range(count):
            z = lax.bitwise_xor(z0, jnp.int32(first + k))
            start = pl.multiple_of(((z * yn + y) * 2 + c) * rows + p * half, half)
            spots.append((i, k * half, first + k, start))
    return spots


def pack_kernel(*refs):
    time_ref, vectors, out_ref = refs[0], refs[1:-1], refs[-1]
    out_ref[...] = jnp.zeros_like(out_ref)
    rows = time_ref.shape[0]
    out_ref[:rows, :] = time_ref[...]
    for i, item in enumerate(vectors):
        out_ref[rows + i : rows + i + 1, : item.shape[1]] = item[...]


def small_kernel(rows, te_rows, sizes, yn, where_ref, embed_ref, own_ref, other_ref, *refs):
    scale_ref, all_ref, outs, held, sems = refs[0], refs[1], refs[2:-2], refs[-2], refs[-1]
    z0, y0, c0 = where_ref[0], where_ref[1], where_ref[2]
    copies = []
    for side, piece_ref in enumerate((own_ref, other_ref)):
        c = lax.rem(c0 + side, 2)
        for s in range(yn):
            y = lax.rem(y0 + yn - s, yn)
            for k in range(ZN):
                z = lax.bitwise_xor(z0, jnp.int32(k))
                copies.append(
                    pltpu.make_async_copy(
                        piece_ref.at[s * ZN + k],
                        held.at[(z * yn + y) * 2 + c],
                        sems.at[len(copies)],
                    )
                )
    for copy in copies:
        copy.start()
    for copy in copies:
        copy.wait()
    fs = held.shape[0]
    scale = jnp.ones_like(scale_ref)
    whole = jnp.concatenate([held[f, :te_rows, :] for f in range(fs)], axis=0)
    scale_ref[...] = scale + jnp.dot(embed_ref[...], whole, preferred_element_type=F32)
    for i, (size, out_ref) in enumerate(zip(sizes, outs)):
        pieces = [
            held[f, te_rows + i : te_rows + i + 1, :size].astype(F32) for f in range(fs)
        ]
        out_ref[...] = jnp.concatenate(pieces, axis=1)
    last, wide = te_rows + len(sizes), embed_ref.shape[1]
    all_ref[...] = jnp.concatenate(
        [held[f, last : last + 1, :wide].astype(F32) for f in range(fs)], axis=0
    )


class SmallGather:
    def __init__(self, net, time_weight, vectors, embed):
        self.net, self.sizes = net, [item.shape[0] for item in vectors]
        self.te_rows, self.width = time_weight.shape
        self.rows = self.te_rows + len(vectors) + 1
        self.rows += -self.rows % 16
        self.packed = pl.pallas_call(
            pack_kernel,
            out_shape=jax.ShapeDtypeStruct((self.rows, self.width), BF16),
            cost_estimate=cost(),
            name="pack_small",
        )(time_weight, *[item.reshape(1, -1) for item in vectors], embed)
        self.parts = [net.z(self.packed, k) for k in range(1, ZN)]

    def across(self, order):
        net = self.net
        self.line = jnp.stack(order(self.packed, *self.parts))
        self.beside = [net.y(self.line, s) for s in range(1, net.yn)]

    def other(self, order):
        self.line, *self.beside = order(self.line, *self.beside)
        self.sides = jnp.concatenate([self.line] + self.beside, axis=0)
        self.moved = self.net.c(self.sides)

    def finish(self, order, embed):
        net, fs = self.net, self.net.fs
        moved = order(self.moved)
        where = jnp.stack([net.z0, net.y0, net.c0]).astype(jnp.int32)
        shapes = [(1, self.width), (fs, embed.shape[1])]
        shapes += [(1, size * fs) for size in self.sizes]
        outs = pl.pallas_call(
            functools.partial(small_kernel, self.rows, self.te_rows, self.sizes, net.yn),
            out_shape=[jax.ShapeDtypeStruct(shape, F32) for shape in shapes],
            grid_spec=pltpu.PrefetchScalarGridSpec(
                num_scalar_prefetch=1,
                grid=(1,),
                in_specs=[pl.BlockSpec(embed.shape, lambda i, r: (0, 0))]
                + [pl.BlockSpec(memory_space=pl.ANY)] * 2,
                out_specs=[whole_spec(shape) for shape in shapes],
                scratch_shapes=[
                    pltpu.VMEM((fs, self.rows, self.width), BF16),
                    pltpu.SemaphoreType.DMA((fs,)),
                ],
            ),
            cost_estimate=cost(3.0),
            name="small_join",
        )(where, embed, self.sides, moved)
        order.note(outs[0])
        return outs


def relative_order(net, rows, total):
    half = rows // 2
    d = jnp.arange(total, dtype=jnp.int32)
    f, i = d // rows, d % rows
    z, y, c = f // (2 * net.yn), (f // 2) % net.yn, f % 2
    p, j = i // half, i % half
    c, y, p, z = c ^ net.c0, (y - net.y0) % net.yn, p ^ net.p0, z ^ net.z0
    z = 2 * (z % 2) + z // 2
    return (((c * net.yn + y) * 2 + p) * ZN + z) * half + j


def add_low(*items):
    total = items[0].astype(F32)
    for item in items[1:]:
        total = total + item.astype(F32)
    return total.astype(BF16)


def sum_kernel(counts, keep, *refs):
    total = sum(counts)
    kept_ref, sent_ref = refs[total], refs[total + 1]
    at, column = 0, 0
    for count in counts:
        items = refs[at : at + count]
        at += count
        wide = items[0].shape[1]
        value = items[0][...].astype(F32)
        for item in items[1:]:
            value = value + item[...].astype(F32)
        kept_ref[:, column : column + wide] = value[:keep, :]
        sent_ref[:, column : column + wide] = value[keep:, :].astype(BF16)
        column += wide


def sum_split(groups, keep):
    rows = groups[0][0].shape[0]
    columns = sum(group[0].shape[1] for group in groups)
    return pl.pallas_call(
        functools.partial(sum_kernel, [len(group) for group in groups], keep),
        out_shape=[
            jax.ShapeDtypeStruct((keep, columns), F32),
            jax.ShapeDtypeStruct((rows - keep, columns), BF16),
        ],
        cost_estimate=cost(3.0),
        name="sum_split",
    )(*[item for group in groups for item in group])


def merge_kernel(shifts, over_ref, *refs):
    sides, came_x, came_y = (refs[i * shifts : (i + 1) * shifts] for i in range(3))
    over_out, outs = refs[3 * shifts], refs[3 * shifts + 1 :]
    half = over_ref.shape[0] // 2
    over_out[:half, :] = over_ref[:half, :]
    value = over_ref[half:, :].astype(F32)
    for item in came_y:
        value = value + item[...].astype(F32)
    over_out[half:, :] = value.astype(BF16)
    for side_ref, item, out_ref in zip(sides, came_x, outs):
        value = side_ref[:half, :].astype(F32) + item[...].astype(F32)
        out_ref[:half, :] = value.astype(BF16)
        out_ref[half:, :] = side_ref[half:, :]


def merge_corners(over, sides, came_x, came_y):
    shape = jax.ShapeDtypeStruct(over.shape, BF16)
    return pl.pallas_call(
        functools.partial(merge_kernel, len(sides)),
        out_shape=[shape] * (1 + len(sides)),
        cost_estimate=cost(2.0),
        name="merge_corners",
    )(over, *sides, *came_x, *came_y)


class Scatter:
    def __init__(self, net):
        self.net = net

    def core(self, send):
        self.sent = self.net.c(send)

    def join_core(self, order):
        self.sent = order(self.sent)
        return self.sent

    def corners(self, own, over, *rest):
        net = self.net
        self.own, self.over, self.side = own, over, list(rest[0::3])
        self.came_x = [net.x(item) for item in rest[1::3]]
        self.came_y = [net.y(item, s + 1) for s, item in enumerate(rest[2::3])]

    def across(self, order):
        net, count = self.net, len(self.side)
        came = order(*self.came_x, *self.came_y)
        self.over, *self.side = merge_corners(self.over, self.side, came[:count], came[count:])
        order.note(self.over)
        self.over = net.x(self.over)
        self.side = [net.y(item, s + 1) for s, item in enumerate(self.side)]

    def group(self, order):
        return [self.own, *order(self.over, *self.side)]


class Line:
    def __init__(self, net, half, groups):
        self.net, self.half = net, half
        self.kept, far = sum_split(groups, (ZN // 2) * half)
        self.far = net.z(far, 1)

    def nearer(self, order):
        self.here, near = sum_split([[self.kept, order(self.far)]], self.half)
        self.near = self.net.z(near, 2)

    def last(self, order):
        net = self.net
        mine = add_low(self.here, order(self.near))
        if net.dp > 2:
            groups = [list(range(q, net.dp, 2)) for q in range(2)]
            mine = lax.psum(mine, "dp", axis_index_groups=groups)
        self.mine, self.other = mine, net.x(mine)

    def finish(self, order):
        mine, other = self.mine, order(self.other)
        first = jnp.where(self.net.p0 == 0, mine, other)
        second = jnp.where(self.net.p0 == 0, other, mine)
        return jnp.concatenate([first, second], axis=0).astype(F32)


def kept_parts(yn, half):
    line = ZN * half
    spots = [(0, line), (line, line)]
    for s in range(1, yn):
        first = 2 * s * line
        spots.append((first, line))
        spots += [(first + line + i * (line // 2), line // 2) for i in range(2)]
    return spots


def cost(micros=1.0):
    return pl.CostEstimate(flops=int(micros * 9e8), bytes_accessed=int(micros * 3e6), transcendentals=0)


def weight_copies(plan, where_ref, rows, half, yn, pieces, targets, sems):
    spots = piece_spots(plan, where_ref, rows, half, yn)
    groups, count, column = [], 0, 0
    for target, first, wide in targets:
        group = []
        for i, row, shift, start in spots:
            group.append(
                pltpu.make_async_copy(
                    pieces[i].at[pl.ds(row, half), pl.ds(column, wide)],
                    target.at[pl.ds(start, half), pl.ds(first, wide)],
                    sems.at[count],
                )
            )
            count += 1
        column += wide
        groups.append(group)
    for group in groups:
        for copy in group:
            copy.start()
    return groups


def finish_copies(copies):
    for copy in copies:
        copy.wait()


def back_copy(held, out, first, wide, sem):
    spot = pl.ds(first, wide)
    copy = pltpu.make_async_copy(held.at[:, spot], out.at[:, spot], sem)
    copy.start()
    return copy


def qkv_kernel(plan, rows, half, yn, where_ref, x_ref, cos_ref, sin_ref, *refs):
    pieces = refs[: len(plan)]
    out_ref, wq_ref, wo_ref, wq, wo, low, sems, back_sems = refs[len(plan) :]
    wide = wo.shape[1]
    targets = [(wq, part * wide, wide) for part in range(3)] + [(wo, 0, wide)]
    groups = weight_copies(plan, where_ref, rows, half, yn, pieces, targets, sems)
    cosine, sine = cos_ref[...], sin_ref[...]
    front = lax.broadcasted_iota(jnp.int32, cosine.shape, 1) % HD < HD // 2
    backs = []
    for part in range(3):
        finish_copies(groups[part])
        backs.append(back_copy(wq, wq_ref, part * wide, wide, back_sems.at[part]))
        for j in range(wide // (2 * PAIR)):
            first = part * wide + j * 2 * PAIR
            acc = jnp.dot(
                x_ref[...], wq[:, first : first + 2 * PAIR], preferred_element_type=F32
            )
            for i in range(2):
                piece = acc[:, i * PAIR : (i + 1) * PAIR]
                if part < 2:
                    turned = jnp.where(
                        front,
                        -pltpu.roll(piece, PAIR - HD // 2, 1),
                        pltpu.roll(piece, HD // 2, 1),
                    )
                    piece = piece * cosine + turned * sine
                low[:, first + i * PAIR : first + (i + 1) * PAIR] = piece.astype(BF16)
        backs.append(back_copy(low, out_ref, part * wide, wide, back_sems.at[4 + part]))
    finish_copies(groups[3])
    backs.append(back_copy(wo, wo_ref, 0, wide, back_sems.at[3]))
    finish_copies(backs)


def attn_in_kernel(low_ref, high_ref, w_ref, out_ref):
    wide = low_ref.shape[2]
    acc = back_dot(low_ref[0], w_ref[:, :wide]) + back_dot(high_ref[0], w_ref[:, wide:])
    step = pl.program_id(0)

    @pl.when(step == 0)
    def _():
        out_ref[...] = acc

    @pl.when(step > 0)
    def _():
        out_ref[...] = out_ref[...] + acc


def attn_in_back(low, high, w):
    parts, tokens, wide = low.shape
    depth = w.shape[0]
    half = pl.BlockSpec((1, tokens, wide), lambda i: (i, 0, 0))
    return pl.pallas_call(
        attn_in_kernel,
        grid=(parts,),
        in_specs=[half, half, pl.BlockSpec((depth, 2 * wide), lambda i: (0, i))],
        out_specs=pl.BlockSpec((tokens, depth), lambda i: (0, 0)),
        out_shape=jax.ShapeDtypeStruct((tokens, depth), F32),
        cost_estimate=cost(5.0),
        name="attn_in_back",
    )(low, high, w)


def where_of(net):
    return jnp.stack([net.z0, net.y0, net.c0, net.p0]).astype(jnp.int32)


ANY = pl.BlockSpec(memory_space=pl.ANY)


def whole_spec(shape):
    return pl.BlockSpec(shape, lambda i, r: (0, 0))


def qkv_rotated(net, x, plan, pieces, rows, cosine, sine):
    tokens, depth = x.shape
    total = net.fs * rows
    blocks = sum(entry[4] for entry in plan)
    half = rows // 2
    return pl.pallas_call(
        functools.partial(qkv_kernel, plan, rows, half, net.yn),
        grid_spec=pltpu.PrefetchScalarGridSpec(
            num_scalar_prefetch=1,
            grid=(1,),
            in_specs=[whole_spec(x.shape), whole_spec(cosine.shape), whole_spec(sine.shape)]
            + [ANY] * len(pieces),
            out_specs=[ANY] * 3,
            scratch_shapes=[
                pltpu.VMEM((total, 3 * depth), BF16),
                pltpu.VMEM((total, depth), BF16),
                pltpu.VMEM((tokens, 3 * depth), BF16),
                pltpu.SemaphoreType.DMA((4 * blocks,)),
                pltpu.SemaphoreType.DMA((7,)),
            ],
        ),
        out_shape=[
            jax.ShapeDtypeStruct((tokens, 3 * depth), BF16),
            jax.ShapeDtypeStruct((total, 3 * depth), BF16),
            jax.ShapeDtypeStruct((total, depth), BF16),
        ],
        compiler_params=pltpu.CompilerParams(vmem_limit_bytes=32 * 2**20),
        cost_estimate=cost(10.0),
        name="qkv_rotated",
    )(where_of(net), x, cosine, sine, *pieces)


def up_kernel(plan, rows, half, yn, where_ref, x_ref, b_ref, *refs):
    pieces = refs[: len(plan)]
    act_out, slope_out, w_out, w, act, slope, sems, back_sems = refs[len(plan) :]
    total = w.shape[1]
    wide = min(1024, total)
    step = min(256, wide)
    parts = total // wide
    targets = [(w, part * wide, wide) for part in range(parts)]
    groups = weight_copies(plan, where_ref, rows, half, yn, pieces, targets, sems)
    backs = []
    for part in range(parts):
        finish_copies(groups[part])
        backs.append(back_copy(w, w_out, part * wide, wide, back_sems.at[3 * part]))
        for first in range(part * wide, (part + 1) * wide, step):
            spot = slice(first, first + step)
            v = jnp.dot(x_ref[...], w[:, spot], preferred_element_type=F32) + b_ref[:, spot]
            square = v * v
            bend = jnp.tanh(v * (ROOT + ROOT * 0.044715 * square))
            half_up = 0.5 + 0.5 * bend
            act[:, spot] = (v * half_up).astype(BF16)
            rise = 0.5 * ROOT + (1.5 * 0.044715 * ROOT) * square
            slope[:, spot] = (half_up + v * (1.0 - bend * bend) * rise).astype(BF16)
        backs.append(back_copy(act, act_out, part * wide, wide, back_sems.at[3 * part + 1]))
        backs.append(back_copy(slope, slope_out, part * wide, wide, back_sems.at[3 * part + 2]))
    finish_copies(backs)


def up_gelu(net, x, plan, pieces, rows, bias):
    tokens, depth = x.shape
    total = bias.shape[1]
    parts = total // min(1024, total)
    blocks = sum(entry[4] for entry in plan)
    return pl.pallas_call(
        functools.partial(up_kernel, plan, rows, rows // 2, net.yn),
        grid_spec=pltpu.PrefetchScalarGridSpec(
            num_scalar_prefetch=1,
            grid=(1,),
            in_specs=[whole_spec(x.shape), whole_spec(bias.shape)] + [ANY] * len(pieces),
            out_specs=[ANY] * 3,
            scratch_shapes=[
                pltpu.VMEM((depth, total), BF16),
                pltpu.VMEM((tokens, total), BF16),
                pltpu.VMEM((tokens, total), BF16),
                pltpu.SemaphoreType.DMA((parts * blocks,)),
                pltpu.SemaphoreType.DMA((3 * parts,)),
            ],
        ),
        out_shape=[
            jax.ShapeDtypeStruct((tokens, total), BF16),
            jax.ShapeDtypeStruct((tokens, total), BF16),
            jax.ShapeDtypeStruct((depth, total), BF16),
        ],
        compiler_params=pltpu.CompilerParams(vmem_limit_bytes=40 * 2**20),
        cost_estimate=cost(8.0),
        name="up_gelu",
    )(where_of(net), x, bias, *pieces)


def down_kernel(plan, rows, half, yn, where_ref, g_ref, slope_ref, *refs):
    pieces = refs[: len(plan)]
    out_ref, sum_ref, w_ref, w, slope, low, sems, slope_sems, back_sems = refs[len(plan) :]
    spots = piece_spots(plan, where_ref, rows, half, yn)
    group_rows = w.shape[0] // ZN
    step = min(256, group_rows)
    z0 = where_ref[0]
    groups = [[] for _ in range(ZN)]
    for count, (i, row, shift, start) in enumerate(spots):
        copy = pltpu.make_async_copy(
            pieces[i].at[pl.ds(row, half), :], w.at[pl.ds(start, half), :], sems.at[count]
        )
        groups[shift].append(copy)
    slopes = []
    for k in range(ZN):
        at = pl.multiple_of(lax.bitwise_xor(z0, jnp.int32(k)) * group_rows, group_rows)
        for copy in groups[k]:
            copy.start()
        copy = pltpu.make_async_copy(
            slope_ref.at[:, pl.ds(at, group_rows)], slope.at[k], slope_sems.at[k]
        )
        copy.start()
        slopes.append(copy)
    backs = []
    for k in range(ZN):
        at = pl.multiple_of(lax.bitwise_xor(z0, jnp.int32(k)) * group_rows, group_rows)
        finish_copies(groups[k])
        slopes[k].wait()
        here = pl.ds(at, group_rows)
        copy = pltpu.make_async_copy(w.at[here, :], w_ref.at[here, :], back_sems.at[2 * k])
        copy.start()
        backs.append(copy)
        for j in range(group_rows // step):
            spot = slice(j * step, (j + 1) * step)
            inner = pl.multiple_of(at + j * step, step)
            acc = lax.dot_general(
                g_ref[...],
                w[pl.ds(inner, step), :],
                (((1,), (1,)), ((), ())),
                preferred_element_type=F32,
            )
            rounded = (acc * slope[k, :, spot].astype(F32)).astype(BF16)
            low[k, :, spot] = rounded
            sum_ref[:, pl.ds(inner, step)] = jnp.sum(
                rounded.astype(F32), axis=0, keepdims=True
            )
        copy = pltpu.make_async_copy(low.at[k], out_ref.at[:, here], back_sems.at[2 * k + 1])
        copy.start()
        backs.append(copy)
    finish_copies(backs)


def down_back(net, grad, plan, pieces, rows, slope):
    tokens, depth = grad.shape
    total = slope.shape[1]
    blocks = sum(entry[4] for entry in plan)
    return pl.pallas_call(
        functools.partial(down_kernel, plan, rows, rows // 2, net.yn),
        grid_spec=pltpu.PrefetchScalarGridSpec(
            num_scalar_prefetch=1,
            grid=(1,),
            in_specs=[whole_spec(grad.shape), ANY] + [ANY] * len(pieces),
            out_specs=[ANY, pl.BlockSpec((1, total), lambda i, r: (0, 0)), ANY],
            scratch_shapes=[
                pltpu.VMEM((total, depth), BF16),
                pltpu.VMEM((ZN, tokens, total // ZN), BF16),
                pltpu.VMEM((ZN, tokens, total // ZN), BF16),
                pltpu.SemaphoreType.DMA((blocks,)),
                pltpu.SemaphoreType.DMA((ZN,)),
                pltpu.SemaphoreType.DMA((2 * ZN,)),
            ],
        ),
        out_shape=[
            jax.ShapeDtypeStruct((tokens, total), BF16),
            jax.ShapeDtypeStruct((1, total), F32),
            jax.ShapeDtypeStruct((total, depth), BF16),
        ],
        compiler_params=pltpu.CompilerParams(vmem_limit_bytes=40 * 2**20),
        cost_estimate=cost(10.0),
        name="down_back",
    )(where_of(net), grad, slope, *pieces)


def attend_kernel(len_ref, q_ref, k_ref, v_ref, out_ref):
    q, k, v = q_ref[...], k_ref[...], v_ref[...]
    length = k.shape[0]
    first = lax.broadcasted_iota(jnp.int32, q.shape, 1) < HD
    valid = lax.broadcasted_iota(jnp.int32, (1, length), 1) < len_ref[0]
    zero = jnp.zeros_like(q)
    outs = []
    for h in range(2):
        one = jnp.where(first, q, zero) if h == 0 else jnp.where(first, zero, q)
        scores = lax.dot_general(
            one, k, (((1,), (1,)), ((), ())), preferred_element_type=F32
        )
        scores = jnp.where(valid, scores * HD**-0.5, -1000000000.0)
        top = jnp.max(scores, axis=1, keepdims=True)
        exponent = jnp.exp2((scores - top) * LOG2E)
        total = jnp.sum(exponent, axis=1, keepdims=True)
        mixed = jnp.dot(exponent.astype(BF16), v, preferred_element_type=F32)
        outs.append(mixed * (1.0 / total))
    out_ref[...] = jnp.where(first, outs[0], outs[1]).astype(BF16)


def attend(length, qkv, first_pair, pairs):
    rows, total = qkv.shape
    count = total // 3 // PAIR

    def pick(part):
        return pl.BlockSpec((rows, PAIR), lambda j, r: (0, part * count + first_pair + j))

    return pl.pallas_call(
        attend_kernel,
        grid_spec=pltpu.PrefetchScalarGridSpec(
            num_scalar_prefetch=1,
            grid=(pairs,),
            in_specs=[pick(0), pick(1), pick(2)],
            out_specs=pl.BlockSpec((rows, PAIR), lambda j, r: (0, j)),
        ),
        out_shape=jax.ShapeDtypeStruct((rows, pairs * PAIR), BF16),
        cost_estimate=cost(1.4 * pairs),
        name="attend",
    )(length, qkv, qkv, qkv)


def attend_back_kernel(len_ref, q_ref, k_ref, v_ref, g_ref, cos_ref, sin_ref, out_ref):
    q, k, v, g = q_ref[...], k_ref[...], v_ref[...], g_ref[...]
    length = k.shape[0]
    lane = lax.broadcasted_iota(jnp.int32, q.shape, 1)
    first = lane < HD
    valid = lax.broadcasted_iota(jnp.int32, (length, length), 0) < len_ref[0]
    zero = jnp.zeros_like(q)
    grads = []
    for h in range(2):
        key = jnp.where(first, k, zero) if h == 0 else jnp.where(first, zero, k)
        value = jnp.where(first, v, zero) if h == 0 else jnp.where(first, zero, v)
        scores = lax.dot_general(
            key, q, (((1,), (1,)), ((), ())), preferred_element_type=F32
        )
        scores = jnp.where(valid, scores * HD**-0.5, -1000000000.0)
        top = jnp.max(scores, axis=0, keepdims=True)
        exponent = jnp.exp2((scores - top) * LOG2E)
        total = jnp.sum(exponent, axis=0, keepdims=True)
        probs = exponent * (1.0 / total)
        grad_probs = lax.dot_general(
            value, g, (((1,), (1,)), ((), ())), preferred_element_type=F32
        )
        delta = jnp.sum(grad_probs * probs, axis=0, keepdims=True)
        grad_scores = (probs * (grad_probs - delta)).astype(BF16)
        grads.append(
            (
                lax.dot_general(
                    grad_scores, k, (((0,), (0,)), ((), ())), preferred_element_type=F32
                ),
                jnp.dot(grad_scores, q, preferred_element_type=F32),
                jnp.dot(probs.astype(BF16), g, preferred_element_type=F32),
            )
        )
    front = lane % HD < HD // 2
    cosine, sine = cos_ref[...] * HD**-0.5, sin_ref[...] * HD**-0.5
    for i in range(2):
        grad = jnp.where(first, grads[0][i], grads[1][i])
        sined = grad * sine
        turned = jnp.where(
            front, pltpu.roll(sined, PAIR - HD // 2, 1), -pltpu.roll(sined, HD // 2, 1)
        )
        out_ref[i] = (grad * cosine + turned).astype(BF16)
    out_ref[2] = jnp.where(first, grads[0][2], grads[1][2]).astype(BF16)


def attend_back(length, qkv, grad, cosine, sine, first_pair, pairs):
    rows, total = qkv.shape
    count = total // 3 // PAIR

    def pick(part):
        return pl.BlockSpec((rows, PAIR), lambda j, r: (0, part * count + first_pair + j))

    table = pl.BlockSpec((rows, PAIR), lambda j, r: (0, 0))
    return pl.pallas_call(
        attend_back_kernel,
        grid_spec=pltpu.PrefetchScalarGridSpec(
            num_scalar_prefetch=1,
            grid=(pairs,),
            in_specs=[pick(0), pick(1), pick(2), pick(0), table, table],
            out_specs=pl.BlockSpec((3, rows, PAIR), lambda j, r: (0, 0, j)),
        ),
        out_shape=jax.ShapeDtypeStruct((3, rows, pairs * PAIR), BF16),
        cost_estimate=cost(3.0 * pairs),
        name="attend_back",
    )(length, qkv, qkv, qkv, grad, cosine, sine)


def tall_kernel(left_ref, grad_ref, out_ref):
    out_ref[...] = lax.dot_general(
        left_ref[...], grad_ref[...], (((0,), (0,)), ((), ())), preferred_element_type=F32
    ).astype(BF16)


def tall_rows_dot(left, grad):
    depth, columns = grad.shape
    total = left.shape[1]
    tall = min(1024, total)
    return pl.pallas_call(
        tall_kernel,
        grid=(total // tall,),
        in_specs=[
            pl.BlockSpec((depth, tall), lambda i: (0, i)),
            pl.BlockSpec((depth, columns), lambda i: (0, 0)),
        ],
        out_specs=pl.BlockSpec((tall, columns), lambda i: (i, 0)),
        out_shape=jax.ShapeDtypeStruct((total, columns), BF16),
        cost_estimate=cost(9.0),
        name="tall_rows_dot",
    )(left, grad)


def wide_kernel(bounds, parts, *refs):
    step = pl.program_id(0)
    operands, rest = refs[: 2 * len(bounds)], refs[2 * len(bounds) :]

    def write(left_ref, grad_ref):
        grad = grad_ref[0] if len(grad_ref.shape) == 3 else grad_ref[...]
        acc = jnp.dot(left_ref[...], grad, preferred_element_type=F32)
        if parts is None:
            rest[-1][...] = acc.astype(BF16)
            return
        acc = acc + rest[0][...].astype(F32)
        for (first, rows), out_ref in zip(parts, rest[1:]):
            out_ref[...] = acc[first : first + rows, :].astype(BF16)

    for i, (low, high) in enumerate(bounds):

        @pl.when((step >= low) & (step < high))
        def _(i=i):
            write(operands[2 * i], operands[2 * i + 1])


def wide_rows_dot(at, rows, pairs, extra=None, parts=None):
    in_specs, args, bounds, done = [], [], [], 0
    wide = min(min(1024, grad.shape[-1]) for _, grad in pairs)
    for left, grad in pairs:
        depth = left.shape[1]
        count = grad.shape[0] if grad.ndim == 3 else grad.shape[1] // wide
        in_specs.append(pl.BlockSpec((rows, depth), lambda j: (at, 0)))

        def clip(j, done=done, count=count):
            return jnp.clip(j - done, 0, count - 1)

        if grad.ndim == 3:
            in_specs.append(pl.BlockSpec((1, depth, wide), lambda j, clip=clip: (clip(j), 0, 0)))
        else:
            in_specs.append(pl.BlockSpec((depth, wide), lambda j, clip=clip: (0, clip(j))))
        args += [left, grad]
        bounds.append((done, done + count))
        done += count
    spec = pl.BlockSpec((rows, wide), lambda j: (0, j))
    columns = done * wide
    if parts is None:
        out_specs, out_shape = spec, jax.ShapeDtypeStruct((rows, columns), BF16)
    else:
        in_specs.append(spec)
        args.append(extra)
        out_specs = [pl.BlockSpec((count, wide), lambda j: (0, j)) for _, count in parts]
        out_shape = [jax.ShapeDtypeStruct((count, columns), BF16) for _, count in parts]
    return pl.pallas_call(
        functools.partial(wide_kernel, bounds, parts),
        grid=(done,),
        in_specs=in_specs,
        out_specs=out_specs,
        out_shape=out_shape,
        cost_estimate=cost(1.5 * done),
        name="wide_rows_dot",
    )(*args)


def per_device(
    dp,
    fs,
    tokens,
    lengths,
    time_embed,
    cotangent,
    time_weight,
    attn_gain,
    attn_shift,
    qkv_weight,
    out_weight,
    mlp_gain,
    mlp_shift,
    up_weight,
    up_bias,
    down_weight,
    down_bias,
):
    net = Net(dp, fs)
    length, width = tokens.shape[1:]
    tokens, cotangent = tokens.reshape(length, width), cotangent.reshape(length, width)
    order = Order()
    wide_rows, tall_rows = qkv_weight.shape[0], down_weight.shape[0]
    te_rows = time_weight.shape[0]
    heads = width // HD
    half = width // 2
    with jax.named_scope("small_gather"):
        small = SmallGather(
            net,
            time_weight,
            [attn_gain, attn_shift, mlp_gain, mlp_shift, down_bias, up_bias],
            time_embed,
        )
    order.note(small.packed)
    with jax.named_scope("attn_gather"):
        attn_net = Gather(net, jnp.concatenate([qkv_weight, out_weight], axis=1))
        attn_net.along(order(attn_net.own))
    up_net = Gather(net, up_weight)
    down_net = Gather(net, down_weight)
    residual = tokens.astype(F32)
    normed_one, inverse_one = normalize(residual)
    up_net.own, down_net.own = order(inverse_one, up_net.own, down_net.own)[1:]
    with jax.named_scope("small_gather"):
        small.across(order)
    with jax.named_scope("small_gather"):
        small.other(order)
    with jax.named_scope("attn_gather"):
        attn_net.join_line(order)
        order.note(attn_net.line)
        attn_net.across()
    with jax.named_scope("up_gather"):
        up_net.along(order(up_net.own))
    with jax.named_scope("small_gather"):
        (
            time_scale,
            embeds,
            gain_one,
            shift_one,
            gain_two,
            shift_two,
            down_bias_full,
            up_bias_full,
        ) = small.finish(order, time_embed)

    place = relative_order(net, wide_rows, width)
    permute = (jnp.arange(width, dtype=jnp.int32)[:, None] == place[None, :]).astype(BF16)

    def turn(values_in):
        return back_dot(permute, values_in).astype(BF16)

    key_mask = jnp.arange(length, dtype=jnp.int32)[:, None] < lengths[None, :]
    affine_one = normed_one * gain_one + shift_one
    attn_in = (affine_one * time_scale).astype(BF16)
    cosine, sine = rotary_tables(length)
    order.note(attn_in, cosine, sine)
    turned_one = order.note(turn(order(attn_in)))
    with jax.named_scope("up_gather"):
        up_net.join_line(order)
        order.note(up_net.line)
    with jax.named_scope("attn_gather"):
        attn_net.join_across(order)
        attn_net.corners()
    with jax.named_scope("down_gather"):
        down_net.along(order(down_net.own))
    with jax.named_scope("attn_gather"):
        plan, pieces = attn_net.finish(order)
    with jax.named_scope("up_gather"):
        up_net.line = order(up_net.line)
        up_net.across()
    qkv, qkv_full, out_full = qkv_rotated(net, attn_in, plan, pieces, wide_rows, cosine, sine)
    order.note(qkv)
    pairs = heads // 2
    part = pairs // 2
    with jax.named_scope("down_gather"):
        down_net.join_line(order)
        order.note(down_net.line)
    with jax.named_scope("up_gather"):
        up_net.join_across(order)
        up_net.corners()
    context = order.note(attend(lengths, order(qkv), 0, pairs))
    with jax.named_scope("up_gather"):
        plan, pieces = up_net.finish(order)
    with jax.named_scope("down_gather"):
        down_net.line = order(down_net.line)
        down_net.across()
    context = order(context)
    hidden = residual + jnp.dot(context, out_full, preferred_element_type=F32)
    normed_two, inverse_two = normalize(hidden)
    affine_two = normed_two * gain_two + shift_two
    mlp_in = (affine_two * time_scale).astype(BF16)
    order.note(mlp_in)
    turned_ctx = order.note(turn(order(context)))
    active, slope, up_full = up_gelu(
        net, order(mlp_in), plan, pieces, wide_rows, up_bias_full
    )
    order.note(active)
    with jax.named_scope("down_gather"):
        down_net.join_across(order)
        down_net.corners()

    grad_out = cotangent.astype(F32) * key_mask.astype(F32)
    grad_branch = grad_out.astype(BF16)
    with jax.named_scope("down_grad"):
        tall = order.note(tall_rows_dot(order(active), grad_branch))
        down_mine = lax.psum_scatter(tall, "fsdp", scatter_dimension=0, tiled=True)
    down_bias_grad = jnp.sum(grad_branch.astype(F32), axis=0, keepdims=True)
    turned_two = order.note(turn(order(mlp_in)))
    with jax.named_scope("down_gather"):
        plan, pieces = down_net.finish(order)
    grad_pre, up_bias_grad, down_full = down_back(
        net, order(grad_branch), plan, pieces, tall_rows, slope
    )
    grad_pre = order(order.note(grad_pre))
    grad_mlp_in = back_dot(grad_pre, up_full)
    grad_affine_two = grad_mlp_in * time_scale
    grad_scale = jnp.sum(grad_mlp_in * affine_two, axis=0, keepdims=True)
    mlp_gain_grad = jnp.sum(grad_affine_two * normed_two, axis=0, keepdims=True)
    mlp_shift_grad = jnp.sum(grad_affine_two, axis=0, keepdims=True)
    grad_hidden = grad_out + norm_back(grad_affine_two * gain_two, normed_two, inverse_two)
    grad_attn = order.note(grad_hidden.astype(BF16))
    wide_half = wide_rows // 2
    wide_parts = kept_parts(net.yn, wide_half)
    up_red, low_red, high_red = Scatter(net), Scatter(net), Scatter(net)
    up_pairs = [(turned_two, grad_pre), (turned_ctx, grad_attn)]
    with jax.named_scope("up_grad"):
        order(grad_pre)
        up_red.core(order.note(wide_rows_dot(1, half, up_pairs)))
    grad_context = order.note(back_dot(order(grad_attn), out_full).astype(BF16))
    with jax.named_scope("up_grad"):
        sent = up_red.join_core(order)
        kept = wide_rows_dot(0, half, up_pairs, sent, wide_parts)
        order.note(kept[0])
        up_red.corners(*kept)
    low = attend_back(lengths, qkv, order(grad_context), cosine, sine, 0, part)
    order.note(low)
    with jax.named_scope("qkv_grad"):
        low_red.core(order.note(wide_rows_dot(1, half, [(turned_one, order(low))])))
    with jax.named_scope("up_grad"):
        up_red.across(order)
    high = attend_back(lengths, qkv, order(grad_context), cosine, sine, part, pairs - part)
    order.note(high)
    with jax.named_scope("qkv_grad"):
        sent = low_red.join_core(order)
        kept = wide_rows_dot(0, half, [(turned_one, low)], sent, wide_parts)
        order.note(kept[0])
        low_red.corners(*kept)
        high_red.core(order.note(wide_rows_dot(1, half, [(turned_one, order(high))])))
    grad_attn_in = attn_in_back(low, order(high), qkv_full)
    grad_affine_one = grad_attn_in * time_scale
    grad_scale = grad_scale + jnp.sum(grad_attn_in * affine_one, axis=0, keepdims=True)
    attn_gain_grad = jnp.sum(grad_affine_one * normed_one, axis=0, keepdims=True)
    attn_shift_grad = jnp.sum(grad_affine_one, axis=0, keepdims=True)
    token_grad = (
        grad_hidden + norm_back(grad_affine_one * gain_one, normed_one, inverse_one)
    ).astype(BF16)
    order.note(token_grad, grad_scale)
    with jax.named_scope("qkv_grad"):
        sent = high_red.join_core(order)
        kept = wide_rows_dot(0, half, [(turned_one, high)], sent, wide_parts)
        order.note(kept[0])
        high_red.corners(*kept)
    with jax.named_scope("small_sums"):
        sums = jnp.concatenate(
            [
                attn_gain_grad,
                attn_shift_grad,
                mlp_gain_grad,
                mlp_shift_grad,
                down_bias_grad,
                up_bias_grad.reshape(-1, width),
            ],
            axis=0,
        )
        count = sums.shape[0]
        spots = jnp.arange(fs, dtype=jnp.int32)[:, None] == net.me
        packed = jnp.concatenate([sums, jnp.where(spots, grad_scale, 0.0)], axis=0)
        moved = net.c(packed)
    with jax.named_scope("up_grad"):
        up_line = Line(net, wide_half, [up_red.group(order)])
        order.note(up_line.kept)
    with jax.named_scope("qkv_grad"):
        low_red.across(order)
        high_red.across(order)
    with jax.named_scope("down_grad"):
        down_mine = order(down_mine)
        if dp > 2:
            down_weight_grad = lax.psum(down_mine, "dp").astype(F32)
        else:
            down_other = net.x(down_mine)
    branch_out = jnp.dot(order(active), down_full, preferred_element_type=F32) + down_bias_full
    layer_out = (hidden + branch_out).astype(BF16)
    order.note(layer_out)
    with jax.named_scope("small_sums"):
        packed = packed + order(moved)
        order.note(packed)
        moved = [net.y(packed, s) for s in range(1, net.yn)]
    with jax.named_scope("up_grad"):
        up_line.nearer(order)
        order.note(up_line.here)
    with jax.named_scope("small_sums"):
        for item in moved:
            packed = packed + order(item)
        order.note(packed)
        moved = [net.z(packed, k) for k in range(1, ZN)]
    with jax.named_scope("qkv_grad"):
        qkv_line = Line(net, wide_half, [low_red.group(order), high_red.group(order)])
        order.note(qkv_line.kept)
    with jax.named_scope("up_grad"):
        up_line.last(order)
    with jax.named_scope("qkv_grad"):
        qkv_line.nearer(order)
    with jax.named_scope("small_sums"):
        for item in order(*moved):
            packed = packed + item
        mine = lax.dynamic_slice_in_dim(embeds, net.me * te_rows, te_rows, 1)
        time_part = lax.dot_general(
            mine,
            packed[count:],
            (((0,), (0,)), ((), ())),
            precision=lax.Precision.HIGHEST,
            preferred_element_type=F32,
        )
        each = attn_gain.shape[0]
        vector_part = lax.dynamic_slice_in_dim(packed[:5], net.me * each, each, 1)
        bias_part = lax.dynamic_slice_in_dim(
            packed[5:count].reshape(1, -1), net.me * up_bias.shape[0], up_bias.shape[0], 1
        )
        packed = jnp.concatenate(
            [
                time_part,
                jnp.pad(vector_part, ((0, 0), (0, width - each))),
                jnp.pad(bias_part, ((0, 0), (0, width - up_bias.shape[0]))),
            ],
            axis=0,
        )
        if dp > 2:
            packed = lax.psum(packed, "dp")
        else:
            packed = packed + net.x(packed)
        time_weight_grad = packed[:te_rows]
        vector_grads = [packed[te_rows + i, :each] for i in range(5)]
        up_bias_out = packed[te_rows + 5, : up_bias.shape[0]]
    with jax.named_scope("qkv_grad"):
        qkv_line.last(order)
        whole = qkv_line.finish(order)
    with jax.named_scope("up_grad"):
        both = up_line.finish(order)
        ups = grad_pre.shape[1]
        up_weight_grad, out_weight_grad = both[:, :ups], both[:, ups:]
    if dp == 2:
        down_weight_grad = down_mine.astype(F32) + down_other.astype(F32)
    wide_low, wide_high = low.shape[2], high.shape[2]
    low_part, high_part = whole[:, : 3 * wide_low], whole[:, 3 * wide_low :]
    qkv_weight_grad = jnp.concatenate(
        [
            item
            for i in range(3)
            for item in (
                low_part[:, i * wide_low : (i + 1) * wide_low],
                high_part[:, i * wide_high : (i + 1) * wide_high],
            )
        ],
        axis=1,
    )
    return (
        layer_out[None],
        token_grad[None],
        time_weight_grad,
        vector_grads[0],
        vector_grads[1],
        qkv_weight_grad,
        out_weight_grad,
        vector_grads[2],
        vector_grads[3],
        up_weight_grad,
        up_bias_out,
        down_weight_grad,
        vector_grads[4],
    )


def solution(mesh):
    return jax.shard_map(
        functools.partial(per_device, mesh.shape["dp"], mesh.shape["fsdp"]),
        mesh=mesh,
        in_specs=(
            P(("dp", "fsdp"), None, None),
            P(("dp", "fsdp")),
            P(("dp", "fsdp"), None),
            P(("dp", "fsdp"), None, None),
            P("fsdp", None),
            P("fsdp"),
            P("fsdp"),
            P("fsdp", None),
            P("fsdp", None),
            P("fsdp"),
            P("fsdp"),
            P("fsdp", None),
            P("fsdp"),
            P("fsdp", None),
            P("fsdp"),
        ),
        out_specs=(
            P(("dp", "fsdp"), None, None),
            P(("dp", "fsdp"), None, None),
            P("fsdp", None),
            P("fsdp"),
            P("fsdp"),
            P("fsdp", None),
            P("fsdp", None),
            P("fsdp"),
            P("fsdp"),
            P("fsdp", None),
            P("fsdp"),
            P("fsdp", None),
            P("fsdp"),
        ),
        check_vma=False,
    )
```

```python
import functools
import math

import jax
import jax.numpy as jnp
from jax import lax
from jax.experimental import pallas as pl
from jax.experimental.pallas import tpu as pltpu
from jax.sharding import PartitionSpec as P

HD = 64
ZN = 4
PAIR = 128
LOG2E = math.log2(math.e)
ROOT = math.sqrt(2.0 / math.pi)
F32 = jnp.float32
BF16 = jnp.bfloat16


def normalize(values_in):
    center = values_in - jnp.mean(values_in, axis=-1, keepdims=True)
    inverse = lax.rsqrt(jnp.mean(center * center, axis=-1, keepdims=True) + 1e-05)
    return (center * inverse, inverse)


def norm_back(grad_hat, normed, inverse):
    return inverse * (
        grad_hat
        - jnp.mean(grad_hat, axis=-1, keepdims=True)
        - normed * jnp.mean(grad_hat * normed, axis=-1, keepdims=True)
    )


def rows_dot(left, right):
    return lax.dot_general(
        left, right, (((0,), (0,)), ((), ())), preferred_element_type=F32
    )


def back_dot(grad_in, weight):
    return lax.dot_general(
        grad_in, weight, (((1,), (1,)), ((), ())), preferred_element_type=F32
    )


def rotary_tables(length):
    half_size = HD // 2
    frequency = jnp.exp(
        jnp.arange(half_size, dtype=F32) * (-2.0 * math.log(10000.0) / HD)
    )
    angles = jnp.arange(length, dtype=F32)[:, None] * frequency[None, :]
    angles = jnp.concatenate([angles] * (PAIR // half_size), axis=-1)
    return (jnp.cos(angles), jnp.sin(angles))


class Order:
    def __init__(self):
        self.mark = ()

    def __call__(self, *arrays):
        out = lax.optimization_barrier((*arrays, *self.mark))[: len(arrays)]
        self.mark = (out[0],)
        return out[0] if len(out) == 1 else out

    def note(self, *arrays):
        self.mark = arrays
        return arrays[0] if len(arrays) == 1 else arrays


def scoped(name):
    def wrap(function):
        @functools.wraps(function)
        def inner(*args, **kwargs):
            with jax.named_scope(name):
                return function(*args, **kwargs)

        return inner

    return wrap


class Net:
    def __init__(self, dp, fs):
        self.dp, self.fs = dp, fs
        self.yn = fs // (2 * ZN)
        index = lax.axis_index("fsdp")
        self.me = index
        self.z0 = index // (2 * self.yn)
        self.y0 = (index // 2) % self.yn
        self.c0 = index % 2
        self.p0 = lax.axis_index("dp") % 2

    def perm(self, values_in, zx, dy, dc):
        pairs = []
        for i in range(self.fs):
            z, y, c = i // (2 * self.yn), (i // 2) % self.yn, i % 2
            to = ((z ^ zx) * self.yn + (y + dy) % self.yn) * 2 + (c ^ dc)
            pairs.append((i, to))
        return lax.ppermute(values_in, "fsdp", pairs)

    @scoped("z_hop")
    def z(self, values_in, k):
        return self.perm(values_in, k, 0, 0)

    @scoped("y_hop")
    def y(self, values_in, s):
        return self.perm(values_in, 0, s, 0)

    @scoped("core_hop")
    def c(self, values_in):
        return self.perm(values_in, 0, 0, 1)

    @scoped("x_hop")
    def x(self, values_in):
        return lax.ppermute(values_in, "dp", [(i, i ^ 1) for i in range(self.dp)])


def stack_kernel(*refs):
    at = 0
    for item in refs[:-1]:
        rows = item.shape[0]
        refs[-1][at : at + rows, :] = item[...]
        at += rows


def stack_rows(*items):
    rows = sum(item.shape[0] for item in items)
    return pl.pallas_call(
        stack_kernel,
        out_shape=jax.ShapeDtypeStruct((rows, items[0].shape[1]), items[0].dtype),
        cost_estimate=cost(2.0),
        name="stack_rows",
    )(*items)


class Gather:
    def __init__(self, net, shard):
        self.net = net
        self.rows, self.columns = shard.shape
        self.half = self.rows // 2
        self.own = lax.dynamic_slice_in_dim(shard, net.p0 * self.half, self.half, 0)

    def along(self, own):
        self.own = own
        self.parts = [self.net.z(own, k) for k in range(1, ZN)]

    def join_line(self, order):
        self.line = stack_rows(*order(self.own, *self.parts))

    def across(self):
        net = self.net
        self.over = net.x(self.line)
        self.beside = [net.y(self.line, s) for s in range(1, net.yn)]

    def join_across(self, order):
        self.over, *self.beside = order(self.over, *self.beside)

    def corners(self):
        net = self.net
        mid = (ZN // 2) * self.half
        self.corner_one = [net.x(item[:mid]) for item in self.beside]
        self.corner_two = [net.y(self.over[mid:], s) for s in range(1, net.yn)]
        self.pieces = [self.line, self.over] + self.beside
        self.plan = [(0, 0, 0, ZN), (0, 1, 0, ZN)]
        self.plan += [(s, 0, 0, ZN) for s in range(1, net.yn)]
        self.moved = [net.c(item) for item in self.pieces]

    def finish(self, order):
        net = self.net
        late = order(*self.corner_one, *self.corner_two)
        plan = [(s, 1, 0, ZN // 2) for s in range(1, net.yn)]
        plan += [(s, 1, ZN // 2, ZN - ZN // 2) for s in range(1, net.yn)]
        pieces = self.pieces + list(late) + self.moved + [net.c(item) for item in late]
        plan = self.plan + plan
        full = [(s, q, side, first, count) for side in range(2) for s, q, first, count in plan]
        return full, pieces


def piece_spots(plan, where_ref, rows, half, yn):
    z0, y0, c0, p0 = where_ref[0], where_ref[1], where_ref[2], where_ref[3]
    spots = []
    for i, (s, q, side, first, count) in enumerate(plan):
        y = lax.rem(y0 + yn - s, yn)
        p = lax.rem(p0 + q, 2)
        c = lax.rem(c0 + side, 2)
        for k in range(count):
            z = lax.bitwise_xor(z0, jnp.int32(first + k))
            start = pl.multiple_of(((z * yn + y) * 2 + c) * rows + p * half, half)
            spots.append((i, k * half, first + k, start))
    return spots


def pack_kernel(*refs):
    time_ref, vectors, out_ref = refs[0], refs[1:-1], refs[-1]
    out_ref[...] = jnp.zeros_like(out_ref)
    rows = time_ref.shape[0]
    out_ref[:rows, :] = time_ref[...]
    for i, item in enumerate(vectors):
        out_ref[rows + i : rows + i + 1, : item.shape[1]] = item[...]


def small_kernel(rows, te_rows, sizes, yn, where_ref, embed_ref, own_ref, other_ref, *refs):
    scale_ref, all_ref, outs, held, sems = refs[0], refs[1], refs[2:-2], refs[-2], refs[-1]
    z0, y0, c0 = where_ref[0], where_ref[1], where_ref[2]
    copies = []
    for side, piece_ref in enumerate((own_ref, other_ref)):
        c = lax.rem(c0 + side, 2)
        for s in range(yn):
            y = lax.rem(y0 + yn - s, yn)
            for k in range(ZN):
                z = lax.bitwise_xor(z0, jnp.int32(k))
                copies.append(
                    pltpu.make_async_copy(
                        piece_ref.at[s * ZN + k],
                        held.at[(z * yn + y) * 2 + c],
                        sems.at[len(copies)],
                    )
                )
    for copy in copies:
        copy.start()
    for copy in copies:
        copy.wait()
    fs = held.shape[0]
    scale = jnp.ones_like(scale_ref)
    whole = jnp.concatenate([held[f, :te_rows, :] for f in range(fs)], axis=0)
    scale_ref[...] = scale + jnp.dot(embed_ref[...], whole, preferred_element_type=F32)
    for i, (size, out_ref) in enumerate(zip(sizes, outs)):
        pieces = [
            held[f, te_rows + i : te_rows + i + 1, :size].astype(F32) for f in range(fs)
        ]
        out_ref[...] = jnp.concatenate(pieces, axis=1)
    last, wide = te_rows + len(sizes), embed_ref.shape[1]
    all_ref[...] = jnp.concatenate(
        [held[f, last : last + 1, :wide].astype(F32) for f in range(fs)], axis=0
    )


class SmallGather:
    def __init__(self, net, time_weight, vectors, embed):
        self.net, self.sizes = net, [item.shape[0] for item in vectors]
        self.te_rows, self.width = time_weight.shape
        self.rows = self.te_rows + len(vectors) + 1
        self.rows += -self.rows % 16
        self.packed = pl.pallas_call(
            pack_kernel,
            out_shape=jax.ShapeDtypeStruct((self.rows, self.width), BF16),
            cost_estimate=cost(),
            name="pack_small",
        )(time_weight, *[item.reshape(1, -1) for item in vectors], embed)
        self.parts = [net.z(self.packed, k) for k in range(1, ZN)]

    def across(self, order):
        net = self.net
        self.line = jnp.stack(order(self.packed, *self.parts))
        self.beside = [net.y(self.line, s) for s in range(1, net.yn)]

    def other(self, order):
        self.line, *self.beside = order(self.line, *self.beside)
        self.sides = jnp.concatenate([self.line] + self.beside, axis=0)
        self.moved = self.net.c(self.sides)

    def finish(self, order, embed):
        net, fs = self.net, self.net.fs
        moved = order(self.moved)
        where = jnp.stack([net.z0, net.y0, net.c0]).astype(jnp.int32)
        shapes = [(1, self.width), (fs, embed.shape[1])]
        shapes += [(1, size * fs) for size in self.sizes]
        outs = pl.pallas_call(
            functools.partial(small_kernel, self.rows, self.te_rows, self.sizes, net.yn),
            out_shape=[jax.ShapeDtypeStruct(shape, F32) for shape in shapes],
            grid_spec=pltpu.PrefetchScalarGridSpec(
                num_scalar_prefetch=1,
                grid=(1,),
                in_specs=[pl.BlockSpec(embed.shape, lambda i, r: (0, 0))]
                + [pl.BlockSpec(memory_space=pl.ANY)] * 2,
                out_specs=[whole_spec(shape) for shape in shapes],
                scratch_shapes=[
                    pltpu.VMEM((fs, self.rows, self.width), BF16),
                    pltpu.SemaphoreType.DMA((fs,)),
                ],
            ),
            cost_estimate=cost(3.0),
            name="small_join",
        )(where, embed, self.sides, moved)
        order.note(outs[0])
        return outs


def relative_order(net, rows, total):
    half = rows // 2
    d = jnp.arange(total, dtype=jnp.int32)
    f, i = d // rows, d % rows
    z, y, c = f // (2 * net.yn), (f // 2) % net.yn, f % 2
    p, j = i // half, i % half
    c, y, p, z = c ^ net.c0, (y - net.y0) % net.yn, p ^ net.p0, z ^ net.z0
    z = 2 * (z % 2) + z // 2
    return (((c * net.yn + y) * 2 + p) * ZN + z) * half + j


def add_low(*items):
    total = items[0].astype(F32)
    for item in items[1:]:
        total = total + item.astype(F32)
    return total.astype(BF16)


def sum_kernel(counts, keep, *refs):
    total = sum(counts)
    kept_ref, sent_ref = refs[total], refs[total + 1]
    at, column = 0, 0
    for count in counts:
        items = refs[at : at + count]
        at += count
        wide = items[0].shape[1]
        value = items[0][...].astype(F32)
        for item in items[1:]:
            value = value + item[...].astype(F32)
        kept_ref[:, column : column + wide] = value[:keep, :]
        sent_ref[:, column : column + wide] = value[keep:, :].astype(BF16)
        column += wide


def sum_split(groups, keep, micros=0.5):
    rows = groups[0][0].shape[0]
    columns = sum(group[0].shape[1] for group in groups)
    return pl.pallas_call(
        functools.partial(sum_kernel, [len(group) for group in groups], keep),
        out_shape=[
            jax.ShapeDtypeStruct((keep, columns), F32),
            jax.ShapeDtypeStruct((rows - keep, columns), BF16),
        ],
        cost_estimate=cost(micros),
        name="sum_split",
    )(*[item for group in groups for item in group])


def merge_kernel(shifts, over_ref, *refs):
    sides, came_x, came_y = (refs[i * shifts : (i + 1) * shifts] for i in range(3))
    over_out, outs = refs[3 * shifts], refs[3 * shifts + 1 :]
    half = over_ref.shape[0] // 2
    over_out[:half, :] = over_ref[:half, :]
    value = over_ref[half:, :].astype(F32)
    for item in came_y:
        value = value + item[...].astype(F32)
    over_out[half:, :] = value.astype(BF16)
    for side_ref, item, out_ref in zip(sides, came_x, outs):
        value = side_ref[:half, :].astype(F32) + item[...].astype(F32)
        out_ref[:half, :] = value.astype(BF16)
        out_ref[half:, :] = side_ref[half:, :]


def merge_corners(over, sides, came_x, came_y):
    shape = jax.ShapeDtypeStruct(over.shape, BF16)
    return pl.pallas_call(
        functools.partial(merge_kernel, len(sides)),
        out_shape=[shape] * (1 + len(sides)),
        cost_estimate=cost(0.5),
        name="merge_corners",
    )(over, *sides, *came_x, *came_y)


class Scatter:
    def __init__(self, net):
        self.net = net

    def core(self, send):
        self.sent = self.net.c(send)

    def join_core(self, order):
        self.sent = order(self.sent)
        return self.sent

    def corners(self, own, over, *rest):
        net = self.net
        self.own, self.over, self.side = own, over, list(rest[0::3])
        self.came_x = [net.x(item) for item in rest[1::3]]
        self.came_y = [net.y(item, s + 1) for s, item in enumerate(rest[2::3])]

    def across(self, order):
        net, count = self.net, len(self.side)
        came = order(*self.came_x, *self.came_y)
        self.over, *self.side = merge_corners(self.over, self.side, came[:count], came[count:])
        order.note(self.over)
        self.over = net.x(self.over)
        self.side = [net.y(item, s + 1) for s, item in enumerate(self.side)]

    def group(self, order):
        return [self.own, *order(self.over, *self.side)]


class Line:
    def __init__(self, net, half, groups):
        self.net, self.half = net, half
        self.kept, far = sum_split(groups, (ZN // 2) * half, 9.0 / len(groups) ** 3)
        self.far = net.z(far, 1)

    def nearer(self, order):
        self.here, near = sum_split([[self.kept, order(self.far)]], self.half)
        self.near = self.net.z(near, 2)

    def last(self, order):
        net = self.net
        mine = add_low(self.here, order(self.near))
        if net.dp > 2:
            groups = [list(range(q, net.dp, 2)) for q in range(2)]
            mine = lax.psum(mine, "dp", axis_index_groups=groups)
        self.mine, self.other = mine, net.x(mine)

    def finish(self, order):
        mine, other = self.mine, order(self.other)
        first = jnp.where(self.net.p0 == 0, mine, other)
        second = jnp.where(self.net.p0 == 0, other, mine)
        return jnp.concatenate([first, second], axis=0).astype(F32)


def kept_parts(yn, half):
    line = ZN * half
    spots = [(0, line), (line, line)]
    for s in range(1, yn):
        first = 2 * s * line
        spots.append((first, line))
        spots += [(first + line + i * (line // 2), line // 2) for i in range(2)]
    return spots


def cost(micros=1.0):
    return pl.CostEstimate(flops=int(micros * 9e8), bytes_accessed=int(micros * 3e6), transcendentals=0)


def weight_copies(plan, where_ref, rows, half, yn, pieces, targets, sems):
    spots = piece_spots(plan, where_ref, rows, half, yn)
    groups, count, column = [], 0, 0
    for target, first, wide in targets:
        group = []
        for i, row, shift, start in spots:
            group.append(
                pltpu.make_async_copy(
                    pieces[i].at[pl.ds(row, half), pl.ds(column, wide)],
                    target.at[pl.ds(start, half), pl.ds(first, wide)],
                    sems.at[count],
                )
            )
            count += 1
        column += wide
        groups.append(group)
    for group in groups:
        for copy in group:
            copy.start()
    return groups


def finish_copies(copies):
    for copy in copies:
        copy.wait()


def back_copy(held, out, first, wide, sem):
    spot = pl.ds(first, wide)
    copy = pltpu.make_async_copy(held.at[:, spot], out.at[:, spot], sem)
    copy.start()
    return copy


def qkv_kernel(plan, rows, half, yn, where_ref, x_ref, cos_ref, sin_ref, *refs):
    pieces = refs[: len(plan)]
    out_ref, wq_ref, wo_ref, wq, wo, low, sems, back_sems = refs[len(plan) :]
    wide = wo.shape[1]
    targets = [(wq, part * wide, wide) for part in range(3)] + [(wo, 0, wide)]
    groups = weight_copies(plan, where_ref, rows, half, yn, pieces, targets, sems)
    cosine, sine = cos_ref[...], sin_ref[...]
    front = lax.broadcasted_iota(jnp.int32, cosine.shape, 1) % HD < HD // 2
    backs = []
    for part in range(3):
        finish_copies(groups[part])
        backs.append(back_copy(wq, wq_ref, part * wide, wide, back_sems.at[part]))
        for j in range(wide // (2 * PAIR)):
            first = part * wide + j * 2 * PAIR
            acc = jnp.dot(
                x_ref[...], wq[:, first : first + 2 * PAIR], preferred_element_type=F32
            )
            for i in range(2):
                piece = acc[:, i * PAIR : (i + 1) * PAIR]
                if part < 2:
                    turned = jnp.where(
                        front,
                        -pltpu.roll(piece, PAIR - HD // 2, 1),
                        pltpu.roll(piece, HD // 2, 1),
                    )
                    piece = piece * cosine + turned * sine
                low[:, first + i * PAIR : first + (i + 1) * PAIR] = piece.astype(BF16)
        backs.append(back_copy(low, out_ref, part * wide, wide, back_sems.at[4 + part]))
    finish_copies(groups[3])
    backs.append(back_copy(wo, wo_ref, 0, wide, back_sems.at[3]))
    finish_copies(backs)


def attn_in_kernel(low_ref, high_ref, w_ref, out_ref):
    wide = low_ref.shape[2]
    acc = back_dot(low_ref[0], w_ref[:, :wide]) + back_dot(high_ref[0], w_ref[:, wide:])
    step = pl.program_id(0)

    @pl.when(step == 0)
    def _():
        out_ref[...] = acc

    @pl.when(step > 0)
    def _():
        out_ref[...] = out_ref[...] + acc


def attn_in_back(low, high, w):
    parts, tokens, wide = low.shape
    depth = w.shape[0]
    half = pl.BlockSpec((1, tokens, wide), lambda i: (i, 0, 0))
    return pl.pallas_call(
        attn_in_kernel,
        grid=(parts,),
        in_specs=[half, half, pl.BlockSpec((depth, 2 * wide), lambda i: (0, i))],
        out_specs=pl.BlockSpec((tokens, depth), lambda i: (0, 0)),
        out_shape=jax.ShapeDtypeStruct((tokens, depth), F32),
        cost_estimate=cost(1.0),
        name="attn_in_back",
    )(low, high, w)


def where_of(net):
    return jnp.stack([net.z0, net.y0, net.c0, net.p0]).astype(jnp.int32)


ANY = pl.BlockSpec(memory_space=pl.ANY)


def whole_spec(shape):
    return pl.BlockSpec(shape, lambda i, r: (0, 0))


def qkv_rotated(net, x, plan, pieces, rows, cosine, sine):
    tokens, depth = x.shape
    total = net.fs * rows
    blocks = sum(entry[4] for entry in plan)
    half = rows // 2
    return pl.pallas_call(
        functools.partial(qkv_kernel, plan, rows, half, net.yn),
        grid_spec=pltpu.PrefetchScalarGridSpec(
            num_scalar_prefetch=1,
            grid=(1,),
            in_specs=[whole_spec(x.shape), whole_spec(cosine.shape), whole_spec(sine.shape)]
            + [ANY] * len(pieces),
            out_specs=[ANY] * 3,
            scratch_shapes=[
                pltpu.VMEM((total, 3 * depth), BF16),
                pltpu.VMEM((total, depth), BF16),
                pltpu.VMEM((tokens, 3 * depth), BF16),
                pltpu.SemaphoreType.DMA((4 * blocks,)),
                pltpu.SemaphoreType.DMA((7,)),
            ],
        ),
        out_shape=[
            jax.ShapeDtypeStruct((tokens, 3 * depth), BF16),
            jax.ShapeDtypeStruct((total, 3 * depth), BF16),
            jax.ShapeDtypeStruct((total, depth), BF16),
        ],
        compiler_params=pltpu.CompilerParams(vmem_limit_bytes=32 * 2**20),
        cost_estimate=cost(10.0),
        name="qkv_rotated",
    )(where_of(net), x, cosine, sine, *pieces)


def up_kernel(plan, rows, half, yn, where_ref, x_ref, b_ref, *refs):
    pieces = refs[: len(plan)]
    act_out, slope_out, w_out, w, act, slope, sems, back_sems = refs[len(plan) :]
    total = w.shape[1]
    wide = min(1024, total)
    step = min(256, wide)
    parts = total // wide
    targets = [(w, part * wide, wide) for part in range(parts)]
    groups = weight_copies(plan, where_ref, rows, half, yn, pieces, targets, sems)
    backs = []
    for part in range(parts):
        finish_copies(groups[part])
        backs.append(back_copy(w, w_out, part * wide, wide, back_sems.at[3 * part]))
        for first in range(part * wide, (part + 1) * wide, step):
            spot = slice(first, first + step)
            v = jnp.dot(x_ref[...], w[:, spot], preferred_element_type=F32) + b_ref[:, spot]
            square = v * v
            bend = jnp.tanh(v * (ROOT + ROOT * 0.044715 * square))
            half_up = 0.5 + 0.5 * bend
            act[:, spot] = (v * half_up).astype(BF16)
            rise = 0.5 * ROOT + (1.5 * 0.044715 * ROOT) * square
            slope[:, spot] = (half_up + v * (1.0 - bend * bend) * rise).astype(BF16)
        backs.append(back_copy(act, act_out, part * wide, wide, back_sems.at[3 * part + 1]))
        backs.append(back_copy(slope, slope_out, part * wide, wide, back_sems.at[3 * part + 2]))
    finish_copies(backs)


def up_gelu(net, x, plan, pieces, rows, bias):
    tokens, depth = x.shape
    total = bias.shape[1]
    parts = total // min(1024, total)
    blocks = sum(entry[4] for entry in plan)
    return pl.pallas_call(
        functools.partial(up_kernel, plan, rows, rows // 2, net.yn),
        grid_spec=pltpu.PrefetchScalarGridSpec(
            num_scalar_prefetch=1,
            grid=(1,),
            in_specs=[whole_spec(x.shape), whole_spec(bias.shape)] + [ANY] * len(pieces),
            out_specs=[ANY] * 3,
            scratch_shapes=[
                pltpu.VMEM((depth, total), BF16),
                pltpu.VMEM((tokens, total), BF16),
                pltpu.VMEM((tokens, total), BF16),
                pltpu.SemaphoreType.DMA((parts * blocks,)),
                pltpu.SemaphoreType.DMA((3 * parts,)),
            ],
        ),
        out_shape=[
            jax.ShapeDtypeStruct((tokens, total), BF16),
            jax.ShapeDtypeStruct((tokens, total), BF16),
            jax.ShapeDtypeStruct((depth, total), BF16),
        ],
        compiler_params=pltpu.CompilerParams(vmem_limit_bytes=40 * 2**20),
        cost_estimate=cost(8.0),
        name="up_gelu",
    )(where_of(net), x, bias, *pieces)


def down_kernel(plan, rows, half, yn, where_ref, g_ref, slope_ref, *refs):
    pieces = refs[: len(plan)]
    out_ref, sum_ref, w_ref, w, slope, low, sems, slope_sems, back_sems = refs[len(plan) :]
    spots = piece_spots(plan, where_ref, rows, half, yn)
    group_rows = w.shape[0] // ZN
    step = min(256, group_rows)
    z0 = where_ref[0]
    groups = [[] for _ in range(ZN)]
    for count, (i, row, shift, start) in enumerate(spots):
        copy = pltpu.make_async_copy(
            pieces[i].at[pl.ds(row, half), :], w.at[pl.ds(start, half), :], sems.at[count]
        )
        groups[shift].append(copy)
    slopes = []
    for k in range(ZN):
        at = pl.multiple_of(lax.bitwise_xor(z0, jnp.int32(k)) * group_rows, group_rows)
        for copy in groups[k]:
            copy.start()
        copy = pltpu.make_async_copy(
            slope_ref.at[:, pl.ds(at, group_rows)], slope.at[k], slope_sems.at[k]
        )
        copy.start()
        slopes.append(copy)
    backs = []
    for k in range(ZN):
        at = pl.multiple_of(lax.bitwise_xor(z0, jnp.int32(k)) * group_rows, group_rows)
        finish_copies(groups[k])
        slopes[k].wait()
        here = pl.ds(at, group_rows)
        copy = pltpu.make_async_copy(w.at[here, :], w_ref.at[here, :], back_sems.at[2 * k])
        copy.start()
        backs.append(copy)
        for j in range(group_rows // step):
            spot = slice(j * step, (j + 1) * step)
            inner = pl.multiple_of(at + j * step, step)
            acc = lax.dot_general(
                g_ref[...],
                w[pl.ds(inner, step), :],
                (((1,), (1,)), ((), ())),
                preferred_element_type=F32,
            )
            rounded = (acc * slope[k, :, spot].astype(F32)).astype(BF16)
            low[k, :, spot] = rounded
            sum_ref[:, pl.ds(inner, step)] = jnp.sum(
                rounded.astype(F32), axis=0, keepdims=True
            )
        copy = pltpu.make_async_copy(low.at[k], out_ref.at[:, here], back_sems.at[2 * k + 1])
        copy.start()
        backs.append(copy)
    finish_copies(backs)


def down_back(net, grad, plan, pieces, rows, slope):
    tokens, depth = grad.shape
    total = slope.shape[1]
    blocks = sum(entry[4] for entry in plan)
    return pl.pallas_call(
        functools.partial(down_kernel, plan, rows, rows // 2, net.yn),
        grid_spec=pltpu.PrefetchScalarGridSpec(
            num_scalar_prefetch=1,
            grid=(1,),
            in_specs=[whole_spec(grad.shape), ANY] + [ANY] * len(pieces),
            out_specs=[ANY, pl.BlockSpec((1, total), lambda i, r: (0, 0)), ANY],
            scratch_shapes=[
                pltpu.VMEM((total, depth), BF16),
                pltpu.VMEM((ZN, tokens, total // ZN), BF16),
                pltpu.VMEM((ZN, tokens, total // ZN), BF16),
                pltpu.SemaphoreType.DMA((blocks,)),
                pltpu.SemaphoreType.DMA((ZN,)),
                pltpu.SemaphoreType.DMA((2 * ZN,)),
            ],
        ),
        out_shape=[
            jax.ShapeDtypeStruct((tokens, total), BF16),
            jax.ShapeDtypeStruct((1, total), F32),
            jax.ShapeDtypeStruct((total, depth), BF16),
        ],
        compiler_params=pltpu.CompilerParams(vmem_limit_bytes=40 * 2**20),
        cost_estimate=cost(10.0),
        name="down_back",
    )(where_of(net), grad, slope, *pieces)


def attend_kernel(len_ref, q_ref, k_ref, v_ref, out_ref):
    q, k, v = q_ref[...], k_ref[...], v_ref[...]
    length = k.shape[0]
    first = lax.broadcasted_iota(jnp.int32, q.shape, 1) < HD
    valid = lax.broadcasted_iota(jnp.int32, (1, length), 1) < len_ref[0]
    zero = jnp.zeros_like(q)
    outs = []
    for h in range(2):
        one = jnp.where(first, q, zero) if h == 0 else jnp.where(first, zero, q)
        scores = lax.dot_general(
            one, k, (((1,), (1,)), ((), ())), preferred_element_type=F32
        )
        scores = jnp.where(valid, scores * HD**-0.5, -1000000000.0)
        top = jnp.max(scores, axis=1, keepdims=True)
        exponent = jnp.exp2((scores - top) * LOG2E)
        total = jnp.sum(exponent, axis=1, keepdims=True)
        mixed = jnp.dot(exponent.astype(BF16), v, preferred_element_type=F32)
        outs.append(mixed * (1.0 / total))
    out_ref[...] = jnp.where(first, outs[0], outs[1]).astype(BF16)


def attend(length, qkv, first_pair, pairs):
    rows, total = qkv.shape
    count = total // 3 // PAIR

    def pick(part):
        return pl.BlockSpec((rows, PAIR), lambda j, r: (0, part * count + first_pair + j))

    return pl.pallas_call(
        attend_kernel,
        grid_spec=pltpu.PrefetchScalarGridSpec(
            num_scalar_prefetch=1,
            grid=(pairs,),
            in_specs=[pick(0), pick(1), pick(2)],
            out_specs=pl.BlockSpec((rows, PAIR), lambda j, r: (0, j)),
        ),
        out_shape=jax.ShapeDtypeStruct((rows, pairs * PAIR), BF16),
        cost_estimate=cost(1.4 * pairs),
        name="attend",
    )(length, qkv, qkv, qkv)


def attend_back_kernel(len_ref, q_ref, k_ref, v_ref, g_ref, cos_ref, sin_ref, out_ref):
    q, k, v, g = q_ref[...], k_ref[...], v_ref[...], g_ref[...]
    length = k.shape[0]
    lane = lax.broadcasted_iota(jnp.int32, q.shape, 1)
    first = lane < HD
    valid = lax.broadcasted_iota(jnp.int32, (length, length), 0) < len_ref[0]
    zero = jnp.zeros_like(q)
    grads = []
    for h in range(2):
        key = jnp.where(first, k, zero) if h == 0 else jnp.where(first, zero, k)
        value = jnp.where(first, v, zero) if h == 0 else jnp.where(first, zero, v)
        scores = lax.dot_general(
            key, q, (((1,), (1,)), ((), ())), preferred_element_type=F32
        )
        scores = jnp.where(valid, scores * HD**-0.5, -1000000000.0)
        top = jnp.max(scores, axis=0, keepdims=True)
        exponent = jnp.exp2((scores - top) * LOG2E)
        total = jnp.sum(exponent, axis=0, keepdims=True)
        probs = exponent * (1.0 / total)
        grad_probs = lax.dot_general(
            value, g, (((1,), (1,)), ((), ())), preferred_element_type=F32
        )
        delta = jnp.sum(grad_probs * probs, axis=0, keepdims=True)
        grad_scores = (probs * (grad_probs - delta)).astype(BF16)
        grads.append(
            (
                lax.dot_general(
                    grad_scores, k, (((0,), (0,)), ((), ())), preferred_element_type=F32
                ),
                jnp.dot(grad_scores, q, preferred_element_type=F32),
                jnp.dot(probs.astype(BF16), g, preferred_element_type=F32),
            )
        )
    front = lane % HD < HD // 2
    cosine, sine = cos_ref[...] * HD**-0.5, sin_ref[...] * HD**-0.5
    for i in range(2):
        grad = jnp.where(first, grads[0][i], grads[1][i])
        sined = grad * sine
        turned = jnp.where(
            front, pltpu.roll(sined, PAIR - HD // 2, 1), -pltpu.roll(sined, HD // 2, 1)
        )
        out_ref[i] = (grad * cosine + turned).astype(BF16)
    out_ref[2] = jnp.where(first, grads[0][2], grads[1][2]).astype(BF16)


def attend_back(length, qkv, grad, cosine, sine, first_pair, pairs):
    rows, total = qkv.shape
    count = total // 3 // PAIR

    def pick(part):
        return pl.BlockSpec((rows, PAIR), lambda j, r: (0, part * count + first_pair + j))

    table = pl.BlockSpec((rows, PAIR), lambda j, r: (0, 0))
    return pl.pallas_call(
        attend_back_kernel,
        grid_spec=pltpu.PrefetchScalarGridSpec(
            num_scalar_prefetch=1,
            grid=(pairs,),
            in_specs=[pick(0), pick(1), pick(2), pick(0), table, table],
            out_specs=pl.BlockSpec((3, rows, PAIR), lambda j, r: (0, 0, j)),
        ),
        out_shape=jax.ShapeDtypeStruct((3, rows, pairs * PAIR), BF16),
        cost_estimate=cost(3.0 * pairs),
        name="attend_back",
    )(length, qkv, qkv, qkv, grad, cosine, sine)


def tall_kernel(left_ref, grad_ref, out_ref):
    out_ref[...] = lax.dot_general(
        left_ref[...], grad_ref[...], (((0,), (0,)), ((), ())), preferred_element_type=F32
    ).astype(BF16)


def tall_rows_dot(left, grad):
    depth, columns = grad.shape
    total = left.shape[1]
    tall = min(1024, total)
    return pl.pallas_call(
        tall_kernel,
        grid=(total // tall,),
        in_specs=[
            pl.BlockSpec((depth, tall), lambda i: (0, i)),
            pl.BlockSpec((depth, columns), lambda i: (0, 0)),
        ],
        out_specs=pl.BlockSpec((tall, columns), lambda i: (i, 0)),
        out_shape=jax.ShapeDtypeStruct((total, columns), BF16),
        cost_estimate=cost(9.0),
        name="tall_rows_dot",
    )(left, grad)


def wide_kernel(bounds, parts, *refs):
    step = pl.program_id(0)
    operands, rest = refs[: 2 * len(bounds)], refs[2 * len(bounds) :]

    def write(left_ref, grad_ref):
        grad = grad_ref[0] if len(grad_ref.shape) == 3 else grad_ref[...]
        acc = jnp.dot(left_ref[...], grad, preferred_element_type=F32)
        if parts is None:
            rest[-1][...] = acc.astype(BF16)
            return
        acc = acc + rest[0][...].astype(F32)
        for (first, rows), out_ref in zip(parts, rest[1:]):
            out_ref[...] = acc[first : first + rows, :].astype(BF16)

    for i, (low, high) in enumerate(bounds):

        @pl.when((step >= low) & (step < high))
        def _(i=i):
            write(operands[2 * i], operands[2 * i + 1])


def wide_rows_dot(at, rows, pairs, extra=None, parts=None):
    in_specs, args, bounds, done = [], [], [], 0
    wide = min(min(1024, grad.shape[-1]) for _, grad in pairs)
    for left, grad in pairs:
        depth = left.shape[1]
        count = grad.shape[0] if grad.ndim == 3 else grad.shape[1] // wide
        in_specs.append(pl.BlockSpec((rows, depth), lambda j: (at, 0)))

        def clip(j, done=done, count=count):
            return jnp.clip(j - done, 0, count - 1)

        if grad.ndim == 3:
            in_specs.append(pl.BlockSpec((1, depth, wide), lambda j, clip=clip: (clip(j), 0, 0)))
        else:
            in_specs.append(pl.BlockSpec((depth, wide), lambda j, clip=clip: (0, clip(j))))
        args += [left, grad]
        bounds.append((done, done + count))
        done += count
    spec = pl.BlockSpec((rows, wide), lambda j: (0, j))
    columns = done * wide
    if parts is None:
        out_specs, out_shape = spec, jax.ShapeDtypeStruct((rows, columns), BF16)
    else:
        in_specs.append(spec)
        args.append(extra)
        out_specs = [pl.BlockSpec((count, wide), lambda j: (0, j)) for _, count in parts]
        out_shape = [jax.ShapeDtypeStruct((count, columns), BF16) for _, count in parts]
    return pl.pallas_call(
        functools.partial(wide_kernel, bounds, parts),
        grid=(done,),
        in_specs=in_specs,
        out_specs=out_specs,
        out_shape=out_shape,
        cost_estimate=cost(1.5 * done),
        name="wide_rows_dot",
    )(*args)


def per_device(
    dp,
    fs,
    tokens,
    lengths,
    time_embed,
    cotangent,
    time_weight,
    attn_gain,
    attn_shift,
    qkv_weight,
    out_weight,
    mlp_gain,
    mlp_shift,
    up_weight,
    up_bias,
    down_weight,
    down_bias,
):
    net = Net(dp, fs)
    length, width = tokens.shape[1:]
    tokens, cotangent = tokens.reshape(length, width), cotangent.reshape(length, width)
    order = Order()
    wide_rows, tall_rows = qkv_weight.shape[0], down_weight.shape[0]
    te_rows = time_weight.shape[0]
    heads = width // HD
    half = width // 2
    with jax.named_scope("small_gather"):
        small = SmallGather(
            net,
            time_weight,
            [attn_gain, attn_shift, mlp_gain, mlp_shift, down_bias, up_bias],
            time_embed,
        )
    order.note(small.packed)
    with jax.named_scope("attn_gather"):
        attn_net = Gather(net, jnp.concatenate([qkv_weight, out_weight], axis=1))
        attn_net.along(order(attn_net.own))
    up_net = Gather(net, up_weight)
    down_net = Gather(net, down_weight)
    residual = tokens.astype(F32)
    normed_one, inverse_one = normalize(residual)
    up_net.own, down_net.own = order(inverse_one, up_net.own, down_net.own)[1:]
    with jax.named_scope("small_gather"):
        small.across(order)
    with jax.named_scope("small_gather"):
        small.other(order)
    with jax.named_scope("attn_gather"):
        attn_net.join_line(order)
        order.note(attn_net.line)
        attn_net.across()
    with jax.named_scope("up_gather"):
        up_net.along(order(up_net.own))
    with jax.named_scope("small_gather"):
        (
            time_scale,
            embeds,
            gain_one,
            shift_one,
            gain_two,
            shift_two,
            down_bias_full,
            up_bias_full,
        ) = small.finish(order, time_embed)

    place = relative_order(net, wide_rows, width)
    permute = (jnp.arange(width, dtype=jnp.int32)[:, None] == place[None, :]).astype(BF16)

    def turn(values_in):
        return back_dot(permute, values_in).astype(BF16)

    key_mask = jnp.arange(length, dtype=jnp.int32)[:, None] < lengths[None, :]
    affine_one = normed_one * gain_one + shift_one
    attn_in = (affine_one * time_scale).astype(BF16)
    cosine, sine = rotary_tables(length)
    order.note(attn_in, cosine, sine)
    turned_one = order.note(turn(order(attn_in)))
    with jax.named_scope("up_gather"):
        up_net.join_line(order)
        order.note(up_net.line)
    with jax.named_scope("attn_gather"):
        attn_net.join_across(order)
        attn_net.corners()
    with jax.named_scope("down_gather"):
        down_net.along(order(down_net.own))
    with jax.named_scope("attn_gather"):
        plan, pieces = attn_net.finish(order)
    with jax.named_scope("up_gather"):
        up_net.line = order(up_net.line)
        up_net.across()
    qkv, qkv_full, out_full = qkv_rotated(net, attn_in, plan, pieces, wide_rows, cosine, sine)
    order.note(qkv)
    pairs = heads // 2
    part = pairs // 2
    with jax.named_scope("down_gather"):
        down_net.join_line(order)
        order.note(down_net.line)
    with jax.named_scope("up_gather"):
        up_net.join_across(order)
        up_net.corners()
    context = order.note(attend(lengths, order(qkv), 0, pairs))
    with jax.named_scope("up_gather"):
        plan, pieces = up_net.finish(order)
    with jax.named_scope("down_gather"):
        down_net.line = order(down_net.line)
        down_net.across()
    context = order(context)
    hidden = residual + jnp.dot(context, out_full, preferred_element_type=F32)
    normed_two, inverse_two = normalize(hidden)
    affine_two = normed_two * gain_two + shift_two
    mlp_in = (affine_two * time_scale).astype(BF16)
    order.note(mlp_in)
    turned_ctx = order.note(turn(order(context)))
    active, slope, up_full = up_gelu(
        net, order(mlp_in), plan, pieces, wide_rows, up_bias_full
    )
    order.note(active)
    with jax.named_scope("down_gather"):
        down_net.join_across(order)
        down_net.corners()

    grad_out = cotangent.astype(F32) * key_mask.astype(F32)
    grad_branch = grad_out.astype(BF16)
    with jax.named_scope("down_grad"):
        tall = order.note(tall_rows_dot(order(active), grad_branch))
        down_mine = lax.psum_scatter(tall, "fsdp", scatter_dimension=0, tiled=True)
    down_bias_grad = jnp.sum(grad_branch.astype(F32), axis=0, keepdims=True)
    turned_two = order.note(turn(order(mlp_in)))
    with jax.named_scope("down_gather"):
        plan, pieces = down_net.finish(order)
    grad_pre, up_bias_grad, down_full = down_back(
        net, order(grad_branch), plan, pieces, tall_rows, slope
    )
    grad_pre = order(order.note(grad_pre))
    grad_mlp_in = back_dot(grad_pre, up_full)
    grad_affine_two = grad_mlp_in * time_scale
    grad_scale = jnp.sum(grad_mlp_in * affine_two, axis=0, keepdims=True)
    mlp_gain_grad = jnp.sum(grad_affine_two * normed_two, axis=0, keepdims=True)
    mlp_shift_grad = jnp.sum(grad_affine_two, axis=0, keepdims=True)
    grad_hidden = grad_out + norm_back(grad_affine_two * gain_two, normed_two, inverse_two)
    grad_attn = order.note(grad_hidden.astype(BF16))
    wide_half = wide_rows // 2
    wide_parts = kept_parts(net.yn, wide_half)
    up_red, low_red, high_red = Scatter(net), Scatter(net), Scatter(net)
    up_pairs = [(turned_two, grad_pre), (turned_ctx, grad_attn)]
    with jax.named_scope("up_grad"):
        order(grad_pre)
        up_red.core(order.note(wide_rows_dot(1, half, up_pairs)))
    grad_context = order.note(back_dot(order(grad_attn), out_full).astype(BF16))
    with jax.named_scope("up_grad"):
        sent = up_red.join_core(order)
        kept = wide_rows_dot(0, half, up_pairs, sent, wide_parts)
        order.note(kept[0])
        up_red.corners(*kept)
    low = attend_back(lengths, qkv, order(grad_context), cosine, sine, 0, part)
    order.note(low)
    with jax.named_scope("qkv_grad"):
        low_red.core(order.note(wide_rows_dot(1, half, [(turned_one, order(low))])))
    with jax.named_scope("up_grad"):
        up_red.across(order)
    high = attend_back(lengths, qkv, order(grad_context), cosine, sine, part, pairs - part)
    order.note(high)
    with jax.named_scope("qkv_grad"):
        sent = low_red.join_core(order)
        kept = wide_rows_dot(0, half, [(turned_one, low)], sent, wide_parts)
        order.note(kept[0])
        low_red.corners(*kept)
        high_red.core(order.note(wide_rows_dot(1, half, [(turned_one, order(high))])))
    with jax.named_scope("up_grad"):
        up_line = Line(net, wide_half, [up_red.group(order)])
        order.note(up_line.kept)
    with jax.named_scope("qkv_grad"):
        sent = high_red.join_core(order)
        kept = wide_rows_dot(0, half, [(turned_one, high)], sent, wide_parts)
        order.note(kept[0])
        high_red.corners(*kept)
    with jax.named_scope("qkv_grad"):
        low_red.across(order)
        high_red.across(order)
    grad_attn_in = attn_in_back(low, order(high), qkv_full)
    grad_affine_one = grad_attn_in * time_scale
    grad_scale = grad_scale + jnp.sum(grad_attn_in * affine_one, axis=0, keepdims=True)
    attn_gain_grad = jnp.sum(grad_affine_one * normed_one, axis=0, keepdims=True)
    attn_shift_grad = jnp.sum(grad_affine_one, axis=0, keepdims=True)
    token_grad = (
        grad_hidden + norm_back(grad_affine_one * gain_one, normed_one, inverse_one)
    ).astype(BF16)
    order.note(token_grad, grad_scale)
    with jax.named_scope("small_sums"):
        sums = jnp.concatenate(
            [
                attn_gain_grad,
                attn_shift_grad,
                mlp_gain_grad,
                mlp_shift_grad,
                down_bias_grad,
                up_bias_grad.reshape(-1, width),
            ],
            axis=0,
        )
        count = sums.shape[0]
        spots = jnp.arange(fs, dtype=jnp.int32)[:, None] == net.me
        packed = jnp.concatenate([sums, jnp.where(spots, grad_scale, 0.0)], axis=0)
        moved = net.c(packed)
    with jax.named_scope("up_grad"):
        up_line.nearer(order)
        order.note(up_line.here)
    with jax.named_scope("qkv_grad"):
        qkv_line = Line(net, wide_half, [low_red.group(order), high_red.group(order)])
        order.note(qkv_line.kept)
    with jax.named_scope("small_sums"):
        packed = packed + order(moved)
        order.note(packed)
        moved = [net.y(packed, s) for s in range(1, net.yn)]
    with jax.named_scope("down_grad"):
        down_mine = order(down_mine)
        if dp > 2:
            down_weight_grad = lax.psum(down_mine, "dp").astype(F32)
        else:
            down_other = net.x(down_mine)
    branch_out = jnp.dot(order(active), down_full, preferred_element_type=F32) + down_bias_full
    layer_out = (hidden + branch_out).astype(BF16)
    order.note(layer_out)
    with jax.named_scope("small_sums"):
        for item in moved:
            packed = packed + order(item)
        order.note(packed)
        moved = [net.z(packed, k) for k in range(1, ZN)]
    with jax.named_scope("up_grad"):
        up_line.last(order)
    with jax.named_scope("qkv_grad"):
        qkv_line.nearer(order)
    with jax.named_scope("small_sums"):
        for item in order(*moved):
            packed = packed + item
        mine = lax.dynamic_slice_in_dim(embeds, net.me * te_rows, te_rows, 1)
        time_part = lax.dot_general(
            mine,
            packed[count:],
            (((0,), (0,)), ((), ())),
            precision=lax.Precision.HIGHEST,
            preferred_element_type=F32,
        )
        each = attn_gain.shape[0]
        vector_part = lax.dynamic_slice_in_dim(packed[:5], net.me * each, each, 1)
        bias_part = lax.dynamic_slice_in_dim(
            packed[5:count].reshape(1, -1), net.me * up_bias.shape[0], up_bias.shape[0], 1
        )
        packed = jnp.concatenate(
            [
                time_part,
                jnp.pad(vector_part, ((0, 0), (0, width - each))),
                jnp.pad(bias_part, ((0, 0), (0, width - up_bias.shape[0]))),
            ],
            axis=0,
        )
        if dp > 2:
            packed = lax.psum(packed, "dp")
        else:
            packed = packed + net.x(packed)
        time_weight_grad = packed[:te_rows]
        vector_grads = [packed[te_rows + i, :each] for i in range(5)]
        up_bias_out = packed[te_rows + 5, : up_bias.shape[0]]
    with jax.named_scope("qkv_grad"):
        qkv_line.last(order)
        whole = qkv_line.finish(order)
    with jax.named_scope("up_grad"):
        both = up_line.finish(order)
        ups = grad_pre.shape[1]
        up_weight_grad, out_weight_grad = both[:, :ups], both[:, ups:]
    if dp == 2:
        down_weight_grad = down_mine.astype(F32) + down_other.astype(F32)
    wide_low, wide_high = low.shape[2], high.shape[2]
    low_part, high_part = whole[:, : 3 * wide_low], whole[:, 3 * wide_low :]
    qkv_weight_grad = jnp.concatenate(
        [
            item
            for i in range(3)
            for item in (
                low_part[:, i * wide_low : (i + 1) * wide_low],
                high_part[:, i * wide_high : (i + 1) * wide_high],
            )
        ],
        axis=1,
    )
    return (
        layer_out[None],
        token_grad[None],
        time_weight_grad,
        vector_grads[0],
        vector_grads[1],
        qkv_weight_grad,
        out_weight_grad,
        vector_grads[2],
        vector_grads[3],
        up_weight_grad,
        up_bias_out,
        down_weight_grad,
        vector_grads[4],
    )


def solution(mesh):
    return jax.shard_map(
        functools.partial(per_device, mesh.shape["dp"], mesh.shape["fsdp"]),
        mesh=mesh,
        in_specs=(
            P(("dp", "fsdp"), None, None),
            P(("dp", "fsdp")),
            P(("dp", "fsdp"), None),
            P(("dp", "fsdp"), None, None),
            P("fsdp", None),
            P("fsdp"),
            P("fsdp"),
            P("fsdp", None),
            P("fsdp", None),
            P("fsdp"),
            P("fsdp"),
            P("fsdp", None),
            P("fsdp"),
            P("fsdp", None),
            P("fsdp"),
        ),
        out_specs=(
            P(("dp", "fsdp"), None, None),
            P(("dp", "fsdp"), None, None),
            P("fsdp", None),
            P("fsdp"),
            P("fsdp"),
            P("fsdp", None),
            P("fsdp", None),
            P("fsdp"),
            P("fsdp"),
            P("fsdp", None),
            P("fsdp"),
            P("fsdp", None),
            P("fsdp"),
        ),
        check_vma=False,
    )
```

```python
import functools
import math

import jax
import jax.numpy as jnp
from jax import lax
from jax.experimental import pallas as pl
from jax.experimental.pallas import tpu as pltpu
from jax.sharding import PartitionSpec as P

HD = 64
ZN = 4
PAIR = 128
LOG2E = math.log2(math.e)
ROOT = math.sqrt(2.0 / math.pi)
F32 = jnp.float32
BF16 = jnp.bfloat16


def normalize(values_in):
    center = values_in - jnp.mean(values_in, axis=-1, keepdims=True)
    inverse = lax.rsqrt(jnp.mean(center * center, axis=-1, keepdims=True) + 1e-05)
    return (center * inverse, inverse)


def norm_back(grad_hat, normed, inverse):
    return inverse * (
        grad_hat
        - jnp.mean(grad_hat, axis=-1, keepdims=True)
        - normed * jnp.mean(grad_hat * normed, axis=-1, keepdims=True)
    )


def rows_dot(left, right):
    return lax.dot_general(
        left, right, (((0,), (0,)), ((), ())), preferred_element_type=F32
    )


def back_dot(grad_in, weight):
    return lax.dot_general(
        grad_in, weight, (((1,), (1,)), ((), ())), preferred_element_type=F32
    )


def rotary_tables(length):
    half_size = HD // 2
    frequency = jnp.exp(
        jnp.arange(half_size, dtype=F32) * (-2.0 * math.log(10000.0) / HD)
    )
    angles = jnp.arange(length, dtype=F32)[:, None] * frequency[None, :]
    angles = jnp.concatenate([angles] * (PAIR // half_size), axis=-1)
    return (jnp.cos(angles), jnp.sin(angles))


class Order:
    def __init__(self):
        self.mark = ()

    def __call__(self, *arrays):
        out = lax.optimization_barrier((*arrays, *self.mark))[: len(arrays)]
        self.mark = (out[0],)
        return out[0] if len(out) == 1 else out

    def note(self, *arrays):
        self.mark = arrays
        return arrays[0] if len(arrays) == 1 else arrays


def scoped(name):
    def wrap(function):
        @functools.wraps(function)
        def inner(*args, **kwargs):
            with jax.named_scope(name):
                return function(*args, **kwargs)

        return inner

    return wrap


class Net:
    def __init__(self, dp, fs):
        self.dp, self.fs = dp, fs
        self.yn = fs // (2 * ZN)
        index = lax.axis_index("fsdp")
        self.me = index
        self.z0 = index // (2 * self.yn)
        self.y0 = (index // 2) % self.yn
        self.c0 = index % 2
        self.p0 = lax.axis_index("dp") % 2

    def perm(self, values_in, zx, dy, dc):
        pairs = []
        for i in range(self.fs):
            z, y, c = i // (2 * self.yn), (i // 2) % self.yn, i % 2
            to = ((z ^ zx) * self.yn + (y + dy) % self.yn) * 2 + (c ^ dc)
            pairs.append((i, to))
        return lax.ppermute(values_in, "fsdp", pairs)

    @scoped("z_hop")
    def z(self, values_in, k):
        return self.perm(values_in, k, 0, 0)

    @scoped("y_hop")
    def y(self, values_in, s):
        return self.perm(values_in, 0, s, 0)

    @scoped("core_hop")
    def c(self, values_in):
        return self.perm(values_in, 0, 0, 1)

    @scoped("x_hop")
    def x(self, values_in):
        return lax.ppermute(values_in, "dp", [(i, i ^ 1) for i in range(self.dp)])


def stack_kernel(*refs):
    at = 0
    for item in refs[:-1]:
        rows = item.shape[0]
        refs[-1][at : at + rows, :] = item[...]
        at += rows


def stack_rows(*items):
    rows = sum(item.shape[0] for item in items)
    return pl.pallas_call(
        stack_kernel,
        out_shape=jax.ShapeDtypeStruct((rows, items[0].shape[1]), items[0].dtype),
        cost_estimate=cost(2.0),
        name="stack_rows",
    )(*items)


class Gather:
    def __init__(self, net, shard):
        self.net = net
        self.rows, self.columns = shard.shape
        self.half = self.rows // 2
        self.own = lax.dynamic_slice_in_dim(shard, net.p0 * self.half, self.half, 0)

    def along(self, own):
        self.own = own
        self.parts = [self.net.z(own, k) for k in range(1, ZN)]

    def join_line(self, order):
        self.line = stack_rows(*order(self.own, *self.parts))

    def across(self):
        net = self.net
        self.over = net.x(self.line)
        self.beside = [net.y(self.line, s) for s in range(1, net.yn)]

    def join_across(self, order):
        self.over, *self.beside = order(self.over, *self.beside)

    def corners(self):
        net = self.net
        mid = (ZN // 2) * self.half
        self.corner_one = [net.x(item[:mid]) for item in self.beside]
        self.corner_two = [net.y(self.over[mid:], s) for s in range(1, net.yn)]
        self.pieces = [self.line, self.over] + self.beside
        self.plan = [(0, 0, 0, ZN), (0, 1, 0, ZN)]
        self.plan += [(s, 0, 0, ZN) for s in range(1, net.yn)]
        self.moved = [net.c(item) for item in self.pieces]

    def finish(self, order):
        net = self.net
        late = order(*self.corner_one, *self.corner_two)
        plan = [(s, 1, 0, ZN // 2) for s in range(1, net.yn)]
        plan += [(s, 1, ZN // 2, ZN - ZN // 2) for s in range(1, net.yn)]
        pieces = self.pieces + list(late) + self.moved + [net.c(item) for item in late]
        plan = self.plan + plan
        full = [(s, q, side, first, count) for side in range(2) for s, q, first, count in plan]
        return full, pieces


def piece_spots(plan, where_ref, rows, half, yn):
    z0, y0, c0, p0 = where_ref[0], where_ref[1], where_ref[2], where_ref[3]
    spots = []
    for i, (s, q, side, first, count) in enumerate(plan):
        y = lax.rem(y0 + yn - s, yn)
        p = lax.rem(p0 + q, 2)
        c = lax.rem(c0 + side, 2)
        for k in range(count):
            z = lax.bitwise_xor(z0, jnp.int32(first + k))
            start = pl.multiple_of(((z * yn + y) * 2 + c) * rows + p * half, half)
            spots.append((i, k * half, first + k, start))
    return spots


def pack_kernel(*refs):
    time_ref, vectors, out_ref = refs[0], refs[1:-1], refs[-1]
    out_ref[...] = jnp.zeros_like(out_ref)
    rows = time_ref.shape[0]
    out_ref[:rows, :] = time_ref[...]
    for i, item in enumerate(vectors):
        out_ref[rows + i : rows + i + 1, : item.shape[1]] = item[...]


def small_kernel(rows, te_rows, sizes, yn, where_ref, embed_ref, own_ref, other_ref, *refs):
    scale_ref, all_ref, outs, held, sems = refs[0], refs[1], refs[2:-2], refs[-2], refs[-1]
    z0, y0, c0 = where_ref[0], where_ref[1], where_ref[2]
    copies = []
    for side, piece_ref in enumerate((own_ref, other_ref)):
        c = lax.rem(c0 + side, 2)
        for s in range(yn):
            y = lax.rem(y0 + yn - s, yn)
            for k in range(ZN):
                z = lax.bitwise_xor(z0, jnp.int32(k))
                copies.append(
                    pltpu.make_async_copy(
                        piece_ref.at[s * ZN + k],
                        held.at[(z * yn + y) * 2 + c],
                        sems.at[len(copies)],
                    )
                )
    for copy in copies:
        copy.start()
    for copy in copies:
        copy.wait()
    fs = held.shape[0]
    scale = jnp.ones_like(scale_ref)
    whole = jnp.concatenate([held[f, :te_rows, :] for f in range(fs)], axis=0)
    scale_ref[...] = scale + jnp.dot(embed_ref[...], whole, preferred_element_type=F32)
    for i, (size, out_ref) in enumerate(zip(sizes, outs)):
        pieces = [
            held[f, te_rows + i : te_rows + i + 1, :size].astype(F32) for f in range(fs)
        ]
        out_ref[...] = jnp.concatenate(pieces, axis=1)
    last, wide = te_rows + len(sizes), embed_ref.shape[1]
    all_ref[...] = jnp.concatenate(
        [held[f, last : last + 1, :wide].astype(F32) for f in range(fs)], axis=0
    )


class SmallGather:
    def __init__(self, net, time_weight, vectors, embed):
        self.net, self.sizes = net, [item.shape[0] for item in vectors]
        self.te_rows, self.width = time_weight.shape
        self.rows = self.te_rows + len(vectors) + 1
        self.rows += -self.rows % 16
        self.packed = pl.pallas_call(
            pack_kernel,
            out_shape=jax.ShapeDtypeStruct((self.rows, self.width), BF16),
            cost_estimate=cost(),
            name="pack_small",
        )(time_weight, *[item.reshape(1, -1) for item in vectors], embed)
        self.parts = [net.z(self.packed, k) for k in range(1, ZN)]

    def across(self, order):
        net = self.net
        self.line = jnp.stack(order(self.packed, *self.parts))
        self.beside = [net.y(self.line, s) for s in range(1, net.yn)]

    def other(self, order):
        self.line, *self.beside = order(self.line, *self.beside)
        self.sides = jnp.concatenate([self.line] + self.beside, axis=0)
        self.moved = self.net.c(self.sides)

    def finish(self, order, embed):
        net, fs = self.net, self.net.fs
        moved = order(self.moved)
        where = jnp.stack([net.z0, net.y0, net.c0]).astype(jnp.int32)
        shapes = [(1, self.width), (fs, embed.shape[1])]
        shapes += [(1, size * fs) for size in self.sizes]
        outs = pl.pallas_call(
            functools.partial(small_kernel, self.rows, self.te_rows, self.sizes, net.yn),
            out_shape=[jax.ShapeDtypeStruct(shape, F32) for shape in shapes],
            grid_spec=pltpu.PrefetchScalarGridSpec(
                num_scalar_prefetch=1,
                grid=(1,),
                in_specs=[pl.BlockSpec(embed.shape, lambda i, r: (0, 0))]
                + [pl.BlockSpec(memory_space=pl.ANY)] * 2,
                out_specs=[whole_spec(shape) for shape in shapes],
                scratch_shapes=[
                    pltpu.VMEM((fs, self.rows, self.width), BF16),
                    pltpu.SemaphoreType.DMA((fs,)),
                ],
            ),
            cost_estimate=cost(3.0),
            name="small_join",
        )(where, embed, self.sides, moved)
        order.note(outs[0])
        return outs


def relative_order(net, rows, total):
    half = rows // 2
    d = jnp.arange(total, dtype=jnp.int32)
    f, i = d // rows, d % rows
    z, y, c = f // (2 * net.yn), (f // 2) % net.yn, f % 2
    p, j = i // half, i % half
    c, y, p, z = c ^ net.c0, (y - net.y0) % net.yn, p ^ net.p0, z ^ net.z0
    z = 2 * (z % 2) + z // 2
    return (((c * net.yn + y) * 2 + p) * ZN + z) * half + j


def add_low(*items):
    total = items[0].astype(F32)
    for item in items[1:]:
        total = total + item.astype(F32)
    return total.astype(BF16)


def sum_kernel(counts, keep, *refs):
    total = sum(counts)
    kept_ref, sent_ref = refs[total], refs[total + 1]
    at, column = 0, 0
    for count in counts:
        items = refs[at : at + count]
        at += count
        wide = items[0].shape[1]
        value = items[0][...].astype(F32)
        for item in items[1:]:
            value = value + item[...].astype(F32)
        kept_ref[:, column : column + wide] = value[:keep, :]
        sent_ref[:, column : column + wide] = value[keep:, :].astype(BF16)
        column += wide


def sum_split(groups, keep, micros=0.5):
    rows = groups[0][0].shape[0]
    columns = sum(group[0].shape[1] for group in groups)
    return pl.pallas_call(
        functools.partial(sum_kernel, [len(group) for group in groups], keep),
        out_shape=[
            jax.ShapeDtypeStruct((keep, columns), F32),
            jax.ShapeDtypeStruct((rows - keep, columns), BF16),
        ],
        cost_estimate=cost(micros),
        name="sum_split",
    )(*[item for group in groups for item in group])


def merge_kernel(shifts, over_ref, *refs):
    sides, came_x, came_y = (refs[i * shifts : (i + 1) * shifts] for i in range(3))
    over_out, outs = refs[3 * shifts], refs[3 * shifts + 1 :]
    half = over_ref.shape[0] // 2
    over_out[:half, :] = over_ref[:half, :]
    value = over_ref[half:, :].astype(F32)
    for item in came_y:
        value = value + item[...].astype(F32)
    over_out[half:, :] = value.astype(BF16)
    for side_ref, item, out_ref in zip(sides, came_x, outs):
        value = side_ref[:half, :].astype(F32) + item[...].astype(F32)
        out_ref[:half, :] = value.astype(BF16)
        out_ref[half:, :] = side_ref[half:, :]


def merge_corners(over, sides, came_x, came_y):
    shape = jax.ShapeDtypeStruct(over.shape, BF16)
    return pl.pallas_call(
        functools.partial(merge_kernel, len(sides)),
        out_shape=[shape] * (1 + len(sides)),
        cost_estimate=cost(0.5),
        name="merge_corners",
    )(over, *sides, *came_x, *came_y)


class Scatter:
    def __init__(self, net):
        self.net = net

    def core(self, send):
        self.sent = self.net.c(send)

    def join_core(self, order):
        self.sent = order(self.sent)
        return self.sent

    def corners(self, own, over, *rest):
        net = self.net
        self.own, self.over, self.side = own, over, list(rest[0::3])
        self.came_x = [net.x(item) for item in rest[1::3]]
        self.came_y = [net.y(item, s + 1) for s, item in enumerate(rest[2::3])]

    def across(self, order):
        net, count = self.net, len(self.side)
        came = order(*self.came_x, *self.came_y)
        self.over, *self.side = merge_corners(self.over, self.side, came[:count], came[count:])
        order.note(self.over)
        self.over = net.x(self.over)
        self.side = [net.y(item, s + 1) for s, item in enumerate(self.side)]

    def group(self, order):
        return [self.own, *order(self.over, *self.side)]


class Line:
    def __init__(self, net, half, groups):
        self.net, self.half = net, half
        self.kept, far = sum_split(groups, (ZN // 2) * half, 9.0 / len(groups) ** 3)
        self.far = net.z(far, 1)

    def nearer(self, order):
        self.here, near = sum_split([[self.kept, order(self.far)]], self.half)
        self.near = self.net.z(near, 2)

    def last(self, order):
        net = self.net
        mine = add_low(self.here, order(self.near))
        if net.dp > 2:
            groups = [list(range(q, net.dp, 2)) for q in range(2)]
            mine = lax.psum(mine, "dp", axis_index_groups=groups)
        self.mine, self.other = mine, net.x(mine)

    def finish(self, order):
        mine, other = self.mine, order(self.other)
        first = jnp.where(self.net.p0 == 0, mine, other)
        second = jnp.where(self.net.p0 == 0, other, mine)
        return jnp.concatenate([first, second], axis=0).astype(F32)


def kept_parts(yn, half):
    line = ZN * half
    spots = [(0, line), (line, line)]
    for s in range(1, yn):
        first = 2 * s * line
        spots.append((first, line))
        spots += [(first + line + i * (line // 2), line // 2) for i in range(2)]
    return spots


def cost(micros=1.0):
    return pl.CostEstimate(flops=int(micros * 9e8), bytes_accessed=int(micros * 3e6), transcendentals=0)


def weight_copies(plan, where_ref, rows, half, yn, pieces, targets, sems):
    spots = piece_spots(plan, where_ref, rows, half, yn)
    groups, count, column = [], 0, 0
    for target, first, wide in targets:
        group = []
        for i, row, shift, start in spots:
            group.append(
                pltpu.make_async_copy(
                    pieces[i].at[pl.ds(row, half), pl.ds(column, wide)],
                    target.at[pl.ds(start, half), pl.ds(first, wide)],
                    sems.at[count],
                )
            )
            count += 1
        column += wide
        groups.append(group)
    for group in groups:
        for copy in group:
            copy.start()
    return groups


def finish_copies(copies):
    for copy in copies:
        copy.wait()


def back_copy(held, out, first, wide, sem):
    spot = pl.ds(first, wide)
    copy = pltpu.make_async_copy(held.at[:, spot], out.at[:, spot], sem)
    copy.start()
    return copy


def qkv_kernel(plan, rows, half, yn, where_ref, x_ref, cos_ref, sin_ref, *refs):
    pieces = refs[: len(plan)]
    out_ref, wq_ref, wo_ref, wq, wo, low, sems, back_sems = refs[len(plan) :]
    wide = wo.shape[1]
    targets = [(wq, part * wide, wide) for part in range(3)] + [(wo, 0, wide)]
    groups = weight_copies(plan, where_ref, rows, half, yn, pieces, targets, sems)
    cosine, sine = cos_ref[...], sin_ref[...]
    front = lax.broadcasted_iota(jnp.int32, cosine.shape, 1) % HD < HD // 2
    backs = []
    for part in range(3):
        finish_copies(groups[part])
        backs.append(back_copy(wq, wq_ref, part * wide, wide, back_sems.at[part]))
        for j in range(wide // (2 * PAIR)):
            first = part * wide + j * 2 * PAIR
            acc = jnp.dot(
                x_ref[...], wq[:, first : first + 2 * PAIR], preferred_element_type=F32
            )
            for i in range(2):
                piece = acc[:, i * PAIR : (i + 1) * PAIR]
                if part < 2:
                    turned = jnp.where(
                        front,
                        -pltpu.roll(piece, PAIR - HD // 2, 1),
                        pltpu.roll(piece, HD // 2, 1),
                    )
                    piece = piece * cosine + turned * sine
                low[:, first + i * PAIR : first + (i + 1) * PAIR] = piece.astype(BF16)
        backs.append(back_copy(low, out_ref, part * wide, wide, back_sems.at[4 + part]))
    finish_copies(groups[3])
    backs.append(back_copy(wo, wo_ref, 0, wide, back_sems.at[3]))
    finish_copies(backs)


def attn_in_kernel(low_ref, high_ref, w_ref, out_ref):
    wide = low_ref.shape[2]
    acc = back_dot(low_ref[0], w_ref[:, :wide]) + back_dot(high_ref[0], w_ref[:, wide:])
    step = pl.program_id(0)

    @pl.when(step == 0)
    def _():
        out_ref[...] = acc

    @pl.when(step > 0)
    def _():
        out_ref[...] = out_ref[...] + acc


def attn_in_back(low, high, w):
    parts, tokens, wide = low.shape
    depth = w.shape[0]
    half = pl.BlockSpec((1, tokens, wide), lambda i: (i, 0, 0))
    return pl.pallas_call(
        attn_in_kernel,
        grid=(parts,),
        in_specs=[half, half, pl.BlockSpec((depth, 2 * wide), lambda i: (0, i))],
        out_specs=pl.BlockSpec((tokens, depth), lambda i: (0, 0)),
        out_shape=jax.ShapeDtypeStruct((tokens, depth), F32),
        cost_estimate=cost(5.0),
        name="attn_in_back",
    )(low, high, w)


def where_of(net):
    return jnp.stack([net.z0, net.y0, net.c0, net.p0]).astype(jnp.int32)


ANY = pl.BlockSpec(memory_space=pl.ANY)


def whole_spec(shape):
    return pl.BlockSpec(shape, lambda i, r: (0, 0))


def qkv_rotated(net, x, plan, pieces, rows, cosine, sine):
    tokens, depth = x.shape
    total = net.fs * rows
    blocks = sum(entry[4] for entry in plan)
    half = rows // 2
    return pl.pallas_call(
        functools.partial(qkv_kernel, plan, rows, half, net.yn),
        grid_spec=pltpu.PrefetchScalarGridSpec(
            num_scalar_prefetch=1,
            grid=(1,),
            in_specs=[whole_spec(x.shape), whole_spec(cosine.shape), whole_spec(sine.shape)]
            + [ANY] * len(pieces),
            out_specs=[ANY] * 3,
            scratch_shapes=[
                pltpu.VMEM((total, 3 * depth), BF16),
                pltpu.VMEM((total, depth), BF16),
                pltpu.VMEM((tokens, 3 * depth), BF16),
                pltpu.SemaphoreType.DMA((4 * blocks,)),
                pltpu.SemaphoreType.DMA((7,)),
            ],
        ),
        out_shape=[
            jax.ShapeDtypeStruct((tokens, 3 * depth), BF16),
            jax.ShapeDtypeStruct((total, 3 * depth), BF16),
            jax.ShapeDtypeStruct((total, depth), BF16),
        ],
        compiler_params=pltpu.CompilerParams(vmem_limit_bytes=32 * 2**20),
        cost_estimate=cost(10.0),
        name="qkv_rotated",
    )(where_of(net), x, cosine, sine, *pieces)


def up_kernel(plan, rows, half, yn, where_ref, x_ref, b_ref, *refs):
    pieces = refs[: len(plan)]
    act_out, slope_out, w_out, w, act, slope, sems, back_sems = refs[len(plan) :]
    total = w.shape[1]
    wide = min(1024, total)
    step = min(256, wide)
    parts = total // wide
    targets = [(w, part * wide, wide) for part in range(parts)]
    groups = weight_copies(plan, where_ref, rows, half, yn, pieces, targets, sems)
    backs = []
    for part in range(parts):
        finish_copies(groups[part])
        backs.append(back_copy(w, w_out, part * wide, wide, back_sems.at[3 * part]))
        for first in range(part * wide, (part + 1) * wide, step):
            spot = slice(first, first + step)
            v = jnp.dot(x_ref[...], w[:, spot], preferred_element_type=F32) + b_ref[:, spot]
            square = v * v
            bend = jnp.tanh(v * (ROOT + ROOT * 0.044715 * square))
            half_up = 0.5 + 0.5 * bend
            act[:, spot] = (v * half_up).astype(BF16)
            rise = 0.5 * ROOT + (1.5 * 0.044715 * ROOT) * square
            slope[:, spot] = (half_up + v * (1.0 - bend * bend) * rise).astype(BF16)
        backs.append(back_copy(act, act_out, part * wide, wide, back_sems.at[3 * part + 1]))
        backs.append(back_copy(slope, slope_out, part * wide, wide, back_sems.at[3 * part + 2]))
    finish_copies(backs)


def up_gelu(net, x, plan, pieces, rows, bias):
    tokens, depth = x.shape
    total = bias.shape[1]
    parts = total // min(1024, total)
    blocks = sum(entry[4] for entry in plan)
    return pl.pallas_call(
        functools.partial(up_kernel, plan, rows, rows // 2, net.yn),
        grid_spec=pltpu.PrefetchScalarGridSpec(
            num_scalar_prefetch=1,
            grid=(1,),
            in_specs=[whole_spec(x.shape), whole_spec(bias.shape)] + [ANY] * len(pieces),
            out_specs=[ANY] * 3,
            scratch_shapes=[
                pltpu.VMEM((depth, total), BF16),
                pltpu.VMEM((tokens, total), BF16),
                pltpu.VMEM((tokens, total), BF16),
                pltpu.SemaphoreType.DMA((parts * blocks,)),
                pltpu.SemaphoreType.DMA((3 * parts,)),
            ],
        ),
        out_shape=[
            jax.ShapeDtypeStruct((tokens, total), BF16),
            jax.ShapeDtypeStruct((tokens, total), BF16),
            jax.ShapeDtypeStruct((depth, total), BF16),
        ],
        compiler_params=pltpu.CompilerParams(vmem_limit_bytes=40 * 2**20),
        cost_estimate=cost(8.0),
        name="up_gelu",
    )(where_of(net), x, bias, *pieces)


def down_kernel(plan, rows, half, yn, where_ref, g_ref, slope_ref, *refs):
    pieces = refs[: len(plan)]
    out_ref, sum_ref, w_ref, w, slope, low, sems, slope_sems, back_sems = refs[len(plan) :]
    spots = piece_spots(plan, where_ref, rows, half, yn)
    group_rows = w.shape[0] // ZN
    step = min(256, group_rows)
    z0 = where_ref[0]
    groups = [[] for _ in range(ZN)]
    for count, (i, row, shift, start) in enumerate(spots):
        copy = pltpu.make_async_copy(
            pieces[i].at[pl.ds(row, half), :], w.at[pl.ds(start, half), :], sems.at[count]
        )
        groups[shift].append(copy)
    slopes = []
    for k in range(ZN):
        at = pl.multiple_of(lax.bitwise_xor(z0, jnp.int32(k)) * group_rows, group_rows)
        for copy in groups[k]:
            copy.start()
        copy = pltpu.make_async_copy(
            slope_ref.at[:, pl.ds(at, group_rows)], slope.at[k], slope_sems.at[k]
        )
        copy.start()
        slopes.append(copy)
    backs = []
    for k in range(ZN):
        at = pl.multiple_of(lax.bitwise_xor(z0, jnp.int32(k)) * group_rows, group_rows)
        finish_copies(groups[k])
        slopes[k].wait()
        here = pl.ds(at, group_rows)
        copy = pltpu.make_async_copy(w.at[here, :], w_ref.at[here, :], back_sems.at[2 * k])
        copy.start()
        backs.append(copy)
        for j in range(group_rows // step):
            spot = slice(j * step, (j + 1) * step)
            inner = pl.multiple_of(at + j * step, step)
            acc = lax.dot_general(
                g_ref[...],
                w[pl.ds(inner, step), :],
                (((1,), (1,)), ((), ())),
                preferred_element_type=F32,
            )
            rounded = (acc * slope[k, :, spot].astype(F32)).astype(BF16)
            low[k, :, spot] = rounded
            sum_ref[:, pl.ds(inner, step)] = jnp.sum(
                rounded.astype(F32), axis=0, keepdims=True
            )
        copy = pltpu.make_async_copy(low.at[k], out_ref.at[:, here], back_sems.at[2 * k + 1])
        copy.start()
        backs.append(copy)
    finish_copies(backs)


def down_back(net, grad, plan, pieces, rows, slope):
    tokens, depth = grad.shape
    total = slope.shape[1]
    blocks = sum(entry[4] for entry in plan)
    return pl.pallas_call(
        functools.partial(down_kernel, plan, rows, rows // 2, net.yn),
        grid_spec=pltpu.PrefetchScalarGridSpec(
            num_scalar_prefetch=1,
            grid=(1,),
            in_specs=[whole_spec(grad.shape), ANY] + [ANY] * len(pieces),
            out_specs=[ANY, pl.BlockSpec((1, total), lambda i, r: (0, 0)), ANY],
            scratch_shapes=[
                pltpu.VMEM((total, depth), BF16),
                pltpu.VMEM((ZN, tokens, total // ZN), BF16),
                pltpu.VMEM((ZN, tokens, total // ZN), BF16),
                pltpu.SemaphoreType.DMA((blocks,)),
                pltpu.SemaphoreType.DMA((ZN,)),
                pltpu.SemaphoreType.DMA((2 * ZN,)),
            ],
        ),
        out_shape=[
            jax.ShapeDtypeStruct((tokens, total), BF16),
            jax.ShapeDtypeStruct((1, total), F32),
            jax.ShapeDtypeStruct((total, depth), BF16),
        ],
        compiler_params=pltpu.CompilerParams(vmem_limit_bytes=40 * 2**20),
        cost_estimate=cost(10.0),
        name="down_back",
    )(where_of(net), grad, slope, *pieces)


def attend_kernel(len_ref, q_ref, k_ref, v_ref, out_ref):
    q, k, v = q_ref[...], k_ref[...], v_ref[...]
    length = k.shape[0]
    first = lax.broadcasted_iota(jnp.int32, q.shape, 1) < HD
    valid = lax.broadcasted_iota(jnp.int32, (1, length), 1) < len_ref[0]
    zero = jnp.zeros_like(q)
    outs = []
    for h in range(2):
        one = jnp.where(first, q, zero) if h == 0 else jnp.where(first, zero, q)
        scores = lax.dot_general(
            one, k, (((1,), (1,)), ((), ())), preferred_element_type=F32
        )
        scores = jnp.where(valid, scores * HD**-0.5, -1000000000.0)
        top = jnp.max(scores, axis=1, keepdims=True)
        exponent = jnp.exp2((scores - top) * LOG2E)
        total = jnp.sum(exponent, axis=1, keepdims=True)
        mixed = jnp.dot(exponent.astype(BF16), v, preferred_element_type=F32)
        outs.append(mixed * (1.0 / total))
    out_ref[...] = jnp.where(first, outs[0], outs[1]).astype(BF16)


def attend(length, qkv, first_pair, pairs):
    rows, total = qkv.shape
    count = total // 3 // PAIR

    def pick(part):
        return pl.BlockSpec((rows, PAIR), lambda j, r: (0, part * count + first_pair + j))

    return pl.pallas_call(
        attend_kernel,
        grid_spec=pltpu.PrefetchScalarGridSpec(
            num_scalar_prefetch=1,
            grid=(pairs,),
            in_specs=[pick(0), pick(1), pick(2)],
            out_specs=pl.BlockSpec((rows, PAIR), lambda j, r: (0, j)),
        ),
        out_shape=jax.ShapeDtypeStruct((rows, pairs * PAIR), BF16),
        cost_estimate=cost(1.4 * pairs),
        name="attend",
    )(length, qkv, qkv, qkv)


def attend_back_kernel(len_ref, q_ref, k_ref, v_ref, g_ref, cos_ref, sin_ref, out_ref):
    q, k, v, g = q_ref[...], k_ref[...], v_ref[...], g_ref[...]
    length = k.shape[0]
    lane = lax.broadcasted_iota(jnp.int32, q.shape, 1)
    first = lane < HD
    valid = lax.broadcasted_iota(jnp.int32, (length, length), 0) < len_ref[0]
    zero = jnp.zeros_like(q)
    grads = []
    for h in range(2):
        key = jnp.where(first, k, zero) if h == 0 else jnp.where(first, zero, k)
        value = jnp.where(first, v, zero) if h == 0 else jnp.where(first, zero, v)
        scores = lax.dot_general(
            key, q, (((1,), (1,)), ((), ())), preferred_element_type=F32
        )
        scores = jnp.where(valid, scores * HD**-0.5, -1000000000.0)
        top = jnp.max(scores, axis=0, keepdims=True)
        exponent = jnp.exp2((scores - top) * LOG2E)
        total = jnp.sum(exponent, axis=0, keepdims=True)
        probs = exponent * (1.0 / total)
        grad_probs = lax.dot_general(
            value, g, (((1,), (1,)), ((), ())), preferred_element_type=F32
        )
        delta = jnp.sum(grad_probs * probs, axis=0, keepdims=True)
        grad_scores = (probs * (grad_probs - delta)).astype(BF16)
        grads.append(
            (
                lax.dot_general(
                    grad_scores, k, (((0,), (0,)), ((), ())), preferred_element_type=F32
                ),
                jnp.dot(grad_scores, q, preferred_element_type=F32),
                jnp.dot(probs.astype(BF16), g, preferred_element_type=F32),
            )
        )
    front = lane % HD < HD // 2
    cosine, sine = cos_ref[...] * HD**-0.5, sin_ref[...] * HD**-0.5
    for i in range(2):
        grad = jnp.where(first, grads[0][i], grads[1][i])
        sined = grad * sine
        turned = jnp.where(
            front, pltpu.roll(sined, PAIR - HD // 2, 1), -pltpu.roll(sined, HD // 2, 1)
        )
        out_ref[i] = (grad * cosine + turned).astype(BF16)
    out_ref[2] = jnp.where(first, grads[0][2], grads[1][2]).astype(BF16)


def attend_back(length, qkv, grad, cosine, sine, first_pair, pairs):
    rows, total = qkv.shape
    count = total // 3 // PAIR

    def pick(part):
        return pl.BlockSpec((rows, PAIR), lambda j, r: (0, part * count + first_pair + j))

    table = pl.BlockSpec((rows, PAIR), lambda j, r: (0, 0))
    return pl.pallas_call(
        attend_back_kernel,
        grid_spec=pltpu.PrefetchScalarGridSpec(
            num_scalar_prefetch=1,
            grid=(pairs,),
            in_specs=[pick(0), pick(1), pick(2), pick(0), table, table],
            out_specs=pl.BlockSpec((3, rows, PAIR), lambda j, r: (0, 0, j)),
        ),
        out_shape=jax.ShapeDtypeStruct((3, rows, pairs * PAIR), BF16),
        cost_estimate=cost(3.0 * pairs),
        name="attend_back",
    )(length, qkv, qkv, qkv, grad, cosine, sine)


def tall_kernel(left_ref, grad_ref, out_ref):
    out_ref[...] = lax.dot_general(
        left_ref[...], grad_ref[...], (((0,), (0,)), ((), ())), preferred_element_type=F32
    ).astype(BF16)


def tall_rows_dot(left, grad):
    depth, columns = grad.shape
    total = left.shape[1]
    tall = min(1024, total)
    return pl.pallas_call(
        tall_kernel,
        grid=(total // tall,),
        in_specs=[
            pl.BlockSpec((depth, tall), lambda i: (0, i)),
            pl.BlockSpec((depth, columns), lambda i: (0, 0)),
        ],
        out_specs=pl.BlockSpec((tall, columns), lambda i: (i, 0)),
        out_shape=jax.ShapeDtypeStruct((total, columns), BF16),
        cost_estimate=cost(9.0),
        name="tall_rows_dot",
    )(left, grad)


def wide_kernel(bounds, parts, *refs):
    step = pl.program_id(0)
    operands, rest = refs[: 2 * len(bounds)], refs[2 * len(bounds) :]

    def write(left_ref, grad_ref):
        grad = grad_ref[0] if len(grad_ref.shape) == 3 else grad_ref[...]
        acc = jnp.dot(left_ref[...], grad, preferred_element_type=F32)
        if parts is None:
            rest[-1][...] = acc.astype(BF16)
            return
        acc = acc + rest[0][...].astype(F32)
        for (first, rows), out_ref in zip(parts, rest[1:]):
            out_ref[...] = acc[first : first + rows, :].astype(BF16)

    for i, (low, high) in enumerate(bounds):

        @pl.when((step >= low) & (step < high))
        def _(i=i):
            write(operands[2 * i], operands[2 * i + 1])


def wide_rows_dot(at, rows, pairs, extra=None, parts=None):
    in_specs, args, bounds, done = [], [], [], 0
    wide = min(min(1024, grad.shape[-1]) for _, grad in pairs)
    for left, grad in pairs:
        depth = left.shape[1]
        count = grad.shape[0] if grad.ndim == 3 else grad.shape[1] // wide
        in_specs.append(pl.BlockSpec((rows, depth), lambda j: (at, 0)))

        def clip(j, done=done, count=count):
            return jnp.clip(j - done, 0, count - 1)

        if grad.ndim == 3:
            in_specs.append(pl.BlockSpec((1, depth, wide), lambda j, clip=clip: (clip(j), 0, 0)))
        else:
            in_specs.append(pl.BlockSpec((depth, wide), lambda j, clip=clip: (0, clip(j))))
        args += [left, grad]
        bounds.append((done, done + count))
        done += count
    spec = pl.BlockSpec((rows, wide), lambda j: (0, j))
    columns = done * wide
    if parts is None:
        out_specs, out_shape = spec, jax.ShapeDtypeStruct((rows, columns), BF16)
    else:
        in_specs.append(spec)
        args.append(extra)
        out_specs = [pl.BlockSpec((count, wide), lambda j: (0, j)) for _, count in parts]
        out_shape = [jax.ShapeDtypeStruct((count, columns), BF16) for _, count in parts]
    return pl.pallas_call(
        functools.partial(wide_kernel, bounds, parts),
        grid=(done,),
        in_specs=in_specs,
        out_specs=out_specs,
        out_shape=out_shape,
        cost_estimate=cost(1.5 * done),
        name="wide_rows_dot",
    )(*args)


def per_device(
    dp,
    fs,
    tokens,
    lengths,
    time_embed,
    cotangent,
    time_weight,
    attn_gain,
    attn_shift,
    qkv_weight,
    out_weight,
    mlp_gain,
    mlp_shift,
    up_weight,
    up_bias,
    down_weight,
    down_bias,
):
    net = Net(dp, fs)
    length, width = tokens.shape[1:]
    tokens, cotangent = tokens.reshape(length, width), cotangent.reshape(length, width)
    order = Order()
    wide_rows, tall_rows = qkv_weight.shape[0], down_weight.shape[0]
    te_rows = time_weight.shape[0]
    heads = width // HD
    half = width // 2
    with jax.named_scope("small_gather"):
        small = SmallGather(
            net,
            time_weight,
            [attn_gain, attn_shift, mlp_gain, mlp_shift, down_bias, up_bias],
            time_embed,
        )
    order.note(small.packed)
    with jax.named_scope("attn_gather"):
        attn_net = Gather(net, jnp.concatenate([qkv_weight, out_weight], axis=1))
        attn_net.along(order(attn_net.own))
    up_net = Gather(net, up_weight)
    down_net = Gather(net, down_weight)
    residual = tokens.astype(F32)
    normed_one, inverse_one = normalize(residual)
    up_net.own, down_net.own = order(inverse_one, up_net.own, down_net.own)[1:]
    with jax.named_scope("small_gather"):
        small.across(order)
    with jax.named_scope("small_gather"):
        small.other(order)
    with jax.named_scope("attn_gather"):
        attn_net.join_line(order)
        order.note(attn_net.line)
        attn_net.across()
    with jax.named_scope("up_gather"):
        up_net.along(order(up_net.own))
    with jax.named_scope("small_gather"):
        (
            time_scale,
            embeds,
            gain_one,
            shift_one,
            gain_two,
            shift_two,
            down_bias_full,
            up_bias_full,
        ) = small.finish(order, time_embed)

    place = relative_order(net, wide_rows, width)
    permute = (jnp.arange(width, dtype=jnp.int32)[:, None] == place[None, :]).astype(BF16)

    def turn(values_in):
        return back_dot(permute, values_in).astype(BF16)

    key_mask = jnp.arange(length, dtype=jnp.int32)[:, None] < lengths[None, :]
    affine_one = normed_one * gain_one + shift_one
    attn_in = (affine_one * time_scale).astype(BF16)
    cosine, sine = rotary_tables(length)
    order.note(attn_in, cosine, sine)
    turned_one = order.note(turn(order(attn_in)))
    with jax.named_scope("up_gather"):
        up_net.join_line(order)
        order.note(up_net.line)
    with jax.named_scope("attn_gather"):
        attn_net.join_across(order)
        attn_net.corners()
    with jax.named_scope("down_gather"):
        down_net.along(order(down_net.own))
    with jax.named_scope("attn_gather"):
        plan, pieces = attn_net.finish(order)
    with jax.named_scope("up_gather"):
        up_net.line = order(up_net.line)
        up_net.across()
    qkv, qkv_full, out_full = qkv_rotated(net, attn_in, plan, pieces, wide_rows, cosine, sine)
    order.note(qkv)
    pairs = heads // 2
    part = pairs // 2
    with jax.named_scope("down_gather"):
        down_net.join_line(order)
        order.note(down_net.line)
    with jax.named_scope("up_gather"):
        up_net.join_across(order)
        up_net.corners()
    context = order.note(attend(lengths, order(qkv), 0, pairs))
    with jax.named_scope("up_gather"):
        plan, pieces = up_net.finish(order)
    with jax.named_scope("down_gather"):
        down_net.line = order(down_net.line)
        down_net.across()
    context = order(context)
    hidden = residual + jnp.dot(context, out_full, preferred_element_type=F32)
    normed_two, inverse_two = normalize(hidden)
    affine_two = normed_two * gain_two + shift_two
    mlp_in = (affine_two * time_scale).astype(BF16)
    order.note(mlp_in)
    turned_ctx = order.note(turn(order(context)))
    active, slope, up_full = up_gelu(
        net, order(mlp_in), plan, pieces, wide_rows, up_bias_full
    )
    order.note(active)
    with jax.named_scope("down_gather"):
        down_net.join_across(order)
        down_net.corners()

    grad_out = cotangent.astype(F32) * key_mask.astype(F32)
    grad_branch = grad_out.astype(BF16)
    with jax.named_scope("down_grad"):
        tall = order.note(tall_rows_dot(order(active), grad_branch))
        down_mine = lax.psum_scatter(tall, "fsdp", scatter_dimension=0, tiled=True)
    down_bias_grad = jnp.sum(grad_branch.astype(F32), axis=0, keepdims=True)
    turned_two = order.note(turn(order(mlp_in)))
    with jax.named_scope("down_gather"):
        plan, pieces = down_net.finish(order)
    grad_pre, up_bias_grad, down_full = down_back(
        net, order(grad_branch), plan, pieces, tall_rows, slope
    )
    grad_pre = order(order.note(grad_pre))
    grad_mlp_in = back_dot(grad_pre, up_full)
    grad_affine_two = grad_mlp_in * time_scale
    grad_scale = jnp.sum(grad_mlp_in * affine_two, axis=0, keepdims=True)
    mlp_gain_grad = jnp.sum(grad_affine_two * normed_two, axis=0, keepdims=True)
    mlp_shift_grad = jnp.sum(grad_affine_two, axis=0, keepdims=True)
    grad_hidden = grad_out + norm_back(grad_affine_two * gain_two, normed_two, inverse_two)
    grad_attn = order.note(grad_hidden.astype(BF16))
    wide_half = wide_rows // 2
    wide_parts = kept_parts(net.yn, wide_half)
    up_red, low_red, high_red = Scatter(net), Scatter(net), Scatter(net)
    up_pairs = [(turned_two, grad_pre), (turned_ctx, grad_attn)]
    with jax.named_scope("up_grad"):
        order(grad_pre)
        up_red.core(order.note(wide_rows_dot(1, half, up_pairs)))
    grad_context = order.note(back_dot(order(grad_attn), out_full).astype(BF16))
    with jax.named_scope("up_grad"):
        sent = up_red.join_core(order)
        kept = wide_rows_dot(0, half, up_pairs, sent, wide_parts)
        order.note(kept[0])
        up_red.corners(*kept)
    low = attend_back(lengths, qkv, order(grad_context), cosine, sine, 0, part)
    order.note(low)
    with jax.named_scope("qkv_grad"):
        low_red.core(order.note(wide_rows_dot(1, half, [(turned_one, order(low))])))
    with jax.named_scope("up_grad"):
        up_red.across(order)
    high = attend_back(lengths, qkv, order(grad_context), cosine, sine, part, pairs - part)
    order.note(high)
    with jax.named_scope("qkv_grad"):
        sent = low_red.join_core(order)
        kept = wide_rows_dot(0, half, [(turned_one, low)], sent, wide_parts)
        order.note(kept[0])
        low_red.corners(*kept)
        high_red.core(order.note(wide_rows_dot(1, half, [(turned_one, order(high))])))
    grad_attn_in = attn_in_back(low, order(high), qkv_full)
    grad_affine_one = grad_attn_in * time_scale
    grad_scale = grad_scale + jnp.sum(grad_attn_in * affine_one, axis=0, keepdims=True)
    attn_gain_grad = jnp.sum(grad_affine_one * normed_one, axis=0, keepdims=True)
    attn_shift_grad = jnp.sum(grad_affine_one, axis=0, keepdims=True)
    token_grad = (
        grad_hidden + norm_back(grad_affine_one * gain_one, normed_one, inverse_one)
    ).astype(BF16)
    order.note(token_grad, grad_scale)
    with jax.named_scope("small_sums"):
        sums = jnp.concatenate(
            [
                attn_gain_grad,
                attn_shift_grad,
                mlp_gain_grad,
                mlp_shift_grad,
                down_bias_grad,
                up_bias_grad.reshape(-1, width),
            ],
            axis=0,
        )
        count = sums.shape[0]
        spots = jnp.arange(fs, dtype=jnp.int32)[:, None] == net.me
        packed = jnp.concatenate([sums, jnp.where(spots, grad_scale, 0.0)], axis=0)
        moved = net.c(packed)
    with jax.named_scope("up_grad"):
        up_line = Line(net, wide_half, [up_red.group(order)])
        order.note(up_line.kept)
    with jax.named_scope("qkv_grad"):
        sent = high_red.join_core(order)
        kept = wide_rows_dot(0, half, [(turned_one, high)], sent, wide_parts)
        order.note(kept[0])
        high_red.corners(*kept)
    with jax.named_scope("qkv_grad"):
        low_red.across(order)
        high_red.across(order)
    with jax.named_scope("up_grad"):
        up_line.nearer(order)
        order.note(up_line.here)
    with jax.named_scope("small_sums"):
        packed = packed + order(moved)
        order.note(packed)
        moved = [net.y(packed, s) for s in range(1, net.yn)]
    branch_out = jnp.dot(order(active), down_full, preferred_element_type=F32) + down_bias_full
    layer_out = (hidden + branch_out).astype(BF16)
    order.note(layer_out)
    with jax.named_scope("up_grad"):
        up_line.last(order)
    with jax.named_scope("small_sums"):
        for item in moved:
            packed = packed + order(item)
        order.note(packed)
        moved = [net.z(packed, k) for k in range(1, ZN)]
    with jax.named_scope("qkv_grad"):
        qkv_line = Line(net, wide_half, [low_red.group(order), high_red.group(order)])
        order.note(qkv_line.kept)
    with jax.named_scope("down_grad"):
        down_mine = order(down_mine)
        if dp > 2:
            down_weight_grad = lax.psum(down_mine, "dp").astype(F32)
        else:
            down_other = net.x(down_mine)
    with jax.named_scope("qkv_grad"):
        qkv_line.nearer(order)
    with jax.named_scope("small_sums"):
        for item in order(*moved):
            packed = packed + item
        mine = lax.dynamic_slice_in_dim(embeds, net.me * te_rows, te_rows, 1)
        time_part = lax.dot_general(
            mine,
            packed[count:],
            (((0,), (0,)), ((), ())),
            precision=lax.Precision.HIGHEST,
            preferred_element_type=F32,
        )
        each = attn_gain.shape[0]
        vector_part = lax.dynamic_slice_in_dim(packed[:5], net.me * each, each, 1)
        bias_part = lax.dynamic_slice_in_dim(
            packed[5:count].reshape(1, -1), net.me * up_bias.shape[0], up_bias.shape[0], 1
        )
        packed = jnp.concatenate(
            [
                time_part,
                jnp.pad(vector_part, ((0, 0), (0, width - each))),
                jnp.pad(bias_part, ((0, 0), (0, width - up_bias.shape[0]))),
            ],
            axis=0,
        )
        if dp > 2:
            packed = lax.psum(packed, "dp")
        else:
            packed = packed + net.x(packed)
        time_weight_grad = packed[:te_rows]
        vector_grads = [packed[te_rows + i, :each] for i in range(5)]
        up_bias_out = packed[te_rows + 5, : up_bias.shape[0]]
    with jax.named_scope("qkv_grad"):
        qkv_line.last(order)
        whole = qkv_line.finish(order)
    with jax.named_scope("up_grad"):
        both = up_line.finish(order)
        ups = grad_pre.shape[1]
        up_weight_grad, out_weight_grad = both[:, :ups], both[:, ups:]
    if dp == 2:
        down_weight_grad = down_mine.astype(F32) + down_other.astype(F32)
    wide_low, wide_high = low.shape[2], high.shape[2]
    low_part, high_part = whole[:, : 3 * wide_low], whole[:, 3 * wide_low :]
    qkv_weight_grad = jnp.concatenate(
        [
            item
            for i in range(3)
            for item in (
                low_part[:, i * wide_low : (i + 1) * wide_low],
                high_part[:, i * wide_high : (i + 1) * wide_high],
            )
        ],
        axis=1,
    )
    return (
        layer_out[None],
        token_grad[None],
        time_weight_grad,
        vector_grads[0],
        vector_grads[1],
        qkv_weight_grad,
        out_weight_grad,
        vector_grads[2],
        vector_grads[3],
        up_weight_grad,
        up_bias_out,
        down_weight_grad,
        vector_grads[4],
    )


def solution(mesh):
    return jax.shard_map(
        functools.partial(per_device, mesh.shape["dp"], mesh.shape["fsdp"]),
        mesh=mesh,
        in_specs=(
            P(("dp", "fsdp"), None, None),
            P(("dp", "fsdp")),
            P(("dp", "fsdp"), None),
            P(("dp", "fsdp"), None, None),
            P("fsdp", None),
            P("fsdp"),
            P("fsdp"),
            P("fsdp", None),
            P("fsdp", None),
            P("fsdp"),
            P("fsdp"),
            P("fsdp", None),
            P("fsdp"),
            P("fsdp", None),
            P("fsdp"),
        ),
        out_specs=(
            P(("dp", "fsdp"), None, None),
            P(("dp", "fsdp"), None, None),
            P("fsdp", None),
            P("fsdp"),
            P("fsdp"),
            P("fsdp", None),
            P("fsdp", None),
            P("fsdp"),
            P("fsdp"),
            P("fsdp", None),
            P("fsdp"),
            P("fsdp", None),
            P("fsdp"),
        ),
        check_vma=False,
    )
```
